32 devices in a mesh: grp: 2 (over y), ch: 4 (over z), fq: 2 (over x), sub: 2 (over core).
Axes of the slice: x: 2, y: 2, z: 4, core: 2. Of those that a mesh axis runs over, the one named last changes fastest.
Arguments:
- spectra: float32 [2, 2048, 8192], P(None, ('grp', 'ch'), ('fq', 'sub')), parts along dimension 1, may hold values from -6 to 6
- quality: int32 [2048], P(('grp', 'ch')), parts along dimension 0, may hold values 0 or 1
- taper: float32 [8192], P(('fq', 'sub')), may hold values from 0.5 to 2
Outputs:
- stack: float32 [8, 32, 512], P(('grp', 'ch'), ('fq', 'sub')), parts along dimension 0
The draws below stay inside these ranges and needn't reach their ends.
There are 2 independent parts, one for each index of `grp`. The reference program is written for one: setup_inputs(seed, part) draws one part's arguments, and reference() takes and returns one part's arrays. A program takes and returns all parts, laid end to end along the dimension named above; an argument that names none is the same for every part. Nothing has to cross between parts.
All inputs are finite; a program needn't handle non-finite values. No bound on the sum of `quality` on one device may be relied on, other than what follows from the above.
Results may differ from the reference program's by a relative error of at most 0.0017.
Values may be sent and summed in bfloat16 or wider, within the bound.
A program may use at most 64 MiB of HBM per device.

```python
import math
import jax
import jax.numpy as jnp
from jax import lax

CB = 256
FREQS = 8192
LAGS = 32
CHANNELS = 1024
N_CH = 4


def place_ends(values, stream_key, low, high):
    longest = values.shape.index(max(values.shape))
    spots = []
    for shift in (0, 1):
        where = [jax.random.randint(jax.random.fold_in(stream_key, axis), (), 0, length) for axis, length in enumerate(values.shape)]
        where[longest] = (where[longest] + shift) % values.shape[longest]
        spots.append(tuple(where))
    return values.at[spots[0]].set(low).at[spots[1]].set(high)


def shard_levels(key, shape, cuts, least, top_value):
    level, own = 1.0, jax.random.fold_in(key, 6)
    for position, shards_of in cuts:
        heights = jnp.exp(jax.random.uniform(jax.random.fold_in(own, position), (shards_of,), jnp.float32, least / len(cuts), top_value / len(cuts)))
        level = level * jnp.repeat(heights, shape[position] // shards_of).reshape([-1 if axis == position else 1 for axis in range(len(shape))])
    return level


def normal_values(stream_key, extent, deviation, limit, pieces=(), kind=jnp.bfloat16):
    gain = shard_levels(stream_key, extent, pieces, -0.22, 0.18) if pieces else 1.0
    values = jax.random.normal(stream_key, extent, jnp.float32) * deviation * gain
    return jnp.minimum(jnp.maximum(values, -limit), limit).astype(kind)


def setup_inputs(seed: int = 0, part: int = 0) -> dict:
    key_of = jax.random.split(jax.random.key(seed), 4)
    part_splits = jax.random.split(jax.random.fold_in(key_of[3], part), 4)
    return {
        "spectra": normal_values(part_splits[0], (2, CHANNELS, FREQS), 1.0, 6.0, ((1, 4), (2, 4)), jnp.float32),
        "quality": place_ends((jax.random.randint(part_splits[1], (CHANNELS,), 0, 8) < 7).astype(jnp.int32), jax.random.fold_in(part_splits[1], 1), 0, 1),
        "taper": jnp.clip(jnp.exp(math.log(2.0) - 1.3862944 * jax.random.uniform(key_of[2], (FREQS,), jnp.float32) ** shard_levels(key_of[2], (FREQS,), ((0, 4),), -0.2, 0.2)), 0.5, 2.0),
    }


def channel_table(block_size):
    padded = 2 * block_size
    row_index = jnp.arange(padded, dtype=jnp.int32)[:, None]
    col_index = jnp.arange(block_size, dtype=jnp.int32)[None, :]
    angle = 2.0 * jnp.pi / padded * (row_index * col_index % padded).astype(jnp.float32)
    cosine = jnp.cos(angle)
    sine = jnp.sin(angle)
    upper = jnp.concatenate([cosine, sine], axis=1)
    lower = jnp.concatenate([-sine, cosine], axis=1)
    return jnp.concatenate([upper, lower], axis=0).astype(jnp.bfloat16)

def inverse_table(block_size):
    padded = 2 * block_size
    row_index = jnp.arange(padded, dtype=jnp.int32)[:, None]
    col_index = jnp.arange(padded, dtype=jnp.int32)[None, :]
    angle = 2.0 * jnp.pi / padded * (row_index * col_index % padded).astype(jnp.float32)
    return jnp.concatenate([jnp.cos(angle), jnp.sin(angle)], axis=0) / padded

def lag_table(taper_band, start, band_size, lag_count, freq_count):
    freq_index = start + jnp.arange(band_size, dtype=jnp.int32)
    lag_index = jnp.arange(lag_count, dtype=jnp.int32) - lag_count // 2
    phase = lag_index[:, None] * freq_index[None, :] % (2 * freq_count)
    angle = jnp.pi / freq_count * phase.astype(jnp.float32)
    cosine = taper_band[None, :] * jnp.cos(angle)
    sine = taper_band[None, :] * jnp.sin(angle)
    upper = jnp.concatenate([cosine, -sine], axis=1)
    lower = jnp.concatenate([sine, cosine], axis=1)
    return jnp.concatenate([upper, lower], axis=0).astype(jnp.bfloat16)

def cross_spectrum(first, second, sign):
    padded = first.shape[0] // 2
    first_real = first[:padded].astype(jnp.float32)
    first_imag = first[padded:].astype(jnp.float32)
    second_real = second[:padded].astype(jnp.float32)
    second_imag = second[padded:].astype(jnp.float32)
    prod_real = first_real * second_real + first_imag * second_imag
    prod_imag = (first_imag * second_real - first_real * second_imag) * sign
    return jnp.concatenate([prod_real, prod_imag], axis=1).astype(jnp.bfloat16)

def pair_counts(lower_mask, upper_mask):
    block_size = lower_mask.shape[0]
    outer = lower_mask[::-1][:, None] * upper_mask[None, :]
    widened = jnp.pad(outer, ((0, 0), (0, block_size)))
    flat = widened.reshape(-1)[:block_size * (2 * block_size - 1)]
    sheared = flat.reshape(block_size, 2 * block_size - 1)
    histogram = jnp.pad(lax.optimization_barrier(jnp.sum(sheared, axis=0)), (0, 1))
    return jnp.roll(histogram, -(block_size - 1))

def reference(spectra, quality, taper):
    block_size = CB
    padded = 2 * block_size
    quality_float = quality.astype(jnp.float32)
    masked = (spectra * quality_float[None, :, None]).astype(jnp.bfloat16)
    table = channel_table(block_size)
    weights = lag_table(taper, 0, FREQS, LAGS, FREQS)
    inverse = inverse_table(block_size)
    hats = []
    masks = []
    for block in range(N_CH):
        piece = masked[:, block * block_size:(block + 1) * block_size, :].reshape(padded, FREQS)
        hats.append(jnp.dot(table, piece, preferred_element_type=jnp.float32).astype(jnp.bfloat16))
        masks.append(quality_float[block * block_size:(block + 1) * block_size])
    results = []
    for offset in range(N_CH):
        lagged = jnp.zeros((2 * LAGS, padded), jnp.float32)
        tally = jnp.zeros((padded,), jnp.float32)
        for lower in range(N_CH - offset):
            upper = lower + offset
            product = cross_spectrum(hats[lower], hats[upper], 1.0)
            lagged = lagged + lax.dot_general(weights, product, (((1,), (1,)), ((), ())), preferred_element_type=jnp.float32)
            tally = tally + pair_counts(masks[lower], masks[upper])
        combined = jnp.concatenate([lagged[:LAGS], lagged[LAGS:]], axis=1)
        result = jnp.dot(combined, inverse, precision=lax.Precision.HIGHEST, preferred_element_type=jnp.float32)
        scale = jnp.sqrt(2.0 * FREQS * jnp.maximum(tally, 1.0))
        results.append(result / scale[None, :])
    return jnp.stack(results, axis=0)
```

```python
import functools

import jax
import jax.numpy as jnp
import numpy as np
from jax import lax
from jax.experimental import pallas as pl
from jax.experimental.pallas import tpu as pltpu
from jax.sharding import PartitionSpec as P

FREQS = 8192
LAGS = 32
CHUNK = 128


def passed_along(value, axis, steps):
    count = lax.axis_size(axis)
    pairs = [(source, (source + steps) % count) for source in range(count)]
    return lax.ppermute(value, axis, pairs)


def channel_table(block_size):
    padded = 2 * block_size
    row_index = jnp.arange(padded, dtype=jnp.int32)[:, None]
    col_index = jnp.arange(block_size, dtype=jnp.int32)[None, :]
    angle = 2.0 * jnp.pi / padded * (row_index * col_index % padded).astype(jnp.float32)
    cosine = jnp.cos(angle)
    sine = jnp.sin(angle)
    upper = jnp.concatenate([cosine, sine], axis=1)
    lower = jnp.concatenate([-sine, cosine], axis=1)
    return jnp.concatenate([upper, lower], axis=0).astype(jnp.bfloat16)


def inverse_table(block_size):
    padded = 2 * block_size
    row_index = jnp.arange(padded, dtype=jnp.int32)[:, None]
    col_index = jnp.arange(padded, dtype=jnp.int32)[None, :]
    angle = 2.0 * jnp.pi / padded * (row_index * col_index % padded).astype(jnp.float32)
    return jnp.concatenate([jnp.cos(angle), jnp.sin(angle)], axis=0) / padded


def lag_table(taper_band, start, band_size, lag_count, freq_count):
    freq_index = start + jnp.arange(band_size, dtype=jnp.int32)
    lag_index = jnp.arange(lag_count, dtype=jnp.int32) - lag_count // 2
    phase = lag_index[:, None] * freq_index[None, :] % (2 * freq_count)
    angle = jnp.pi / freq_count * phase.astype(jnp.float32)
    cosine = taper_band[None, :] * jnp.cos(angle)
    sine = taper_band[None, :] * jnp.sin(angle)
    upper = jnp.concatenate([cosine, -sine], axis=1)
    lower = jnp.concatenate([sine, cosine], axis=1)
    return jnp.concatenate([upper, lower], axis=0).astype(jnp.bfloat16)


def cross_spectrum(first, second, sign):
    padded = first.shape[0] // 2
    first_real = first[:padded].astype(jnp.float32)
    first_imag = first[padded:].astype(jnp.float32)
    second_real = second[:padded].astype(jnp.float32)
    second_imag = second[padded:].astype(jnp.float32)
    prod_real = first_real * second_real + first_imag * second_imag
    prod_imag = (first_imag * second_real - first_real * second_imag) * sign
    return jnp.concatenate([prod_real, prod_imag], axis=1).astype(jnp.bfloat16)


def pair_counts(lower_mask, upper_mask):
    block_size = lower_mask.shape[0]
    outer = lower_mask[::-1][:, None] * upper_mask[None, :]
    widened = jnp.pad(outer, ((0, 0), (0, block_size)))
    flat = widened.reshape(-1)[: block_size * (2 * block_size - 1)]
    sheared = flat.reshape(block_size, 2 * block_size - 1)
    histogram = jnp.pad(jnp.sum(sheared, axis=0), (0, 1))
    return jnp.roll(histogram, -(block_size - 1))


def channel_transform(table, data):
    block_size = data.shape[1]
    stacked = data.reshape(2 * block_size, data.shape[2])
    return jnp.dot(table, stacked, preferred_element_type=jnp.float32).astype(jnp.bfloat16)


def shards(spectra, quality, taper):
    block_size = spectra.shape[1]
    band_size = spectra.shape[2]
    padded = 2 * block_size
    blocks = lax.axis_size("ch")
    position = lax.axis_index("ch")
    quality_float = quality.astype(jnp.float32)
    masked = (spectra * quality_float[None, :, None]).astype(jnp.bfloat16)
    mask_half = quality_float.astype(jnp.bfloat16)
    table = channel_table(block_size)
    start = lax.axis_index(("fq", "sub")) * band_size
    own_hat = channel_transform(table, masked)
    weights = lag_table(taper, start, band_size, LAGS, FREQS)

    def accumulate(state, partner_hat, partner_mask, round_index):
        totals, tallies = state
        wrapped = position + round_index >= blocks
        sign = jnp.where(wrapped, -1.0, 1.0).astype(jnp.float32)
        product = cross_spectrum(own_hat, partner_hat, sign)
        term = lax.dot_general(
            weights, product, (((1,), (1,)), ((), ())), preferred_element_type=jnp.float32
        )
        term = term.reshape(2, LAGS, padded)
        offset = jnp.where(wrapped, blocks - round_index, round_index).astype(jnp.int32)
        keep = jnp.where(jnp.logical_and(wrapped, 2 * round_index == blocks), 0.0, 1.0).astype(
            jnp.float32
        )
        lower_mask = jnp.where(wrapped, partner_mask, mask_half).astype(jnp.float32)
        upper_mask = jnp.where(wrapped, mask_half, partner_mask).astype(jnp.float32)
        pairs = pair_counts(lower_mask, upper_mask)
        old_row = lax.dynamic_slice_in_dim(totals, offset, 1, 0)
        totals = lax.dynamic_update_slice_in_dim(totals, old_row + keep * term[None], offset, 0)
        old_tally = lax.dynamic_slice_in_dim(tallies, offset, 1, 0)
        tallies = lax.dynamic_update_slice_in_dim(
            tallies, old_tally + keep * pairs[None], offset, 0
        )
        return (totals, tallies)

    state = (
        jnp.zeros((blocks, 2, LAGS, padded), jnp.float32),
        jnp.zeros((blocks, padded), jnp.float32),
    )
    state = accumulate(state, own_hat, mask_half, 0)

    def advance(round_index, carry):
        current, held, held_mask = carry
        held, held_mask = passed_along((held, held_mask), "ch", -1)
        current = accumulate(current, channel_transform(table, held), held_mask, round_index)
        return (current, held, held_mask)

    state, _, _ = lax.fori_loop(1, blocks // 2 + 1, advance, (state, masked, mask_half))
    totals, tallies = state
    totals, tallies = (
        lax.psum_scatter(totals, "ch", scatter_dimension=0, tiled=True),
        lax.psum_scatter(tallies, "ch", scatter_dimension=0, tiled=True),
    )
    totals = lax.psum_scatter(totals, ("fq", "sub"), scatter_dimension=2, tiled=True)
    combined = jnp.concatenate([totals[0, 0], totals[0, 1]], axis=1)
    lagged = jnp.dot(
        combined,
        inverse_table(block_size),
        precision=lax.Precision.HIGHEST,
        preferred_element_type=jnp.float32,
    )
    scale = jnp.sqrt(2.0 * FREQS * jnp.maximum(tallies[0], 1.0))
    return (lagged / scale[None, :])[None]


def channel_constant(block_size):
    padded = 2 * block_size
    index = np.outer(np.arange(padded), np.arange(block_size)) % padded
    angle = 2.0 * np.pi / padded * index
    cosine, sine = np.cos(angle), np.sin(angle)
    upper = np.concatenate([cosine, sine], axis=1)
    lower = np.concatenate([-sine, cosine], axis=1)
    return np.concatenate([upper, lower], axis=0).astype(jnp.bfloat16)


def inverse_constant(block_size):
    padded = 2 * block_size
    index = np.outer(np.arange(padded), np.arange(padded)) % padded
    angle = 2.0 * np.pi / padded * index
    full = np.concatenate([np.cos(angle), np.sin(angle)], axis=0) / padded
    high = full.astype(np.float32).astype(jnp.bfloat16)
    low = (full - high.astype(np.float64)).astype(np.float32).astype(jnp.bfloat16)
    return np.stack([high, low])


def lag_constant(lag_count, freq_count):
    lag_index = np.arange(lag_count) - lag_count // 2
    phase = np.outer(lag_index, np.arange(freq_count)) % (2 * freq_count)
    angle = np.pi / freq_count * phase
    return np.stack([np.cos(angle), np.sin(angle)]).astype(np.float32)


def kernel(
    sizes, spectra, quality_hbm, taper_hbm, table_hbm, inverse_hbm, lag_hbm, out,
    quality, taper, raw, send, recv, table, inverse, lagtab, masks, hats, acc, part, part_in, band_sum, band_in,
    raw_sem, const_sem, send_sem, recv_sem, mask_send, mask_recv,
    part_send, part_recv, band_send, band_recv, two_away, three_away,
):
    n, groups, subs, block, chunks = sizes
    padded = 2 * block
    lag_rows = LAGS // groups
    me = lax.axis_index("ch")
    group = lax.axis_index("fq") * subs + lax.axis_index("sub")

    def ch_peer(step):
        return (me, lax.rem(me + 2, 4), 3 - me, me + 1 - 2 * lax.rem(me, 2))[step]

    def group_peer(step):
        return lax.rem(group + step, groups)

    def group_id(index):
        return {"fq": index // subs, "sub": lax.rem(index, subs)}

    def raw_copy(step, c):
        slot = ch_peer(step) * chunks + c
        start = pl.multiple_of(slot * CHUNK, CHUNK)
        return pltpu.make_async_copy(
            spectra.at[:, :, pl.ds(start, CHUNK)], raw.at[slot], raw_sem.at[step, c]
        )

    def data_copy(step, c, source):
        return pltpu.make_async_remote_copy(
            send.at[ch_peer(step) * chunks + c], recv.at[source, c],
            send_sem.at[step - 1, c], recv_sem.at[source, c],
            device_id={"ch": ch_peer(step)}, device_id_type=pl.DeviceIdType.MESH,
        )

    def mask_copy(step, source):
        return pltpu.make_async_remote_copy(
            masks.at[me], masks.at[source], mask_send.at[step - 1], mask_recv.at[source],
            device_id={"ch": ch_peer(step)}, device_id_type=pl.DeviceIdType.MESH,
        )

    def part_copy(side, step, source):
        return pltpu.make_async_remote_copy(
            part.at[side, group_peer(step)], part_in.at[side, source],
            part_send.at[side, step - 1], part_recv.at[side, source],
            device_id=group_id(group_peer(step)), device_id_type=pl.DeviceIdType.MESH,
        )

    def band_copy(target, source):
        return pltpu.make_async_remote_copy(
            band_sum.at[target], band_in.at[source], band_send.at[target], band_recv.at[source],
            device_id={"ch": target}, device_id_type=pl.DeviceIdType.MESH,
        )

    def band_wait(source):
        return band_copy(source, source)

    sides = ((0, n - 1), tuple(range(1, n - 1)))

    middle = (me * (n - 1 - me)) // 2

    def tell(semaphore, target):
        pl.semaphore_signal(
            semaphore, inc=1, device_id={"ch": target}, device_id_type=pl.DeviceIdType.MESH
        )

    barrier = pltpu.get_barrier_semaphore()

    @pl.when(me > 0)
    def _():
        tell(barrier, me - 1)

    @pl.when(me < n - 1)
    def _():
        tell(barrier, me + 1)

    for step in range(1, groups):
        pl.semaphore_signal(
            barrier, inc=1, device_id=group_id(group_peer(step)),
            device_id_type=pl.DeviceIdType.MESH,
        )

    quality_copy = pltpu.make_async_copy(quality_hbm, quality, const_sem.at[3])
    quality_copy.start()
    for step in (2, 3, 1):
        raw_copy(step, 0).start()
    band = n * chunks * CHUNK
    lag_start = pl.multiple_of(group * band + me * (chunks * CHUNK), CHUNK)
    consts = [
        pltpu.make_async_copy(table_hbm, table, const_sem.at[0]),
        pltpu.make_async_copy(
            lag_hbm.at[:, :, pl.ds(lag_start, chunks * CHUNK)], lagtab, const_sem.at[1]
        ),
        pltpu.make_async_copy(inverse_hbm, inverse, const_sem.at[2]),
        pltpu.make_async_copy(taper_hbm, taper, const_sem.at[4]),
    ]

    quality_copy.wait()
    quality_row = quality[...].astype(jnp.float32)
    column = jnp.transpose(jnp.broadcast_to(quality_row, (CHUNK, block)))
    rows = lax.broadcasted_iota(jnp.int32, (8, block), 0)
    masks[me] = jnp.where(rows == 0, jnp.broadcast_to(quality_row, (8, block)), 0.0)
    pl.semaphore_wait(barrier, groups + middle)

    def send_block(step, c):
        raw_copy(step, c).wait()
        slot = ch_peer(step) * chunks + c
        for half in range(2):
            send[slot, half * block:(half + 1) * block, :] = (
                raw[slot, half] * column
            ).astype(jnp.bfloat16)
        data_copy(step, c, me).start()

    @pl.when(middle == 1)
    def _():
        tell(two_away, me - 1)
        tell(two_away, me + 1)
        send_block(2, 0)

    send_block(3, 0)
    for c in range(1, chunks):
        for step in (1, 2, 3) if c < chunks - 1 else (3, 1, 2):
            raw_copy(step, c).start()
    pl.semaphore_wait(two_away, 1)

    @pl.when(middle == 1)
    def _():
        tell(three_away, (n - 1) * (me - 1))

    send_block(1, 0)

    @pl.when(middle == 0)
    def _():
        pl.semaphore_wait(three_away, 1)
        send_block(2, 0)

    for step in range(1, n):
        mask_copy(step, me).start()
    for c in range(1, chunks):
        for step in (1, 2, 3) if c < chunks - 1 else (3, 1, 2):
            send_block(step, c)
    for c in range(chunks):
        raw_copy(0, c).start()
    for copy in consts:
        copy.start()
    acc[...] = jnp.zeros_like(acc)
    for c in range(chunks):
        raw_copy(0, c).wait()
        slot = me * chunks + c
        for half in range(2):
            recv[me, c, half * block:(half + 1) * block, :] = (
                raw[slot, half] * column
            ).astype(jnp.bfloat16)

    for step in range(1, n):
        mask_copy(step, ch_peer(step)).wait_recv()
    flip = jnp.where(
        lax.broadcasted_iota(jnp.int32, (block, block), 0)
        + lax.broadcasted_iota(jnp.int32, (block, block), 1) == block - 1, 1.0, 0.0,
    ).astype(jnp.bfloat16)
    pairs = jnp.zeros((block, block), jnp.float32)
    for low in range(n):
        valid = jnp.where(low + me < n, 1.0, 0.0)
        upper_mask = (masks[lax.rem(low + me, n)] * valid).astype(jnp.bfloat16)
        lower_mask = jnp.dot(
            masks[low].astype(jnp.bfloat16), flip, preferred_element_type=jnp.float32
        )
        pairs += jnp.dot(
            jnp.transpose(lower_mask).astype(jnp.bfloat16), upper_mask,
            preferred_element_type=jnp.float32,
        )
    widened = jnp.concatenate([pairs, jnp.zeros((block, block), jnp.float32)], axis=1)
    sheared = pltpu.roll(widened, 0, 1, stride=1, stride_axis=0)
    counts = jnp.sum(sheared, axis=0, keepdims=True)
    counts = pltpu.roll(jnp.broadcast_to(counts, (8, padded)), padded - block + 1, 1)
    scale = 1.0 / jnp.sqrt(2.0 * FREQS * jnp.maximum(counts[:1], 1.0))

    consts[0].wait()
    consts[1].wait()
    consts[3].wait()

    def lag_weights(c):
        lanes = pl.multiple_of(c * CHUNK, CHUNK)
        taper_lanes = pl.multiple_of((me * chunks + c) * CHUNK, CHUNK)
        weight = taper[:, pl.ds(taper_lanes, CHUNK)]
        wcos = weight * lagtab[0, :, pl.ds(lanes, CHUNK)]
        wsin = weight * lagtab[1, :, pl.ds(lanes, CHUNK)]
        return jnp.concatenate(
            [jnp.concatenate([wcos, -wsin], axis=1), jnp.concatenate([wsin, wcos], axis=1)], axis=0
        ).astype(jnp.bfloat16)

    def half_hats(c, half):
        data = jnp.concatenate([recv[2 * half, c], recv[2 * half + 1, c]], axis=1)
        hats[half] = jnp.dot(table[...], data, preferred_element_type=jnp.float32).astype(
            jnp.bfloat16
        )

    def chunk_hats(c):
        own = me // 2
        data_copy(3, c, ch_peer(3)).wait_recv()
        half_hats(c, own)
        for step in (1, 2):
            data_copy(step, c, ch_peer(step)).wait_recv()
        half_hats(c, 1 - own)

    def lag_sums(c, offsets):
        weights = lag_weights(c)
        for base in range(0, padded, block):
            real, imag = [], []
            for index in range(n):
                lanes = slice((index % 2) * CHUNK, (index % 2 + 1) * CHUNK)
                real.append(hats[index // 2, base:base + block, lanes].astype(jnp.float32))
                imag.append(
                    hats[index // 2, padded + base:padded + base + block, lanes].astype(jnp.float32)
                )
            for j in offsets:
                products = []
                for low in range(n - j):
                    high = low + j
                    products.append(real[low] * real[high] + imag[low] * imag[high])
                    products.append(imag[low] * real[high] - real[low] * imag[high])
                product = jnp.concatenate([p.astype(jnp.bfloat16) for p in products], axis=1)
                repeated = jnp.concatenate([weights] * (n - j), axis=1)
                acc[j, :, base:base + block] += lax.dot_general(
                    repeated, product, (((1,), (1,)), ((), ())),
                    preferred_element_type=jnp.float32,
                )

    def inverse_transform(side):
        total = jnp.concatenate(
            [jnp.concatenate([acc[j, :LAGS, :], acc[j, LAGS:, :]], axis=1) for j in sides[side]],
            axis=0,
        )
        count = len(sides[side]) * LAGS
        high = total.astype(jnp.bfloat16)
        low_part = (total - high.astype(jnp.float32)).astype(jnp.bfloat16)
        both = jnp.dot(
            jnp.concatenate([high, low_part], axis=0), inverse[0],
            preferred_element_type=jnp.float32,
        )
        result = both[:count] + both[count:] + jnp.dot(
            high, inverse[1], preferred_element_type=jnp.float32
        )
        for g in range(groups):
            for index in range(len(sides[side])):
                first = index * LAGS + g * lag_rows
                part[side, g, index] = result[first:first + lag_rows]
        for step in range(1, groups):
            part_copy(side, step, group).start()

    def chunk_step(c, carry):
        chunk_hats(c)
        lag_sums(c, range(n))
        return carry

    lax.fori_loop(0, chunks - 1, chunk_step, 0)
    consts[2].wait()
    chunk_hats(chunks - 1)
    for side in range(2):
        lag_sums(chunks - 1, sides[side])
        inverse_transform(side)

    for side in range(2):
        band_total = part[side, group]
        for step in range(1, groups):
            part_copy(side, step, group_peer(step)).wait_recv()
            band_total += part_in[side, group_peer(step)]
        for index, j in enumerate(sides[side]):
            band_sum[j] = band_total[index]
        for index, j in enumerate(sides[side]):
            @pl.when(me != j)
            def _():
                band_copy(j, me).start()
    final = band_sum[me]
    for step in range(1, n):
        band_wait(ch_peer(step)).wait_recv()
        final += band_in[ch_peer(step)]
    out[0] = final * scale

    for c in range(chunks):
        for step in range(1, n):
            data_copy(step, c, me).wait_send()
    for step in range(1, n):
        mask_copy(step, me).wait_send()
        band_copy(ch_peer(step), me).wait_send()
    for side in range(2):
        for step in range(1, groups):
            part_copy(side, step, group).wait_send()


def fused_shards(spectra, quality, taper):
    block = spectra.shape[1]
    band = spectra.shape[2]
    padded = 2 * block
    n = lax.axis_size("ch")
    subs = lax.axis_size("sub")
    groups = lax.axis_size("fq") * subs
    chunks = band // (n * CHUNK)
    lag_rows = LAGS // groups
    bf16, f32 = jnp.bfloat16, jnp.float32
    in_hbm = pl.BlockSpec(memory_space=pltpu.HBM)
    operands = (
        spectra, quality.reshape(1, block), taper.reshape(1, band),
        jnp.asarray(channel_constant(block)), jnp.asarray(inverse_constant(block)),
        jnp.asarray(lag_constant(LAGS, FREQS)),
    )
    dma = pltpu.SemaphoreType.DMA
    return pl.pallas_call(
        functools.partial(kernel, (n, groups, subs, block, chunks)),
        out_shape=jax.ShapeDtypeStruct((1, lag_rows, padded), f32),
        in_specs=[in_hbm] * 6,
        out_specs=pl.BlockSpec(memory_space=pltpu.VMEM),
        scratch_shapes=[
            pltpu.VMEM((1, block), jnp.int32),
            pltpu.VMEM((1, band), f32),
            pltpu.VMEM((n * chunks, 2, block, CHUNK), f32),
            pltpu.VMEM((n * chunks, padded, CHUNK), bf16),
            pltpu.VMEM((n, chunks, padded, CHUNK), bf16),
            pltpu.VMEM((2 * padded, padded), bf16),
            pltpu.VMEM((2, 2 * padded, padded), bf16),
            pltpu.VMEM((2, LAGS, chunks * CHUNK), f32),
            pltpu.VMEM((n, 8, block), f32),
            pltpu.VMEM((2, 2 * padded, 2 * CHUNK), bf16),
            pltpu.VMEM((n, 2 * LAGS, padded), f32),
            pltpu.VMEM((2, groups, 2, lag_rows, padded), f32),
            pltpu.VMEM((2, groups, 2, lag_rows, padded), f32),
            pltpu.VMEM((n, lag_rows, padded), f32),
            pltpu.VMEM((n, lag_rows, padded), f32),
            dma((n, chunks)), dma((5,)), dma((n - 1, chunks)), dma((n, chunks)),
            dma((n - 1,)), dma((n,)), dma((2, groups - 1)), dma((2, groups)),
            dma((n,)), dma((n,)), pltpu.SemaphoreType.REGULAR, pltpu.SemaphoreType.REGULAR,
        ],
        compiler_params=pltpu.CompilerParams(
            collective_id=0, has_side_effects=True, vmem_limit_bytes=32 << 20
        ),
    )(
        *[pltpu.with_memory_space_constraint(operand, pltpu.HBM) for operand in operands]
    )


def fits(mesh):
    blocks = mesh.shape["ch"]
    groups = mesh.shape["fq"] * mesh.shape["sub"]
    return blocks == 4 and FREQS % (groups * blocks * CHUNK) == 0 and LAGS % (8 * groups) == 0 and groups > 1


def solution(mesh):
    body = fused_shards if fits(mesh) else shards
    in_specs = (P(None, ("grp", "ch"), ("fq", "sub")), P(("grp", "ch")), P(("fq", "sub")))
    out_specs = P(("grp", "ch"), ("fq", "sub"), None)
    return jax.shard_map(body, mesh=mesh, in_specs=in_specs, out_specs=out_specs, check_vma=False)
```

```python
import functools

import jax
import jax.numpy as jnp
import numpy as np
from jax import lax
from jax.experimental import pallas as pl
from jax.experimental.pallas import tpu as pltpu
from jax.sharding import PartitionSpec as P

FREQS = 8192
LAGS = 32
CHUNK = 128
CUT = 1


def passed_along(value, axis, steps):
    count = lax.axis_size(axis)
    pairs = [(source, (source + steps) % count) for source in range(count)]
    return lax.ppermute(value, axis, pairs)


def channel_table(block_size):
    padded = 2 * block_size
    row_index = jnp.arange(padded, dtype=jnp.int32)[:, None]
    col_index = jnp.arange(block_size, dtype=jnp.int32)[None, :]
    angle = 2.0 * jnp.pi / padded * (row_index * col_index % padded).astype(jnp.float32)
    cosine = jnp.cos(angle)
    sine = jnp.sin(angle)
    upper = jnp.concatenate([cosine, sine], axis=1)
    lower = jnp.concatenate([-sine, cosine], axis=1)
    return jnp.concatenate([upper, lower], axis=0).astype(jnp.bfloat16)


def inverse_table(block_size):
    padded = 2 * block_size
    row_index = jnp.arange(padded, dtype=jnp.int32)[:, None]
    col_index = jnp.arange(padded, dtype=jnp.int32)[None, :]
    angle = 2.0 * jnp.pi / padded * (row_index * col_index % padded).astype(jnp.float32)
    return jnp.concatenate([jnp.cos(angle), jnp.sin(angle)], axis=0) / padded


def lag_table(taper_band, start, band_size, lag_count, freq_count):
    freq_index = start + jnp.arange(band_size, dtype=jnp.int32)
    lag_index = jnp.arange(lag_count, dtype=jnp.int32) - lag_count // 2
    phase = lag_index[:, None] * freq_index[None, :] % (2 * freq_count)
    angle = jnp.pi / freq_count * phase.astype(jnp.float32)
    cosine = taper_band[None, :] * jnp.cos(angle)
    sine = taper_band[None, :] * jnp.sin(angle)
    upper = jnp.concatenate([cosine, -sine], axis=1)
    lower = jnp.concatenate([sine, cosine], axis=1)
    return jnp.concatenate([upper, lower], axis=0).astype(jnp.bfloat16)


def cross_spectrum(first, second, sign):
    padded = first.shape[0] // 2
    first_real = first[:padded].astype(jnp.float32)
    first_imag = first[padded:].astype(jnp.float32)
    second_real = second[:padded].astype(jnp.float32)
    second_imag = second[padded:].astype(jnp.float32)
    prod_real = first_real * second_real + first_imag * second_imag
    prod_imag = (first_imag * second_real - first_real * second_imag) * sign
    return jnp.concatenate([prod_real, prod_imag], axis=1).astype(jnp.bfloat16)


def pair_counts(lower_mask, upper_mask):
    block_size = lower_mask.shape[0]
    outer = lower_mask[::-1][:, None] * upper_mask[None, :]
    widened = jnp.pad(outer, ((0, 0), (0, block_size)))
    flat = widened.reshape(-1)[: block_size * (2 * block_size - 1)]
    sheared = flat.reshape(block_size, 2 * block_size - 1)
    histogram = jnp.pad(jnp.sum(sheared, axis=0), (0, 1))
    return jnp.roll(histogram, -(block_size - 1))


def channel_transform(table, data):
    block_size = data.shape[1]
    stacked = data.reshape(2 * block_size, data.shape[2])
    return jnp.dot(table, stacked, preferred_element_type=jnp.float32).astype(jnp.bfloat16)


def shards(spectra, quality, taper):
    block_size = spectra.shape[1]
    band_size = spectra.shape[2]
    padded = 2 * block_size
    blocks = lax.axis_size("ch")
    position = lax.axis_index("ch")
    quality_float = quality.astype(jnp.float32)
    masked = (spectra * quality_float[None, :, None]).astype(jnp.bfloat16)
    mask_half = quality_float.astype(jnp.bfloat16)
    table = channel_table(block_size)
    start = lax.axis_index(("fq", "sub")) * band_size
    own_hat = channel_transform(table, masked)
    weights = lag_table(taper, start, band_size, LAGS, FREQS)

    def accumulate(state, partner_hat, partner_mask, round_index):
        totals, tallies = state
        wrapped = position + round_index >= blocks
        sign = jnp.where(wrapped, -1.0, 1.0).astype(jnp.float32)
        product = cross_spectrum(own_hat, partner_hat, sign)
        term = lax.dot_general(
            weights, product, (((1,), (1,)), ((), ())), preferred_element_type=jnp.float32
        )
        term = term.reshape(2, LAGS, padded)
        offset = jnp.where(wrapped, blocks - round_index, round_index).astype(jnp.int32)
        keep = jnp.where(jnp.logical_and(wrapped, 2 * round_index == blocks), 0.0, 1.0).astype(
            jnp.float32
        )
        lower_mask = jnp.where(wrapped, partner_mask, mask_half).astype(jnp.float32)
        upper_mask = jnp.where(wrapped, mask_half, partner_mask).astype(jnp.float32)
        pairs = pair_counts(lower_mask, upper_mask)
        old_row = lax.dynamic_slice_in_dim(totals, offset, 1, 0)
        totals = lax.dynamic_update_slice_in_dim(totals, old_row + keep * term[None], offset, 0)
        old_tally = lax.dynamic_slice_in_dim(tallies, offset, 1, 0)
        tallies = lax.dynamic_update_slice_in_dim(
            tallies, old_tally + keep * pairs[None], offset, 0
        )
        return (totals, tallies)

    state = (
        jnp.zeros((blocks, 2, LAGS, padded), jnp.float32),
        jnp.zeros((blocks, padded), jnp.float32),
    )
    state = accumulate(state, own_hat, mask_half, 0)

    def advance(round_index, carry):
        current, held, held_mask = carry
        held, held_mask = passed_along((held, held_mask), "ch", -1)
        current = accumulate(current, channel_transform(table, held), held_mask, round_index)
        return (current, held, held_mask)

    state, _, _ = lax.fori_loop(1, blocks // 2 + 1, advance, (state, masked, mask_half))
    totals, tallies = state
    totals, tallies = (
        lax.psum_scatter(totals, "ch", scatter_dimension=0, tiled=True),
        lax.psum_scatter(tallies, "ch", scatter_dimension=0, tiled=True),
    )
    totals = lax.psum_scatter(totals, ("fq", "sub"), scatter_dimension=2, tiled=True)
    combined = jnp.concatenate([totals[0, 0], totals[0, 1]], axis=1)
    lagged = jnp.dot(
        combined,
        inverse_table(block_size),
        precision=lax.Precision.HIGHEST,
        preferred_element_type=jnp.float32,
    )
    scale = jnp.sqrt(2.0 * FREQS * jnp.maximum(tallies[0], 1.0))
    return (lagged / scale[None, :])[None]


def channel_constant(block_size):
    padded = 2 * block_size
    index = np.outer(np.arange(padded), np.arange(block_size)) % padded
    angle = 2.0 * np.pi / padded * index
    cosine, sine = np.cos(angle), np.sin(angle)
    upper = np.concatenate([cosine, sine], axis=1)
    lower = np.concatenate([-sine, cosine], axis=1)
    return np.concatenate([upper, lower], axis=0).astype(jnp.bfloat16)


def inverse_constant(block_size):
    padded = 2 * block_size
    index = np.outer(np.arange(padded), np.arange(padded)) % padded
    angle = 2.0 * np.pi / padded * index
    full = np.concatenate([np.cos(angle), np.sin(angle)], axis=0) / padded
    high = full.astype(np.float32).astype(jnp.bfloat16)
    low = (full - high.astype(np.float64)).astype(np.float32).astype(jnp.bfloat16)
    return np.stack([high, low])


def lag_constant(lag_count, freq_count):
    lag_index = np.arange(lag_count) - lag_count // 2
    phase = np.outer(lag_index, np.arange(freq_count)) % (2 * freq_count)
    angle = np.pi / freq_count * phase
    return np.stack([np.cos(angle), np.sin(angle)]).astype(np.float32)


def kernel(
    sizes, spectra, quality_hbm, taper_hbm, table_hbm, inverse_hbm, lag_hbm, out,
    taper, raw, send, recv, table, inverse, lagtab, masks, hats, acc, part, part_in, band_sum, band_in,
    tail_out, tail_in, tail_sum,
    raw_sem, const_sem, send_sem, recv_sem, mask_sem, mask_send, mask_recv,
    part_send, part_recv, band_send, band_recv, tail_send, tail_recv, two_away, three_away,
):
    n, groups, subs, block, chunks = sizes
    padded = 2 * block
    lag_rows = LAGS // groups
    me = lax.axis_index("ch")
    group = lax.axis_index("fq") * subs + lax.axis_index("sub")
    upper = me // 2
    inner = (me * (n - 1 - me)) // 2
    near = me + 1 - 2 * lax.rem(me, 2)
    far_outer = 3 * (1 - upper)
    far_inner = 2 - upper
    sign = (2 * upper - 1).astype(jnp.float32)
    own_slot = 3 - inner

    def ch_peer(step):
        return lax.rem(me + step, n)

    def group_peer(step):
        return lax.rem(group + step, groups)

    def place(ch, index):
        return {"ch": ch, "fq": index // subs, "sub": lax.rem(index, subs)}

    def raw_copy(slot):
        start = pl.multiple_of(slot * CHUNK, CHUNK)
        return pltpu.make_async_copy(
            spectra.at[:, :, pl.ds(start, CHUNK)], raw.at[slot], raw_sem.at[slot]
        )

    def data_copy(target, c, source):
        return pltpu.make_async_remote_copy(
            send.at[target * chunks + c], recv.at[source, c],
            send_sem.at[target, c], recv_sem.at[source, c],
            device_id={"ch": target}, device_id_type=pl.DeviceIdType.MESH,
        )

    def mask_copy(target, source):
        return pltpu.make_async_remote_copy(
            masks.at[me], masks.at[source], mask_send.at[target], mask_recv.at[source],
            device_id={"ch": target}, device_id_type=pl.DeviceIdType.MESH,
        )

    def part_copy(j, target, source):
        return pltpu.make_async_remote_copy(
            part.at[j, target], part_in.at[j, source],
            part_send.at[j, target], part_recv.at[j, source],
            device_id=place(me, target), device_id_type=pl.DeviceIdType.MESH,
        )

    def band_copy(target, source):
        return pltpu.make_async_remote_copy(
            band_sum.at[target], band_in.at[source], band_send.at[target], band_recv.at[source],
            device_id={"ch": target}, device_id_type=pl.DeviceIdType.MESH,
        )

    def tail_copy(kind, target, source):
        return pltpu.make_async_remote_copy(
            tail_out.at[kind, target], tail_in.at[kind, source],
            tail_send.at[kind, target], tail_recv.at[kind, source],
            device_id=place(3 - me if kind else me, target), device_id_type=pl.DeviceIdType.MESH,
        )

    def tell(semaphore, target):
        pl.semaphore_signal(
            semaphore, inc=1, device_id={"ch": target}, device_id_type=pl.DeviceIdType.MESH
        )

    barrier = pltpu.get_barrier_semaphore()

    @pl.when(me > 0)
    def _():
        tell(barrier, me - 1)

    @pl.when(me < n - 1)
    def _():
        tell(barrier, me + 1)

    for step in range(1, groups):
        pl.semaphore_signal(
            barrier, inc=1, device_id=place(me, group_peer(step)),
            device_id_type=pl.DeviceIdType.MESH,
        )

    quality_copy = pltpu.make_async_copy(quality_hbm, masks.at[me], mask_sem)
    quality_copy.start()
    for target in (far_inner, near, far_outer):
        raw_copy(target * chunks).start()
    order = []
    inner_order = [(t, c) for c in range(1, chunks) for t in (far_outer, near)]
    inner_order += [(far_inner, c) for c in range(1, chunks)]
    outer_order = [(t, c) for c in range(1, chunks) for t in (far_outer, far_inner, near)]
    for (inner_target, inner_c), (outer_target, outer_c) in zip(inner_order, outer_order):
        order.append((
            inner * inner_target + (1 - inner) * outer_target,
            inner * inner_c + (1 - inner) * outer_c,
        ))
    band = n * chunks * CHUNK
    lag_start = pl.multiple_of(group * band, CHUNK)
    consts = [
        pltpu.make_async_copy(table_hbm, table, const_sem.at[0]),
        pltpu.make_async_copy(lag_hbm.at[:, :, pl.ds(lag_start, band)], lagtab, const_sem.at[1]),
        pltpu.make_async_copy(inverse_hbm, inverse, const_sem.at[2]),
        pltpu.make_async_copy(taper_hbm, taper, const_sem.at[3]),
    ]

    quality_copy.wait()
    quality_row = masks[me].astype(jnp.float32)
    column = jnp.transpose(jnp.broadcast_to(quality_row, (CHUNK, block)))
    pl.semaphore_wait(barrier, groups + inner)

    def mask_block(slot):
        raw_copy(slot).wait()
        for half in range(2):
            send[slot, half * block:(half + 1) * block, :] = (
                raw[slot, half] * column
            ).astype(jnp.bfloat16)

    def send_block(target, c):
        mask_block(target * chunks + c)
        data_copy(target, c, me).start()

    @pl.when(inner == 1)
    def _():
        tell(two_away, me - 1)
        tell(two_away, me + 1)
        send_block(far_inner, 0)

    send_block(near, 0)
    for target, c in order:
        raw_copy(target * chunks + c).start()
    for c in range(chunks):
        raw_copy(me * chunks + c).start()
    pl.semaphore_wait(two_away, 1)

    @pl.when(inner == 1)
    def _():
        tell(three_away, (n - 1) * (me - 1))
        send_block(far_outer, 0)

    @pl.when(inner == 0)
    def _():
        send_block(far_inner, 0)
        pl.semaphore_wait(three_away, 1)
        send_block(far_outer, 0)

    for step in range(1, n):
        mask_copy(ch_peer(step), me).start()
    for target, c in order[:3]:
        send_block(target, c)
    for copy in consts:
        copy.start()
    for target, c in order[3:]:
        send_block(target, c)
    for c in range(chunks):
        mask_block(me * chunks + c)
    acc[...] = jnp.zeros_like(acc)
    consts[0].wait()
    consts[1].wait()
    consts[3].wait()

    def lag_factors(start, width):
        lanes = pl.ds(pl.multiple_of(start, CHUNK), width)
        weight = taper[:, lanes]
        return weight * lagtab[0, :, lanes], weight * lagtab[1, :, lanes]

    def transform(blocks_of_data):
        data = jnp.concatenate(blocks_of_data, axis=1)
        return jnp.dot(table[...], data, preferred_element_type=jnp.float32).astype(jnp.bfloat16)

    def contract(weights, product):
        return lax.dot_general(
            weights, product, (((1,), (1,)), ((), ())), preferred_element_type=jnp.float32
        )

    def own_pair(slot):
        hat = transform([send[slot], send[slot + 1]])
        wcos, wsin = lag_factors(slot * CHUNK, 2 * CHUNK)
        weights = jnp.concatenate([wcos, wsin], axis=0).astype(jnp.bfloat16)
        real = hat[:padded].astype(jnp.float32)
        imag = hat[padded:].astype(jnp.float32)
        power = (real * real + imag * imag).astype(jnp.bfloat16)
        acc[0] += contract(weights, power)
        return hat

    def other_step(index, carry):
        step = 1 + index // (chunks // 2)
        half = lax.rem(index, chunks // 2)
        own_pair(ch_peer(step) * chunks + 2 * half)
        return carry

    def own_step(half, carry):
        hat = own_pair(me * chunks + 2 * half)
        for index in range(2):
            hats[own_slot, 2 * half + index] = hat[:, index * CHUNK:(index + 1) * CHUNK]
        return carry

    lax.fori_loop(0, chunks // 2, own_step, 0)
    lax.fori_loop(0, (n - 1) * (chunks // 2), other_step, 0)

    def spectrum(slot, c, base):
        return (
            hats[slot, c, base:base + block].astype(jnp.float32),
            hats[slot, c, padded + base:padded + base + block].astype(jnp.float32),
        )

    def lag_sums(c, pairs):
        wcos, wsin = lag_factors((me * chunks + c) * CHUNK, CHUNK)
        weights = jnp.concatenate(
            [
                jnp.concatenate([wcos, -sign * wsin], axis=1),
                jnp.concatenate([wsin, sign * wcos], axis=1),
            ],
            axis=0,
        ).astype(jnp.bfloat16)
        slots = sorted({slot for _, low, high in pairs for slot in (low, high)})
        for base in range(0, padded, block):
            value = {slot: spectrum(slot, c, base) for slot in slots}
            for j in sorted({j for j, _, _ in pairs}):
                products = []
                for index, low, high in pairs:
                    if index == j:
                        low_real, low_imag = value[low]
                        high_real, high_imag = value[high]
                        products.append(low_real * high_real + low_imag * high_imag)
                        products.append(low_imag * high_real - low_real * high_imag)
                product = jnp.concatenate([p.astype(jnp.bfloat16) for p in products], axis=1)
                repeated = jnp.concatenate([weights] * (len(products) // 2), axis=1)
                acc[j, :, base:base + block] += contract(repeated, product)

    def inverse_transform(totals):
        total = jnp.concatenate(
            [jnp.concatenate([t[:LAGS], t[LAGS:]], axis=1) for t in totals], axis=0
        )
        count = len(totals) * LAGS
        high = total.astype(jnp.bfloat16)
        low_part = (total - high.astype(jnp.float32)).astype(jnp.bfloat16)
        both = jnp.dot(
            jnp.concatenate([high, low_part], axis=0), inverse[0],
            preferred_element_type=jnp.float32,
        )
        return both[:count] + both[count:] + jnp.dot(
            high, inverse[1], preferred_element_type=jnp.float32
        )

    def share(offsets):
        result = inverse_transform([acc[j] for j in offsets])
        for index, j in enumerate(offsets):
            for g in range(groups):
                first = index * LAGS + g * lag_rows
                part[j, g] = result[first:first + lag_rows]
            for step in range(1, groups):
                part_copy(j, group_peer(step), group).start()

    def collect(j):
        total = part[j, group]
        for step in range(1, groups):
            part_copy(j, group_peer(step), group_peer(step)).wait_recv()
            total += part_in[j, group_peer(step)]
        band_sum[j] = total

        @pl.when(me != j)
        def _():
            band_copy(j, me).start()

    consts[2].wait()
    share((0,))

    for step in range(1, n):
        mask_copy(ch_peer(step), ch_peer(step)).wait_recv()
    flip = jnp.where(
        lax.broadcasted_iota(jnp.int32, (block, block), 0)
        + lax.broadcasted_iota(jnp.int32, (block, block), 1) == block - 1, 1.0, 0.0,
    ).astype(jnp.bfloat16)

    def mask_rows(index):
        return jnp.broadcast_to(masks[index].astype(jnp.float32), (8, block))

    first_row = jnp.where(lax.broadcasted_iota(jnp.int32, (8, block), 0) == 0, 1.0, 0.0)
    pairs = jnp.zeros((block, block), jnp.float32)
    for low in range(n):
        valid = jnp.where(low + me < n, 1.0, 0.0)
        upper_mask = (mask_rows(lax.rem(low + me, n)) * (first_row * valid)).astype(jnp.bfloat16)
        lower_mask = jnp.dot(
            mask_rows(low).astype(jnp.bfloat16), flip, preferred_element_type=jnp.float32
        )
        pairs += jnp.dot(
            jnp.transpose(lower_mask).astype(jnp.bfloat16), upper_mask,
            preferred_element_type=jnp.float32,
        )
    widened = jnp.concatenate([pairs, jnp.zeros((block, block), jnp.float32)], axis=1)
    sheared = pltpu.roll(widened, 0, 1, stride=1, stride_axis=0)
    counts = jnp.sum(sheared, axis=0, keepdims=True)
    counts = pltpu.roll(jnp.broadcast_to(counts, (8, padded)), padded - block + 1, 1)
    scale = 1.0 / jnp.sqrt(2.0 * FREQS * jnp.maximum(counts[:1], 1.0))

    def first_phase(c, carry):
        data_copy(near, c, near).wait_recv()
        data_copy(far_outer, c, far_outer).wait_recv()
        hat = transform([recv[near, c], recv[far_outer, c]])
        hats[5 - own_slot, c] = hat[:, :CHUNK]
        hats[0, c] = hat[:, CHUNK:]
        lag_sums(c, ((1, 2, 3), (2, 0, 2), (3, 0, 3)))
        return carry

    def second_phase(c, carry):
        data_copy(far_inner, c, far_inner).wait_recv()
        hats[1, c] = transform([recv[far_inner, c]])
        lag_sums(c, ((1, 0, 1), (1, 1, 2), (2, 1, 3)))
        return carry

    lax.fori_loop(0, chunks, first_phase, 0)
    share((3,))
    collect(0)
    lax.fori_loop(0, inner * CUT + (1 - inner) * chunks, second_phase, 0)
    share((1, 2))
    collect(3)
    tail_sum[...] = jnp.zeros_like(tail_sum)

    @pl.when(inner == 0)
    def _():
        collect(1)
        collect(2)

    @pl.when(inner == 1)
    def _():
        for j in (1, 2):
            acc[j] = jnp.zeros((2 * LAGS, padded), jnp.float32)
        for c in range(CUT, chunks):
            if c == chunks - 1:
                collect(1)
                collect(2)
            second_phase(c, 0)
        for kind in (1, 0):
            result = inverse_transform([acc[3 - me if kind else me]])
            for g in range(groups):
                rows = result[g * lag_rows:(g + 1) * lag_rows]
                piece = jnp.concatenate([rows[:, :block], rows[:, block:]], axis=0)
                tail_out[kind, g] = piece.astype(jnp.bfloat16)
            for step in range(1 - kind, groups):
                tail_copy(kind, group_peer(step), group).start()
        total = tail_out[0, group].astype(jnp.float32)
        for kind in (0, 1):
            for step in range(1 - kind, groups):
                tail_copy(kind, group_peer(step), group_peer(step)).wait_recv()
                total += tail_in[kind, group_peer(step)].astype(jnp.float32)
        tail_sum[...] = jnp.concatenate([total[:lag_rows], total[lag_rows:]], axis=1)

    final = band_sum[me] + tail_sum[...]
    for step in range(1, n):
        band_copy(ch_peer(step), ch_peer(step)).wait_recv()
        final += band_in[ch_peer(step)]
    out[0] = final * scale

    for step in range(1, n):
        for c in range(chunks):
            data_copy(ch_peer(step), c, me).wait_send()
        mask_copy(ch_peer(step), me).wait_send()
        band_copy(ch_peer(step), me).wait_send()
    for j in range(n):
        for step in range(1, groups):
            part_copy(j, group_peer(step), group).wait_send()

    @pl.when(inner == 1)
    def _():
        for kind in (1, 0):
            for step in range(1 - kind, groups):
                tail_copy(kind, group_peer(step), group).wait_send()


def fused_shards(spectra, quality, taper):
    block = spectra.shape[1]
    band = spectra.shape[2]
    padded = 2 * block
    n = lax.axis_size("ch")
    subs = lax.axis_size("sub")
    groups = lax.axis_size("fq") * subs
    chunks = band // (n * CHUNK)
    lag_rows = LAGS // groups
    bf16, f32 = jnp.bfloat16, jnp.float32
    in_hbm = pl.BlockSpec(memory_space=pltpu.HBM)
    operands = (
        spectra, quality.reshape(1, block), taper.reshape(1, band),
        jnp.asarray(channel_constant(block)), jnp.asarray(inverse_constant(block)),
        jnp.asarray(lag_constant(LAGS, FREQS)),
    )
    dma = pltpu.SemaphoreType.DMA
    regular = pltpu.SemaphoreType.REGULAR
    return pl.pallas_call(
        functools.partial(kernel, (n, groups, subs, block, chunks)),
        out_shape=jax.ShapeDtypeStruct((1, lag_rows, padded), f32),
        in_specs=[in_hbm] * 6,
        out_specs=pl.BlockSpec(memory_space=pltpu.VMEM),
        scratch_shapes=[
            pltpu.VMEM((1, band), f32),
            pltpu.VMEM((n * chunks, 2, block, CHUNK), f32),
            pltpu.VMEM((n * chunks, padded, CHUNK), bf16),
            pltpu.VMEM((n, chunks, padded, CHUNK), bf16),
            pltpu.VMEM((2 * padded, padded), bf16),
            pltpu.VMEM((2, 2 * padded, padded), bf16),
            pltpu.VMEM((2, LAGS, band), f32),
            pltpu.VMEM((n, 1, block), jnp.int32),
            pltpu.VMEM((n, chunks, 2 * padded, CHUNK), bf16),
            pltpu.VMEM((n, 2 * LAGS, padded), f32),
            pltpu.VMEM((n, groups, lag_rows, padded), f32),
            pltpu.VMEM((n, groups, lag_rows, padded), f32),
            pltpu.VMEM((n, lag_rows, padded), f32),
            pltpu.VMEM((n, lag_rows, padded), f32),
            pltpu.VMEM((2, groups, 2 * lag_rows, block), bf16),
            pltpu.VMEM((2, groups, 2 * lag_rows, block), bf16),
            pltpu.VMEM((lag_rows, padded), f32),
            dma((n * chunks,)), dma((4,)), dma((n, chunks)), dma((n, chunks)),
            dma, dma((n,)), dma((n,)), dma((n, groups)), dma((n, groups)),
            dma((n,)), dma((n,)), dma((2, groups)), dma((2, groups)), regular, regular,
        ],
        compiler_params=pltpu.CompilerParams(
            collective_id=0, has_side_effects=True, vmem_limit_bytes=40 << 20
        ),
    )(
        *[pltpu.with_memory_space_constraint(operand, pltpu.HBM) for operand in operands]
    )


def fits(mesh):
    blocks = mesh.shape["ch"]
    groups = mesh.shape["fq"] * mesh.shape["sub"]
    return blocks == 4 and FREQS % (2 * groups * blocks * CHUNK) == 0 and LAGS % (8 * groups) == 0 and groups > 1


def solution(mesh):
    body = fused_shards if fits(mesh) else shards
    in_specs = (P(None, ("grp", "ch"), ("fq", "sub")), P(("grp", "ch")), P(("fq", "sub")))
    out_specs = P(("grp", "ch"), ("fq", "sub"), None)
    return jax.shard_map(body, mesh=mesh, in_specs=in_specs, out_specs=out_specs, check_vma=False)
```

```python
import functools

import jax
import jax.numpy as jnp
import numpy as np
from jax import lax
from jax.experimental import pallas as pl
from jax.experimental.pallas import tpu as pltpu
from jax.sharding import PartitionSpec as P

FREQS = 8192
LAGS = 32
CHUNK = 128


def passed_along(value, axis, steps):
    count = lax.axis_size(axis)
    pairs = [(source, (source + steps) % count) for source in range(count)]
    return lax.ppermute(value, axis, pairs)


def channel_table(block_size):
    padded = 2 * block_size
    row_index = jnp.arange(padded, dtype=jnp.int32)[:, None]
    col_index = jnp.arange(block_size, dtype=jnp.int32)[None, :]
    angle = 2.0 * jnp.pi / padded * (row_index * col_index % padded).astype(jnp.float32)
    cosine = jnp.cos(angle)
    sine = jnp.sin(angle)
    upper = jnp.concatenate([cosine, sine], axis=1)
    lower = jnp.concatenate([-sine, cosine], axis=1)
    return jnp.concatenate([upper, lower], axis=0).astype(jnp.bfloat16)


def inverse_table(block_size):
    padded = 2 * block_size
    row_index = jnp.arange(padded, dtype=jnp.int32)[:, None]
    col_index = jnp.arange(padded, dtype=jnp.int32)[None, :]
    angle = 2.0 * jnp.pi / padded * (row_index * col_index % padded).astype(jnp.float32)
    return jnp.concatenate([jnp.cos(angle), jnp.sin(angle)], axis=0) / padded


def lag_table(taper_band, start, band_size, lag_count, freq_count):
    freq_index = start + jnp.arange(band_size, dtype=jnp.int32)
    lag_index = jnp.arange(lag_count, dtype=jnp.int32) - lag_count // 2
    phase = lag_index[:, None] * freq_index[None, :] % (2 * freq_count)
    angle = jnp.pi / freq_count * phase.astype(jnp.float32)
    cosine = taper_band[None, :] * jnp.cos(angle)
    sine = taper_band[None, :] * jnp.sin(angle)
    upper = jnp.concatenate([cosine, -sine], axis=1)
    lower = jnp.concatenate([sine, cosine], axis=1)
    return jnp.concatenate([upper, lower], axis=0).astype(jnp.bfloat16)


def cross_spectrum(first, second, sign):
    padded = first.shape[0] // 2
    first_real = first[:padded].astype(jnp.float32)
    first_imag = first[padded:].astype(jnp.float32)
    second_real = second[:padded].astype(jnp.float32)
    second_imag = second[padded:].astype(jnp.float32)
    prod_real = first_real * second_real + first_imag * second_imag
    prod_imag = (first_imag * second_real - first_real * second_imag) * sign
    return jnp.concatenate([prod_real, prod_imag], axis=1).astype(jnp.bfloat16)


def pair_counts(lower_mask, upper_mask):
    block_size = lower_mask.shape[0]
    outer = lower_mask[::-1][:, None] * upper_mask[None, :]
    widened = jnp.pad(outer, ((0, 0), (0, block_size)))
    flat = widened.reshape(-1)[: block_size * (2 * block_size - 1)]
    sheared = flat.reshape(block_size, 2 * block_size - 1)
    histogram = jnp.pad(jnp.sum(sheared, axis=0), (0, 1))
    return jnp.roll(histogram, -(block_size - 1))


def channel_transform(table, data):
    block_size = data.shape[1]
    stacked = data.reshape(2 * block_size, data.shape[2])
    return jnp.dot(table, stacked, preferred_element_type=jnp.float32).astype(jnp.bfloat16)


def shards(spectra, quality, taper):
    block_size = spectra.shape[1]
    band_size = spectra.shape[2]
    padded = 2 * block_size
    blocks = lax.axis_size("ch")
    position = lax.axis_index("ch")
    quality_float = quality.astype(jnp.float32)
    masked = (spectra * quality_float[None, :, None]).astype(jnp.bfloat16)
    mask_half = quality_float.astype(jnp.bfloat16)
    table = channel_table(block_size)
    start = lax.axis_index(("fq", "sub")) * band_size
    own_hat = channel_transform(table, masked)
    weights = lag_table(taper, start, band_size, LAGS, FREQS)

    def accumulate(state, partner_hat, partner_mask, round_index):
        totals, tallies = state
        wrapped = position + round_index >= blocks
        sign = jnp.where(wrapped, -1.0, 1.0).astype(jnp.float32)
        product = cross_spectrum(own_hat, partner_hat, sign)
        term = lax.dot_general(
            weights, product, (((1,), (1,)), ((), ())), preferred_element_type=jnp.float32
        )
        term = term.reshape(2, LAGS, padded)
        offset = jnp.where(wrapped, blocks - round_index, round_index).astype(jnp.int32)
        keep = jnp.where(jnp.logical_and(wrapped, 2 * round_index == blocks), 0.0, 1.0).astype(
            jnp.float32
        )
        lower_mask = jnp.where(wrapped, partner_mask, mask_half).astype(jnp.float32)
        upper_mask = jnp.where(wrapped, mask_half, partner_mask).astype(jnp.float32)
        pairs = pair_counts(lower_mask, upper_mask)
        old_row = lax.dynamic_slice_in_dim(totals, offset, 1, 0)
        totals = lax.dynamic_update_slice_in_dim(totals, old_row + keep * term[None], offset, 0)
        old_tally = lax.dynamic_slice_in_dim(tallies, offset, 1, 0)
        tallies = lax.dynamic_update_slice_in_dim(
            tallies, old_tally + keep * pairs[None], offset, 0
        )
        return (totals, tallies)

    state = (
        jnp.zeros((blocks, 2, LAGS, padded), jnp.float32),
        jnp.zeros((blocks, padded), jnp.float32),
    )
    state = accumulate(state, own_hat, mask_half, 0)

    def advance(round_index, carry):
        current, held, held_mask = carry
        held, held_mask = passed_along((held, held_mask), "ch", -1)
        current = accumulate(current, channel_transform(table, held), held_mask, round_index)
        return (current, held, held_mask)

    state, _, _ = lax.fori_loop(1, blocks // 2 + 1, advance, (state, masked, mask_half))
    totals, tallies = state
    totals, tallies = (
        lax.psum_scatter(totals, "ch", scatter_dimension=0, tiled=True),
        lax.psum_scatter(tallies, "ch", scatter_dimension=0, tiled=True),
    )
    totals = lax.psum_scatter(totals, ("fq", "sub"), scatter_dimension=2, tiled=True)
    combined = jnp.concatenate([totals[0, 0], totals[0, 1]], axis=1)
    lagged = jnp.dot(
        combined,
        inverse_table(block_size),
        precision=lax.Precision.HIGHEST,
        preferred_element_type=jnp.float32,
    )
    scale = jnp.sqrt(2.0 * FREQS * jnp.maximum(tallies[0], 1.0))
    return (lagged / scale[None, :])[None]


def channel_constant(block_size):
    padded = 2 * block_size
    index = np.outer(np.arange(padded), np.arange(block_size)) % padded
    angle = 2.0 * np.pi / padded * index
    cosine, sine = np.cos(angle), np.sin(angle)
    upper = np.concatenate([cosine, sine], axis=1)
    lower = np.concatenate([-sine, cosine], axis=1)
    return np.concatenate([upper, lower], axis=0).astype(jnp.bfloat16)


def inverse_constant(block_size):
    padded = 2 * block_size
    index = np.outer(np.arange(padded), np.arange(padded)) % padded
    angle = 2.0 * np.pi / padded * index
    full = np.concatenate([np.cos(angle), np.sin(angle)], axis=0) / padded
    high = full.astype(np.float32).astype(jnp.bfloat16)
    low = (full - high.astype(np.float64)).astype(np.float32).astype(jnp.bfloat16)
    return np.stack([high, low])


def lag_constant(lag_count, freq_count):
    lag_index = np.arange(lag_count) - lag_count // 2
    phase = np.outer(lag_index, np.arange(freq_count)) % (2 * freq_count)
    angle = np.pi / freq_count * phase
    return np.stack([np.cos(angle), np.sin(angle)]).astype(np.float32)


def kernel(
    sizes, spectra, quality_hbm, taper_hbm, table_hbm, inverse_hbm, lag_hbm, out,
    taper, raw, send, recv, table, inverse, lagtab, masks, hats, acc, part, part_in, band_sum, band_in, near_in,
    tail_out, tail_in,
    raw_sem, const_sem, send_sem, recv_sem, mask_sem, mask_send, mask_recv,
    part_send, part_recv, band_send, band_recv, near_send, near_recv, tail_send, tail_recv, two_away, three_away,
):
    n, groups, subs, block, chunks = sizes
    padded = 2 * block
    lag_rows = LAGS // groups
    me = lax.axis_index("ch")
    group = lax.axis_index("fq") * subs + lax.axis_index("sub")
    upper = me // 2
    inner = (me * (n - 1 - me)) // 2
    near = me + 1 - 2 * lax.rem(me, 2)
    far_outer = 3 * (1 - upper)
    far_inner = 2 - upper
    sign = (2 * upper - 1).astype(jnp.float32)
    own_slot = 3 - inner

    def ch_peer(step):
        return lax.rem(me + step, n)

    def group_peer(step):
        return lax.rem(group + step, groups)

    def place(ch, index):
        return {"ch": ch, "fq": index // subs, "sub": lax.rem(index, subs)}

    def raw_copy(slot):
        start = pl.multiple_of(slot * CHUNK, CHUNK)
        return pltpu.make_async_copy(
            spectra.at[:, :, pl.ds(start, CHUNK)], raw.at[slot], raw_sem.at[slot]
        )

    def data_copy(target, c, source):
        return pltpu.make_async_remote_copy(
            send.at[target * chunks + c], recv.at[source, c],
            send_sem.at[target, c], recv_sem.at[source, c],
            device_id={"ch": target}, device_id_type=pl.DeviceIdType.MESH,
        )

    def mask_copy(target, source):
        return pltpu.make_async_remote_copy(
            masks.at[me], masks.at[source], mask_send.at[target], mask_recv.at[source],
            device_id={"ch": target}, device_id_type=pl.DeviceIdType.MESH,
        )

    def part_copy(j, target, source):
        return pltpu.make_async_remote_copy(
            part.at[j, target], part_in.at[j, source],
            part_send.at[j, target], part_recv.at[j, source],
            device_id=place(me, target), device_id_type=pl.DeviceIdType.MESH,
        )

    def band_copy(target, source):
        return pltpu.make_async_remote_copy(
            band_sum.at[target], band_in.at[source], band_send.at[target], band_recv.at[source],
            device_id={"ch": target}, device_id_type=pl.DeviceIdType.MESH,
        )

    def near_copy(j):
        return pltpu.make_async_remote_copy(
            band_sum.at[j], near_in.at[j], near_send.at[j], near_recv.at[j],
            device_id={"ch": near}, device_id_type=pl.DeviceIdType.MESH,
        )

    def tail_copy(kind, target, source):
        return pltpu.make_async_remote_copy(
            tail_out.at[kind, target], tail_in.at[kind, source],
            tail_send.at[kind, target], tail_recv.at[kind, source],
            device_id=place(3 - me if kind else me, target), device_id_type=pl.DeviceIdType.MESH,
        )

    def tell(semaphore, target):
        pl.semaphore_signal(
            semaphore, inc=1, device_id={"ch": target}, device_id_type=pl.DeviceIdType.MESH
        )

    barrier = pltpu.get_barrier_semaphore()

    @pl.when(me > 0)
    def _():
        tell(barrier, me - 1)

    @pl.when(me < n - 1)
    def _():
        tell(barrier, me + 1)

    for step in range(1, groups):
        pl.semaphore_signal(
            barrier, inc=1, device_id=place(me, group_peer(step)),
            device_id_type=pl.DeviceIdType.MESH,
        )

    quality_copy = pltpu.make_async_copy(quality_hbm, masks.at[me], mask_sem)
    quality_copy.start()
    for target in (far_inner, near, far_outer):
        raw_copy(target * chunks).start()
    inner_order = [
        (far_outer, 1), (near, 1), (far_outer, 2), (near, 2), (far_outer, 3), (near, 3),
        (far_inner, 1), (far_inner, 2), (far_inner, 3),
    ]
    outer_order = [
        (far_outer, 1), (far_inner, 1), (near, 1), (far_outer, 2), (far_inner, 2), (near, 2),
        (far_outer, 3), (far_inner, 3), (near, 3),
    ]
    order = [
        (inner * a + (1 - inner) * b, inner * a_chunk + (1 - inner) * b_chunk)
        for (a, a_chunk), (b, b_chunk) in zip(inner_order, outer_order)
    ]
    band = n * chunks * CHUNK
    lag_start = pl.multiple_of(group * band, CHUNK)
    consts = [
        pltpu.make_async_copy(table_hbm, table, const_sem.at[0]),
        pltpu.make_async_copy(lag_hbm.at[:, :, pl.ds(lag_start, band)], lagtab, const_sem.at[1]),
        pltpu.make_async_copy(inverse_hbm, inverse, const_sem.at[2]),
        pltpu.make_async_copy(taper_hbm, taper, const_sem.at[3]),
    ]

    quality_copy.wait()
    quality_row = masks[me].astype(jnp.float32)
    column = jnp.transpose(jnp.broadcast_to(quality_row, (CHUNK, block)))
    pl.semaphore_wait(barrier, groups + inner)

    def mask_block(slot):
        raw_copy(slot).wait()
        for half in range(2):
            send[slot, half * block:(half + 1) * block, :] = (
                raw[slot, half] * column
            ).astype(jnp.bfloat16)

    def send_block(target, c):
        mask_block(target * chunks + c)
        data_copy(target, c, me).start()

    @pl.when(inner == 1)
    def _():
        tell(two_away, me - 1)
        tell(two_away, me + 1)
        send_block(far_inner, 0)

    send_block(near, 0)
    for target, c in order:
        raw_copy(target * chunks + c).start()
    for c in range(chunks):
        raw_copy(me * chunks + c).start()

    @pl.when(inner == 1)
    def _():
        pl.semaphore_wait(two_away, 1)
        tell(three_away, (n - 1) * (me - 1))
        send_block(far_outer, 0)

    @pl.when(inner == 0)
    def _():
        pl.semaphore_wait(two_away, 1)
        send_block(far_inner, 0)
        pl.semaphore_wait(three_away, 1)
        send_block(far_outer, 0)

    for step in range(1, n):
        mask_copy(ch_peer(step), me).start()
    for target, c in order[:2]:
        send_block(target, c)
    for copy in consts:
        copy.start()
    for target, c in order[2:6]:
        send_block(target, c)
    for target, c in order[6:]:
        mask_block(target * chunks + c)
    for c in range(chunks):
        mask_block(me * chunks + c)
    acc[...] = jnp.zeros_like(acc)
    consts[0].wait()
    consts[1].wait()
    consts[3].wait()

    def lag_factors(start, width):
        lanes = pl.ds(pl.multiple_of(start, CHUNK), width)
        weight = taper[:, lanes]
        return weight * lagtab[0, :, lanes], weight * lagtab[1, :, lanes]

    def transform(blocks_of_data):
        data = jnp.concatenate(blocks_of_data, axis=1)
        return jnp.dot(table[...], data, preferred_element_type=jnp.float32).astype(jnp.bfloat16)

    def contract(weights, product):
        return lax.dot_general(
            weights, product, (((1,), (1,)), ((), ())), preferred_element_type=jnp.float32
        )

    def own_pair(slot):
        hat = transform([send[slot], send[slot + 1]])
        wcos, wsin = lag_factors(slot * CHUNK, 2 * CHUNK)
        weights = jnp.concatenate([wcos, wsin], axis=0).astype(jnp.bfloat16)
        real = hat[:padded].astype(jnp.float32)
        imag = hat[padded:].astype(jnp.float32)
        power = (real * real + imag * imag).astype(jnp.bfloat16)
        acc[0] += contract(weights, power)
        return hat

    def other_step(index, carry):
        step = 1 + index // (chunks // 2)
        half = lax.rem(index, chunks // 2)
        own_pair(ch_peer(step) * chunks + 2 * half)
        return carry

    def own_step(half, carry):
        hat = own_pair(me * chunks + 2 * half)
        for index in range(2):
            hats[own_slot, 2 * half + index] = hat[:, index * CHUNK:(index + 1) * CHUNK]
        return carry

    lax.fori_loop(0, chunks // 2, own_step, 0)
    lax.fori_loop(0, (n - 1) * (chunks // 2), other_step, 0)

    def spectrum(slot, c, base):
        return (
            hats[slot, c, base:base + block].astype(jnp.float32),
            hats[slot, c, padded + base:padded + base + block].astype(jnp.float32),
        )

    def lag_sums(c, pairs):
        wcos, wsin = lag_factors((me * chunks + c) * CHUNK, CHUNK)
        weights = jnp.concatenate(
            [
                jnp.concatenate([wcos, -sign * wsin], axis=1),
                jnp.concatenate([wsin, sign * wcos], axis=1),
            ],
            axis=0,
        ).astype(jnp.bfloat16)
        slots = sorted({slot for _, low, high in pairs for slot in (low, high)})
        for base in range(0, padded, block):
            value = {slot: spectrum(slot, c, base) for slot in slots}
            for j in sorted({j for j, _, _ in pairs}):
                products = []
                for index, low, high in pairs:
                    if index == j:
                        low_real, low_imag = value[low]
                        high_real, high_imag = value[high]
                        products.append(low_real * high_real + low_imag * high_imag)
                        products.append(low_imag * high_real - low_real * high_imag)
                product = jnp.concatenate([p.astype(jnp.bfloat16) for p in products], axis=1)
                repeated = jnp.concatenate([weights] * (len(products) // 2), axis=1)
                acc[j, :, base:base + block] += contract(repeated, product)

    def inverse_transform(totals, fine=True):
        total = jnp.concatenate(
            [jnp.concatenate([t[:LAGS], t[LAGS:]], axis=1) for t in totals], axis=0
        )
        count = len(totals) * LAGS
        high = total.astype(jnp.bfloat16)
        low_part = (total - high.astype(jnp.float32)).astype(jnp.bfloat16)
        both = jnp.dot(
            jnp.concatenate([high, low_part], axis=0), inverse[0],
            preferred_element_type=jnp.float32,
        )
        result = both[:count] + both[count:]
        if fine:
            result += jnp.dot(high, inverse[1], preferred_element_type=jnp.float32)
        return result

    def share(offsets):
        result = inverse_transform([acc[j] for j in offsets])
        for index, j in enumerate(offsets):
            for g in range(groups):
                first = index * LAGS + g * lag_rows
                part[j, g] = result[first:first + lag_rows]
            for step in range(1, groups):
                part_copy(j, group_peer(step), group).start()

    def settle(j):
        total = part[j, group]
        for step in range(1, groups):
            part_copy(j, group_peer(step), group_peer(step)).wait_recv()
            total += part_in[j, group_peer(step)]
        band_sum[j] = total

        @pl.when(jnp.logical_and(inner == 1, far_outer == j))
        def _():
            near_copy(j).wait_recv()
            band_sum[j] += near_in[j]

        @pl.when(inner == 1)
        def _():
            band_copy(j, me).start()

        @pl.when(jnp.logical_and(inner == 0, me != j))
        def _():
            near_copy(j).start()

    consts[2].wait()
    share((0,))

    for step in range(1, n):
        mask_copy(ch_peer(step), ch_peer(step)).wait_recv()
    flip = jnp.where(
        lax.broadcasted_iota(jnp.int32, (block, block), 0)
        + lax.broadcasted_iota(jnp.int32, (block, block), 1) == block - 1, 1.0, 0.0,
    ).astype(jnp.bfloat16)

    def mask_rows(index):
        return jnp.broadcast_to(masks[index].astype(jnp.float32), (8, block))

    first_row = jnp.where(lax.broadcasted_iota(jnp.int32, (8, block), 0) == 0, 1.0, 0.0)
    pairs = jnp.zeros((block, block), jnp.float32)
    for low in range(n):
        valid = jnp.where(low + me < n, 1.0, 0.0)
        upper_mask = (mask_rows(lax.rem(low + me, n)) * (first_row * valid)).astype(jnp.bfloat16)
        lower_mask = jnp.dot(
            mask_rows(low).astype(jnp.bfloat16), flip, preferred_element_type=jnp.float32
        )
        pairs += jnp.dot(
            jnp.transpose(lower_mask).astype(jnp.bfloat16), upper_mask,
            preferred_element_type=jnp.float32,
        )
    widened = jnp.concatenate([pairs, jnp.zeros((block, block), jnp.float32)], axis=1)
    sheared = pltpu.roll(widened, 0, 1, stride=1, stride_axis=0)
    counts = jnp.sum(sheared, axis=0, keepdims=True)
    counts = pltpu.roll(jnp.broadcast_to(counts, (8, padded)), padded - block + 1, 1)
    scale = 1.0 / jnp.sqrt(2.0 * FREQS * jnp.maximum(counts[:1], 1.0))

    def first_phase(c, carry):
        data_copy(near, c, near).wait_recv()
        data_copy(far_outer, c, far_outer).wait_recv()
        hat = transform([recv[near, c], recv[far_outer, c]])
        hats[5 - own_slot, c] = hat[:, :CHUNK]
        hats[0, c] = hat[:, CHUNK:]
        lag_sums(c, ((1, 2, 3), (2, 0, 2), (3, 0, 3)))
        return carry

    def second_phase(c, carry):
        data_copy(far_inner, c, far_inner).wait_recv()
        hats[1, c] = transform([recv[far_inner, c]])
        lag_sums(c, ((1, 0, 1), (1, 1, 2), (2, 1, 3)))
        return carry

    first_phase(0, 0)

    @pl.when(inner == 0)
    def _():
        settle(0)
        for target, c in order[6:]:
            data_copy(target, c, me).start()

    lax.fori_loop(1, chunks - 1, first_phase, 0)

    @pl.when(inner == 1)
    def _():
        settle(0)
        for target, c in order[6:]:
            data_copy(target, c, me).start()

    first_phase(chunks - 1, 0)
    share((3,))
    lax.fori_loop(0, chunks - 1, second_phase, 0)

    def folded(rows):
        return jnp.concatenate([rows[:, :block], rows[:, block:]], axis=0)

    @pl.when(inner == 1)
    def _():
        settle(3)
        second_phase(chunks - 1, 0)
        near_copy(3 - me).wait_recv()
        passed_on = near_in[3 - me]
        total = jnp.zeros((2 * lag_rows, block), jnp.float32)
        result = inverse_transform([acc[me], acc[3 - me]], fine=True)
        for kind in (1, 0):
            for g in range(groups):
                first = kind * LAGS + g * lag_rows
                rows = result[first:first + lag_rows]
                if kind == 1:
                    rows += jnp.where(group == g, passed_on, 0.0)
                else:
                    total += jnp.where(group == g, folded(rows), 0.0)
                tail_out[kind, g] = folded(rows).astype(jnp.bfloat16)
            for step in range(1 - kind, groups):
                tail_copy(kind, group_peer(step), group).start()
        near_copy(me).wait_recv()
        total += folded(near_in[me])
        for kind in (0, 1):
            for step in range(1 - kind, groups):
                tail_copy(kind, group_peer(step), group_peer(step)).wait_recv()
                total += tail_in[kind, group_peer(step)].astype(jnp.float32)
        final = jnp.concatenate([total[:lag_rows], total[lag_rows:]], axis=1)
        out[0] = final * scale
        for kind in (1, 0):
            for step in range(1 - kind, groups):
                tail_copy(kind, group_peer(step), group).wait_send()
        for j in (0, n - 1):
            band_copy(j, me).wait_send()

    @pl.when(inner == 0)
    def _():
        settle(3)
        second_phase(chunks - 1, 0)
        share((1, 2))
        settle(1)
        settle(2)
        final = band_sum[me]
        for source in (near, far_inner):
            band_copy(source, source).wait_recv()
            final += band_in[source]
        out[0] = final * scale
        for j in (1, 2):
            near_copy(j).wait_send()
            for step in range(1, groups):
                part_copy(j, group_peer(step), group).wait_send()
        near_copy(n - 1 - me).wait_send()

    for step in range(1, n):
        for c in range(chunks):
            data_copy(ch_peer(step), c, me).wait_send()
        mask_copy(ch_peer(step), me).wait_send()
    for j in (0, n - 1):
        for step in range(1, groups):
            part_copy(j, group_peer(step), group).wait_send()


def fused_shards(spectra, quality, taper):
    block = spectra.shape[1]
    band = spectra.shape[2]
    padded = 2 * block
    n = lax.axis_size("ch")
    subs = lax.axis_size("sub")
    groups = lax.axis_size("fq") * subs
    chunks = band // (n * CHUNK)
    lag_rows = LAGS // groups
    bf16, f32 = jnp.bfloat16, jnp.float32
    in_hbm = pl.BlockSpec(memory_space=pltpu.HBM)
    operands = (
        spectra, quality.reshape(1, block), taper.reshape(1, band),
        jnp.asarray(channel_constant(block)), jnp.asarray(inverse_constant(block)),
        jnp.asarray(lag_constant(LAGS, FREQS)),
    )
    dma = pltpu.SemaphoreType.DMA
    regular = pltpu.SemaphoreType.REGULAR
    return pl.pallas_call(
        functools.partial(kernel, (n, groups, subs, block, chunks)),
        out_shape=jax.ShapeDtypeStruct((1, lag_rows, padded), f32),
        in_specs=[in_hbm] * 6,
        out_specs=pl.BlockSpec(memory_space=pltpu.VMEM),
        scratch_shapes=[
            pltpu.VMEM((1, band), f32),
            pltpu.VMEM((n * chunks, 2, block, CHUNK), f32),
            pltpu.VMEM((n * chunks, padded, CHUNK), bf16),
            pltpu.VMEM((n, chunks, padded, CHUNK), bf16),
            pltpu.VMEM((2 * padded, padded), bf16),
            pltpu.VMEM((2, 2 * padded, padded), bf16),
            pltpu.VMEM((2, LAGS, band), f32),
            pltpu.VMEM((n, 1, block), jnp.int32),
            pltpu.VMEM((n, chunks, 2 * padded, CHUNK), bf16),
            pltpu.VMEM((n, 2 * LAGS, padded), f32),
            pltpu.VMEM((n, groups, lag_rows, padded), f32),
            pltpu.VMEM((n, groups, lag_rows, padded), f32),
            pltpu.VMEM((n, lag_rows, padded), f32),
            pltpu.VMEM((n, lag_rows, padded), f32),
            pltpu.VMEM((n, lag_rows, padded), f32),
            pltpu.VMEM((2, groups, 2 * lag_rows, block), bf16),
            pltpu.VMEM((2, groups, 2 * lag_rows, block), bf16),
            dma((n * chunks,)), dma((4,)), dma((n, chunks)), dma((n, chunks)),
            dma, dma((n,)), dma((n,)), dma((n, groups)), dma((n, groups)),
            dma((n,)), dma((n,)), dma((n,)), dma((n,)), dma((2, groups)), dma((2, groups)), regular, regular,
        ],
        compiler_params=pltpu.CompilerParams(
            collective_id=0, has_side_effects=True, vmem_limit_bytes=40 << 20
        ),
    )(
        *[pltpu.with_memory_space_constraint(operand, pltpu.HBM) for operand in operands]
    )


def fits(mesh):
    blocks = mesh.shape["ch"]
    groups = mesh.shape["fq"] * mesh.shape["sub"]
    return blocks == 4 and FREQS == 4 * groups * blocks * CHUNK and LAGS % (8 * groups) == 0 and groups > 1


def solution(mesh):
    body = fused_shards if fits(mesh) else shards
    in_specs = (P(None, ("grp", "ch"), ("fq", "sub")), P(("grp", "ch")), P(("fq", "sub")))
    out_specs = P(("grp", "ch"), ("fq", "sub"), None)
    return jax.shard_map(body, mesh=mesh, in_specs=in_specs, out_specs=out_specs, check_vma=False)
```

```python
import functools

import jax
import jax.numpy as jnp
import numpy as np
from jax import lax
from jax.experimental import pallas as pl
from jax.experimental.pallas import tpu as pltpu
from jax.sharding import PartitionSpec as P

FREQS = 8192
LAGS = 32
CHUNK = 128
PIECE = 128


def passed_along(value, axis, steps):
    count = lax.axis_size(axis)
    pairs = [(source, (source + steps) % count) for source in range(count)]
    return lax.ppermute(value, axis, pairs)


def channel_table(block_size):
    padded = 2 * block_size
    row_index = jnp.arange(padded, dtype=jnp.int32)[:, None]
    col_index = jnp.arange(block_size, dtype=jnp.int32)[None, :]
    angle = 2.0 * jnp.pi / padded * (row_index * col_index % padded).astype(jnp.float32)
    cosine = jnp.cos(angle)
    sine = jnp.sin(angle)
    upper = jnp.concatenate([cosine, sine], axis=1)
    lower = jnp.concatenate([-sine, cosine], axis=1)
    return jnp.concatenate([upper, lower], axis=0).astype(jnp.bfloat16)


def inverse_table(block_size):
    padded = 2 * block_size
    row_index = jnp.arange(padded, dtype=jnp.int32)[:, None]
    col_index = jnp.arange(padded, dtype=jnp.int32)[None, :]
    angle = 2.0 * jnp.pi / padded * (row_index * col_index % padded).astype(jnp.float32)
    return jnp.concatenate([jnp.cos(angle), jnp.sin(angle)], axis=0) / padded


def lag_table(taper_band, start, band_size, lag_count, freq_count):
    freq_index = start + jnp.arange(band_size, dtype=jnp.int32)
    lag_index = jnp.arange(lag_count, dtype=jnp.int32) - lag_count // 2
    phase = lag_index[:, None] * freq_index[None, :] % (2 * freq_count)
    angle = jnp.pi / freq_count * phase.astype(jnp.float32)
    cosine = taper_band[None, :] * jnp.cos(angle)
    sine = taper_band[None, :] * jnp.sin(angle)
    upper = jnp.concatenate([cosine, -sine], axis=1)
    lower = jnp.concatenate([sine, cosine], axis=1)
    return jnp.concatenate([upper, lower], axis=0).astype(jnp.bfloat16)


def cross_spectrum(first, second, sign):
    padded = first.shape[0] // 2
    first_real = first[:padded].astype(jnp.float32)
    first_imag = first[padded:].astype(jnp.float32)
    second_real = second[:padded].astype(jnp.float32)
    second_imag = second[padded:].astype(jnp.float32)
    prod_real = first_real * second_real + first_imag * second_imag
    prod_imag = (first_imag * second_real - first_real * second_imag) * sign
    return jnp.concatenate([prod_real, prod_imag], axis=1).astype(jnp.bfloat16)


def pair_counts(lower_mask, upper_mask):
    block_size = lower_mask.shape[0]
    outer = lower_mask[::-1][:, None] * upper_mask[None, :]
    widened = jnp.pad(outer, ((0, 0), (0, block_size)))
    flat = widened.reshape(-1)[: block_size * (2 * block_size - 1)]
    sheared = flat.reshape(block_size, 2 * block_size - 1)
    histogram = jnp.pad(jnp.sum(sheared, axis=0), (0, 1))
    return jnp.roll(histogram, -(block_size - 1))


def channel_transform(table, data):
    block_size = data.shape[1]
    stacked = data.reshape(2 * block_size, data.shape[2])
    return jnp.dot(table, stacked, preferred_element_type=jnp.float32).astype(jnp.bfloat16)


def shards(spectra, quality, taper):
    block_size = spectra.shape[1]
    band_size = spectra.shape[2]
    padded = 2 * block_size
    blocks = lax.axis_size("ch")
    position = lax.axis_index("ch")
    quality_float = quality.astype(jnp.float32)
    masked = (spectra * quality_float[None, :, None]).astype(jnp.bfloat16)
    mask_half = quality_float.astype(jnp.bfloat16)
    table = channel_table(block_size)
    start = lax.axis_index(("fq", "sub")) * band_size
    own_hat = channel_transform(table, masked)
    weights = lag_table(taper, start, band_size, LAGS, FREQS)

    def accumulate(state, partner_hat, partner_mask, round_index):
        totals, tallies = state
        wrapped = position + round_index >= blocks
        sign = jnp.where(wrapped, -1.0, 1.0).astype(jnp.float32)
        product = cross_spectrum(own_hat, partner_hat, sign)
        term = lax.dot_general(
            weights, product, (((1,), (1,)), ((), ())), preferred_element_type=jnp.float32
        )
        term = term.reshape(2, LAGS, padded)
        offset = jnp.where(wrapped, blocks - round_index, round_index).astype(jnp.int32)
        keep = jnp.where(jnp.logical_and(wrapped, 2 * round_index == blocks), 0.0, 1.0).astype(
            jnp.float32
        )
        lower_mask = jnp.where(wrapped, partner_mask, mask_half).astype(jnp.float32)
        upper_mask = jnp.where(wrapped, mask_half, partner_mask).astype(jnp.float32)
        pairs = pair_counts(lower_mask, upper_mask)
        old_row = lax.dynamic_slice_in_dim(totals, offset, 1, 0)
        totals = lax.dynamic_update_slice_in_dim(totals, old_row + keep * term[None], offset, 0)
        old_tally = lax.dynamic_slice_in_dim(tallies, offset, 1, 0)
        tallies = lax.dynamic_update_slice_in_dim(
            tallies, old_tally + keep * pairs[None], offset, 0
        )
        return (totals, tallies)

    state = (
        jnp.zeros((blocks, 2, LAGS, padded), jnp.float32),
        jnp.zeros((blocks, padded), jnp.float32),
    )
    state = accumulate(state, own_hat, mask_half, 0)

    def advance(round_index, carry):
        current, held, held_mask = carry
        held, held_mask = passed_along((held, held_mask), "ch", -1)
        current = accumulate(current, channel_transform(table, held), held_mask, round_index)
        return (current, held, held_mask)

    state, _, _ = lax.fori_loop(1, blocks // 2 + 1, advance, (state, masked, mask_half))
    totals, tallies = state
    totals, tallies = (
        lax.psum_scatter(totals, "ch", scatter_dimension=0, tiled=True),
        lax.psum_scatter(tallies, "ch", scatter_dimension=0, tiled=True),
    )
    totals = lax.psum_scatter(totals, ("fq", "sub"), scatter_dimension=2, tiled=True)
    combined = jnp.concatenate([totals[0, 0], totals[0, 1]], axis=1)
    lagged = jnp.dot(
        combined,
        inverse_table(block_size),
        precision=lax.Precision.HIGHEST,
        preferred_element_type=jnp.float32,
    )
    scale = jnp.sqrt(2.0 * FREQS * jnp.maximum(tallies[0], 1.0))
    return (lagged / scale[None, :])[None]


def halves_first(first, second, block_size):
    return np.concatenate([
        part[start:start + block_size]
        for start in range(0, 2 * block_size, block_size) for part in (first, second)
    ])


def channel_constant(block_size):
    padded = 2 * block_size
    index = np.outer(np.arange(padded), np.arange(block_size)) % padded
    angle = 2.0 * np.pi / padded * index
    cosine, sine = np.cos(angle), np.sin(angle)
    upper = np.concatenate([cosine, sine], axis=1)
    lower = np.concatenate([-sine, cosine], axis=1)
    return halves_first(upper, lower, block_size).astype(jnp.bfloat16)


def inverse_constant(block_size):
    padded = 2 * block_size
    index = np.outer(np.arange(padded), np.arange(padded)) % padded
    angle = 2.0 * np.pi / padded * index
    full = halves_first(np.cos(angle), np.sin(angle), block_size) / padded
    high = full.astype(np.float32).astype(jnp.bfloat16)
    low = (full - high.astype(np.float64)).astype(np.float32).astype(jnp.bfloat16)
    return np.stack([high, low])


def lag_constant(lag_count, freq_count):
    lag_index = np.arange(lag_count) - lag_count // 2
    phase = np.outer(lag_index, np.arange(freq_count)) % (2 * freq_count)
    angle = np.pi / freq_count * phase
    return np.stack([np.cos(angle), np.sin(angle)]).astype(np.float32)


def kernel(
    sizes, spectra, quality_hbm, taper_hbm, table_hbm, flat_hbm, inverse_hbm, lag_hbm, out,
    taper, raw, send, recv, table, inverse, lagtab, masks, hats, acc, part, part_in, band_sum, band_in, near_in,
    tail_out, tail_in, flat_table, flat_send, flat_recv, flat_hats, flat_weights,
    raw_sem, const_sem, send_sem, recv_sem, mask_sem, mask_send, mask_recv,
    part_send, part_recv, band_send, band_recv, near_send, near_recv, tail_send, tail_recv, piece_send, piece_recv, two_away, three_away,
):
    n, groups, subs, block, chunks = sizes
    padded = 2 * block
    lag_rows = LAGS // groups
    me = lax.axis_index("ch")
    group = lax.axis_index("fq") * subs + lax.axis_index("sub")
    upper = me // 2
    inner = (me * (n - 1 - me)) // 2
    near = me + 1 - 2 * lax.rem(me, 2)
    far_outer = 3 * (1 - upper)
    far_inner = 2 - upper
    sign = (2 * upper - 1).astype(jnp.float32)
    own_slot = 3 - inner

    def ch_peer(step):
        return lax.rem(me + step, n)

    def group_peer(step):
        return lax.rem(group + step, groups)

    def place(ch, index):
        return {"ch": ch, "fq": index // subs, "sub": lax.rem(index, subs)}

    def raw_copy(slot):
        start = pl.multiple_of(slot * CHUNK, CHUNK)
        return pltpu.make_async_copy(
            spectra.at[:, :, pl.ds(start, CHUNK)], raw.at[slot], raw_sem.at[slot]
        )

    def data_copy(target, c, source):
        return pltpu.make_async_remote_copy(
            send.at[target * chunks + c], recv.at[source, c],
            send_sem.at[target, c], recv_sem.at[source, c],
            device_id={"ch": target}, device_id_type=pl.DeviceIdType.MESH,
        )

    def piece_copy(piece):
        rows = pl.ds(pl.multiple_of(piece * PIECE, PIECE), PIECE)
        return pltpu.make_async_remote_copy(
            flat_send.at[rows], flat_recv.at[rows], piece_send.at[piece], piece_recv.at[piece],
            device_id={"ch": far_inner}, device_id_type=pl.DeviceIdType.MESH,
        )

    def mask_copy(target, source):
        return pltpu.make_async_remote_copy(
            masks.at[me], masks.at[source], mask_send.at[target], mask_recv.at[source],
            device_id={"ch": target}, device_id_type=pl.DeviceIdType.MESH,
        )

    def part_copy(j, target, source):
        return pltpu.make_async_remote_copy(
            part.at[j, target], part_in.at[j, source],
            part_send.at[j, target], part_recv.at[j, source],
            device_id=place(me, target), device_id_type=pl.DeviceIdType.MESH,
        )

    def band_copy(target, source):
        return pltpu.make_async_remote_copy(
            band_sum.at[target], band_in.at[source], band_send.at[target], band_recv.at[source],
            device_id={"ch": target}, device_id_type=pl.DeviceIdType.MESH,
        )

    def near_copy(j):
        return pltpu.make_async_remote_copy(
            band_sum.at[j], near_in.at[j], near_send.at[j], near_recv.at[j],
            device_id={"ch": near}, device_id_type=pl.DeviceIdType.MESH,
        )

    def tail_copy(kind, target, source):
        return pltpu.make_async_remote_copy(
            tail_out.at[kind, target], tail_in.at[kind, source],
            tail_send.at[kind, target], tail_recv.at[kind, source],
            device_id=place(3 - me if kind else me, target), device_id_type=pl.DeviceIdType.MESH,
        )

    def tell(semaphore, target):
        pl.semaphore_signal(
            semaphore, inc=1, device_id={"ch": target}, device_id_type=pl.DeviceIdType.MESH
        )

    barrier = pltpu.get_barrier_semaphore()

    @pl.when(me > 0)
    def _():
        tell(barrier, me - 1)

    @pl.when(me < n - 1)
    def _():
        tell(barrier, me + 1)

    for step in range(1, groups):
        pl.semaphore_signal(
            barrier, inc=1, device_id=place(me, group_peer(step)),
            device_id_type=pl.DeviceIdType.MESH,
        )

    quality_copy = pltpu.make_async_copy(quality_hbm, masks.at[me], mask_sem)
    quality_copy.start()
    for target in (far_inner, near, far_outer):
        raw_copy(target * chunks).start()
    inner_order = [
        (far_outer, 1), (near, 1), (far_outer, 2), (near, 2), (far_outer, 3), (near, 3),
        (far_inner, 1), (far_inner, 2), (far_inner, 3),
    ]
    outer_order = [
        (far_outer, 1), (far_inner, 1), (near, 1), (far_outer, 2), (far_inner, 2), (near, 2),
        (far_outer, 3), (far_inner, 3), (near, 3),
    ]
    order = [
        (inner * a + (1 - inner) * b, inner * a_chunk + (1 - inner) * b_chunk)
        for (a, a_chunk), (b, b_chunk) in zip(inner_order, outer_order)
    ]
    band = n * chunks * CHUNK
    lag_start = pl.multiple_of(group * band, CHUNK)
    consts = [
        pltpu.make_async_copy(table_hbm, table, const_sem.at[0]),
        pltpu.make_async_copy(lag_hbm.at[:, :, pl.ds(lag_start, band)], lagtab, const_sem.at[1]),
        pltpu.make_async_copy(inverse_hbm, inverse, const_sem.at[2]),
        pltpu.make_async_copy(taper_hbm, taper, const_sem.at[3]),
        pltpu.make_async_copy(flat_hbm, flat_table, const_sem.at[4]),
    ]

    quality_copy.wait()
    quality_row = masks[me].astype(jnp.float32)
    column = jnp.transpose(jnp.broadcast_to(quality_row, (CHUNK, block)))

    def mask_block(slot):
        raw_copy(slot).wait()
        for half in range(2):
            send[slot, half * block:(half + 1) * block, :] = (
                raw[slot, half] * column
            ).astype(jnp.bfloat16)

    def send_block(target, c):
        mask_block(target * chunks + c)
        data_copy(target, c, me).start()

    for target in (far_inner, near, far_outer):
        mask_block(target * chunks)
    pl.semaphore_wait(barrier, groups + inner)

    @pl.when(inner == 1)
    def _():
        tell(two_away, me - 1)
        tell(two_away, me + 1)
        data_copy(far_inner, 0, me).start()

    data_copy(near, 0, me).start()
    for target, c in order:
        raw_copy(target * chunks + c).start()
    for c in range(chunks):
        raw_copy(me * chunks + c).start()

    @pl.when(inner == 1)
    def _():
        pl.semaphore_wait(two_away, 1)
        tell(three_away, (n - 1) * (me - 1))
        data_copy(far_outer, 0, me).start()

    @pl.when(inner == 0)
    def _():
        pl.semaphore_wait(two_away, 1)
        data_copy(far_inner, 0, me).start()
        pl.semaphore_wait(three_away, 1)
        data_copy(far_outer, 0, me).start()

    for step in range(1, n):
        mask_copy(ch_peer(step), me).start()
    for target, c in order[:2]:
        send_block(target, c)
    for copy in consts:
        copy.start()
    for target, c in order[2:6]:
        send_block(target, c)
    for target, c in order[6:]:
        mask_block(target * chunks + c)

    @pl.when(inner == 1)
    def _():
        slot = far_inner * chunks + chunks - 1
        for half in range(2):
            flat_send[:, half * block:(half + 1) * block] = jnp.transpose(
                raw[slot, half] * column
            ).astype(jnp.bfloat16)

    for c in range(chunks):
        mask_block(me * chunks + c)
    acc[...] = jnp.zeros_like(acc)
    for index in (0, 1, 3, 4):
        consts[index].wait()

    def lag_factors(start, width):
        lanes = pl.ds(pl.multiple_of(start, CHUNK), width)
        weight = taper[:, lanes]
        return weight * lagtab[0, :, lanes], weight * lagtab[1, :, lanes]

    def transform(data, half):
        rows = table[half * padded:(half + 1) * padded]
        return jnp.dot(rows, data, preferred_element_type=jnp.float32).astype(jnp.bfloat16)

    def contract(weights, product):
        return lax.dot_general(
            weights, product, (((1,), (1,)), ((), ())), preferred_element_type=jnp.float32
        )

    def own_pair(slot, keep):
        data = jnp.concatenate([send[slot], send[slot + 1]], axis=1)
        wcos, wsin = lag_factors(slot * CHUNK, 2 * CHUNK)
        weights = jnp.concatenate([wcos, wsin], axis=0).astype(jnp.bfloat16)
        for half in range(2):
            hat = transform(data, half)
            keep(half, hat)
            real = hat[:block].astype(jnp.float32)
            imag = hat[block:].astype(jnp.float32)
            power = (real * real + imag * imag).astype(jnp.bfloat16)
            acc[0, :, half * block:(half + 1) * block] += contract(weights, power)

    def keep_at(first, second):
        def keep(half, hat):
            rows = slice(half * padded, (half + 1) * padded)
            hats[(*first, rows)] = hat[:, :CHUNK]
            hats[(*second, rows)] = hat[:, CHUNK:]
        return keep

    def other_step(index, carry):
        step = 1 + index // (chunks // 2)
        half = lax.rem(index, chunks // 2)
        own_pair(ch_peer(step) * chunks + 2 * half, lambda half, hat: None)
        return carry

    def own_step(half, carry):
        keep = keep_at((own_slot, 2 * half), (own_slot, 2 * half + 1))
        own_pair(me * chunks + 2 * half, keep)
        return carry

    lax.fori_loop(0, chunks // 2, own_step, 0)
    lax.fori_loop(0, (n - 1) * (chunks // 2), other_step, 0)

    def lag_weights(c):
        wcos, wsin = lag_factors((me * chunks + c) * CHUNK, CHUNK)
        return jnp.concatenate(
            [
                jnp.concatenate([wcos, -sign * wsin], axis=1),
                jnp.concatenate([wsin, sign * wcos], axis=1),
            ],
            axis=0,
        ).astype(jnp.bfloat16)

    def spectrum(slot, c, half):
        first = half * padded
        return (
            hats[slot, c, first:first + block].astype(jnp.float32),
            hats[slot, c, first + block:first + padded].astype(jnp.float32),
        )

    def lag_sums(weights, half, value, pairs):
        for j in sorted({j for j, _, _ in pairs}):
            products = []
            for index, low, high in pairs:
                if index == j:
                    low_real, low_imag = value[low]
                    high_real, high_imag = value[high]
                    products.append(low_real * high_real + low_imag * high_imag)
                    products.append(low_imag * high_real - low_real * high_imag)
            product = jnp.concatenate([p.astype(jnp.bfloat16) for p in products], axis=1)
            repeated = jnp.concatenate([weights] * (len(products) // 2), axis=1)
            acc[j, :, half * block:(half + 1) * block] += contract(repeated, product)

    def inverse_transform(offsets):
        result = 0.0
        for half in range(2):
            lanes = slice(half * block, (half + 1) * block)
            total = jnp.concatenate(
                [jnp.concatenate([acc[j, :LAGS, lanes], acc[j, LAGS:, lanes]], axis=1) for j in offsets],
                axis=0,
            )
            count = len(offsets) * LAGS
            high = total.astype(jnp.bfloat16)
            low_part = (total - high.astype(jnp.float32)).astype(jnp.bfloat16)
            rows = slice(half * padded, (half + 1) * padded)
            both = jnp.dot(
                jnp.concatenate([high, low_part], axis=0), inverse[0, rows],
                preferred_element_type=jnp.float32,
            )
            result += both[:count] + both[count:] + jnp.dot(
                high, inverse[1, rows], preferred_element_type=jnp.float32
            )
        return result

    def share(offsets):
        result = inverse_transform(offsets)
        for index, j in enumerate(offsets):
            for g in range(groups):
                first = index * LAGS + g * lag_rows
                part[j, g] = result[first:first + lag_rows]
            for step in range(1, groups):
                part_copy(j, group_peer(step), group).start()

    def settle(j):
        total = part[j, group]
        for step in range(1, groups):
            part_copy(j, group_peer(step), group_peer(step)).wait_recv()
            total += part_in[j, group_peer(step)]
        band_sum[j] = total

        @pl.when(jnp.logical_and(inner == 1, far_outer == j))
        def _():
            near_copy(j).wait_recv()
            band_sum[j] += near_in[j]

        @pl.when(inner == 1)
        def _():
            band_copy(j, me).start()

        @pl.when(jnp.logical_and(inner == 0, me != j))
        def _():
            near_copy(j).start()

    consts[2].wait()
    share((0,))

    for step in range(1, n):
        mask_copy(ch_peer(step), ch_peer(step)).wait_recv()
    flip = jnp.where(
        lax.broadcasted_iota(jnp.int32, (block, block), 0)
        + lax.broadcasted_iota(jnp.int32, (block, block), 1) == block - 1, 1.0, 0.0,
    ).astype(jnp.bfloat16)

    def mask_rows(index):
        return jnp.broadcast_to(masks[index].astype(jnp.float32), (8, block))

    first_row = jnp.where(lax.broadcasted_iota(jnp.int32, (8, block), 0) == 0, 1.0, 0.0)
    pairs = jnp.zeros((block, block), jnp.float32)
    for low in range(n):
        valid = jnp.where(low + me < n, 1.0, 0.0)
        upper_mask = (mask_rows(lax.rem(low + me, n)) * (first_row * valid)).astype(jnp.bfloat16)
        lower_mask = jnp.dot(
            mask_rows(low).astype(jnp.bfloat16), flip, preferred_element_type=jnp.float32
        )
        pairs += jnp.dot(
            jnp.transpose(lower_mask).astype(jnp.bfloat16), upper_mask,
            preferred_element_type=jnp.float32,
        )
    widened = jnp.concatenate([pairs, jnp.zeros((block, block), jnp.float32)], axis=1)
    sheared = pltpu.roll(widened, 0, 1, stride=1, stride_axis=0)
    counts = jnp.sum(sheared, axis=0, keepdims=True)
    counts = pltpu.roll(jnp.broadcast_to(counts, (8, padded)), padded - block + 1, 1)
    scale = 1.0 / jnp.sqrt(2.0 * FREQS * jnp.maximum(counts[:1], 1.0))

    def first_phase(c, carry):
        weights = lag_weights(c)
        data_copy(near, c, near).wait_recv()
        data_copy(far_outer, c, far_outer).wait_recv()
        data = jnp.concatenate([recv[near, c], recv[far_outer, c]], axis=1)
        keep = keep_at((5 - own_slot, c), (0, c))
        for half in range(2):
            keep(half, transform(data, half))
            value = {slot: spectrum(slot, c, half) for slot in (0, 2, 3)}
            lag_sums(weights, half, value, ((1, 2, 3), (2, 0, 2), (3, 0, 3)))
        return carry

    def second_phase(c, carry):
        weights = lag_weights(c)
        data_copy(far_inner, c, far_inner).wait_recv()
        for half in range(2):
            hat = transform(recv[far_inner, c], half).astype(jnp.float32)
            value = {slot: spectrum(slot, c, half) for slot in (0, 2, 3)}
            value[1] = hat[:block], hat[block:]
            lag_sums(weights, half, value, ((1, 0, 1), (1, 1, 2), (2, 1, 3)))
        return carry

    first_phase(0, 0)

    @pl.when(inner == 0)
    def _():
        settle(0)
        for target, c in order[6:8] + [(near, chunks - 1)]:
            data_copy(target, c, me).start()

    lax.fori_loop(1, chunks - 1, first_phase, 0)

    @pl.when(inner == 1)
    def _():
        settle(0)
        for target, c in order[6:8]:
            data_copy(target, c, me).start()
        for piece in range(CHUNK // PIECE):
            piece_copy(piece).start()

    first_phase(chunks - 1, 0)
    share((3,))

    @pl.when(inner == 1)
    def _():
        for slot in (0, 2, 3):
            flat_hats[slot] = jnp.transpose(hats[slot, chunks - 1].astype(jnp.float32))
        wcos, wsin = lag_factors((me * chunks + chunks - 1) * CHUNK, CHUNK)
        for piece in range(CHUNK // PIECE):
            cos_part = wcos[:, piece * PIECE:(piece + 1) * PIECE]
            sin_part = wsin[:, piece * PIECE:(piece + 1) * PIECE]
            weights = jnp.concatenate(
                [
                    jnp.concatenate([cos_part, -sign * sin_part], axis=1),
                    jnp.concatenate([sin_part, sign * cos_part], axis=1),
                ],
                axis=0,
            )
            none = jnp.zeros_like(weights)
            flat_weights[piece] = jnp.concatenate(
                [
                    jnp.concatenate([weights, weights, none], axis=1),
                    jnp.concatenate([none, none, weights], axis=1),
                ],
                axis=0,
            ).astype(jnp.bfloat16)

    lax.fori_loop(0, chunks - 1, second_phase, 0)

    def piece_step(piece, carry):
        piece_copy(piece).wait_recv()
        rows = pl.ds(pl.multiple_of(piece * PIECE, PIECE), PIECE)
        hat = jnp.dot(
            flat_recv[rows], flat_table[...], preferred_element_type=jnp.float32
        ).astype(jnp.bfloat16).astype(jnp.float32)
        products = []
        for low, high in ((0, 1), (1, 2), (1, 3)):
            real, imag = [], []
            for half in range(2):
                first = half * padded

                def parts(slot):
                    values = hat if slot == 1 else flat_hats[slot, rows]
                    return values[:, first:first + block], values[:, first + block:first + padded]

                low_real, low_imag = parts(low)
                high_real, high_imag = parts(high)
                real.append(low_real * high_real + low_imag * high_imag)
                imag.append(low_imag * high_real - low_real * high_imag)
            products += [jnp.concatenate(real, axis=1), jnp.concatenate(imag, axis=1)]
        product = jnp.concatenate([p.astype(jnp.bfloat16) for p in products], axis=0)
        sums = jnp.dot(flat_weights[piece], product, preferred_element_type=jnp.float32)
        acc[1] += sums[:2 * LAGS]
        acc[2] += sums[2 * LAGS:]
        return carry

    def wait_sends():
        for step in range(1, n):
            for c in range(chunks - 1):
                data_copy(ch_peer(step), c, me).wait_send()
            mask_copy(ch_peer(step), me).wait_send()
        for target in (near, far_outer):
            data_copy(target, chunks - 1, me).wait_send()
        for j in (0, n - 1):
            for step in range(1, groups):
                part_copy(j, group_peer(step), group).wait_send()

    def folded(rows):
        return jnp.concatenate([rows[:, :block], rows[:, block:]], axis=0)

    @pl.when(inner == 1)
    def _():
        settle(3)
        lax.fori_loop(0, CHUNK // PIECE, piece_step, 0)
        near_copy(3 - me).wait_recv()
        passed_on = near_in[3 - me]
        total = jnp.zeros((2 * lag_rows, block), jnp.float32)
        result = inverse_transform((me, 3 - me))
        for kind in (1, 0):
            for g in range(groups):
                first = kind * LAGS + g * lag_rows
                rows = result[first:first + lag_rows]
                if kind == 1:
                    rows += jnp.where(group == g, passed_on, 0.0)
                else:
                    total += jnp.where(group == g, folded(rows), 0.0)
                tail_out[kind, g] = folded(rows).astype(jnp.bfloat16)
            for step in range(1 - kind, groups):
                tail_copy(kind, group_peer(step), group).start()
        near_copy(me).wait_recv()
        total += folded(near_in[me])
        wait_sends()
        for piece in range(CHUNK // PIECE):
            piece_copy(piece).wait_send()
        for j in (0, n - 1):
            band_copy(j, me).wait_send()
        for kind in (0, 1):
            for step in range(1 - kind, groups):
                tail_copy(kind, group_peer(step), group_peer(step)).wait_recv()
                total += tail_in[kind, group_peer(step)].astype(jnp.float32)
        final = jnp.concatenate([total[:lag_rows], total[lag_rows:]], axis=1)
        out[0] = final * scale
        for kind in (1, 0):
            for step in range(1 - kind, groups):
                tail_copy(kind, group_peer(step), group).wait_send()

    @pl.when(inner == 0)
    def _():
        settle(3)
        second_phase(chunks - 1, 0)
        share((1, 2))
        settle(1)
        settle(2)
        final = band_sum[me]
        for source in (near, far_inner):
            band_copy(source, source).wait_recv()
            final += band_in[source]
        out[0] = final * scale
        for j in (1, 2):
            near_copy(j).wait_send()
            for step in range(1, groups):
                part_copy(j, group_peer(step), group).wait_send()
        near_copy(n - 1 - me).wait_send()
        data_copy(far_inner, chunks - 1, me).wait_send()
        wait_sends()


def fused_shards(spectra, quality, taper):
    block = spectra.shape[1]
    band = spectra.shape[2]
    padded = 2 * block
    n = lax.axis_size("ch")
    subs = lax.axis_size("sub")
    groups = lax.axis_size("fq") * subs
    chunks = band // (n * CHUNK)
    lag_rows = LAGS // groups
    bf16, f32 = jnp.bfloat16, jnp.float32
    in_hbm = pl.BlockSpec(memory_space=pltpu.HBM)
    operands = (
        spectra, quality.reshape(1, block), taper.reshape(1, band),
        jnp.asarray(channel_constant(block)), jnp.asarray(channel_constant(block).T),
        jnp.asarray(inverse_constant(block)),
        jnp.asarray(lag_constant(LAGS, FREQS)),
    )
    dma = pltpu.SemaphoreType.DMA
    regular = pltpu.SemaphoreType.REGULAR
    return pl.pallas_call(
        functools.partial(kernel, (n, groups, subs, block, chunks)),
        out_shape=jax.ShapeDtypeStruct((1, lag_rows, padded), f32),
        in_specs=[in_hbm] * 7,
        out_specs=pl.BlockSpec(memory_space=pltpu.VMEM),
        scratch_shapes=[
            pltpu.VMEM((1, band), f32),
            pltpu.VMEM((n * chunks, 2, block, CHUNK), f32),
            pltpu.VMEM((n * chunks, padded, CHUNK), bf16),
            pltpu.VMEM((n, chunks, padded, CHUNK), bf16),
            pltpu.VMEM((2 * padded, padded), bf16),
            pltpu.VMEM((2, 2 * padded, padded), bf16),
            pltpu.VMEM((2, LAGS, band), f32),
            pltpu.VMEM((n, 1, block), jnp.int32),
            pltpu.VMEM((n, chunks, 2 * padded, CHUNK), bf16),
            pltpu.VMEM((n, 2 * LAGS, padded), f32),
            pltpu.VMEM((n, groups, lag_rows, padded), f32),
            pltpu.VMEM((n, groups, lag_rows, padded), f32),
            pltpu.VMEM((n, lag_rows, padded), f32),
            pltpu.VMEM((n, lag_rows, padded), f32),
            pltpu.VMEM((n, lag_rows, padded), f32),
            pltpu.VMEM((2, groups, 2 * lag_rows, block), bf16),
            pltpu.VMEM((2, groups, 2 * lag_rows, block), bf16),
            pltpu.VMEM((padded, 2 * padded), bf16),
            pltpu.VMEM((CHUNK, padded), bf16),
            pltpu.VMEM((CHUNK, padded), bf16),
            pltpu.VMEM((n, CHUNK, 2 * padded), f32),
            pltpu.VMEM((CHUNK // PIECE, 4 * LAGS, 6 * PIECE), bf16),
            dma((n * chunks,)), dma((5,)), dma((n, chunks)), dma((n, chunks)),
            dma, dma((n,)), dma((n,)), dma((n, groups)), dma((n, groups)),
            dma((n,)), dma((n,)), dma((n,)), dma((n,)), dma((2, groups)), dma((2, groups)),
            dma((CHUNK // PIECE,)), dma((CHUNK // PIECE,)), regular, regular,
        ],
        compiler_params=pltpu.CompilerParams(
            collective_id=0, has_side_effects=True, vmem_limit_bytes=40 << 20
        ),
    )(
        *[pltpu.with_memory_space_constraint(operand, pltpu.HBM) for operand in operands]
    )


def fits(mesh):
    blocks = mesh.shape["ch"]
    groups = mesh.shape["fq"] * mesh.shape["sub"]
    return blocks == 4 and FREQS == 4 * groups * blocks * CHUNK and LAGS % (8 * groups) == 0 and groups > 1


def solution(mesh):
    body = fused_shards if fits(mesh) else shards
    in_specs = (P(None, ("grp", "ch"), ("fq", "sub")), P(("grp", "ch")), P(("fq", "sub")))
    out_specs = P(("grp", "ch"), ("fq", "sub"), None)
    return jax.shard_map(body, mesh=mesh, in_specs=in_specs, out_specs=out_specs, check_vma=False)
```

```python
import functools

import jax
import jax.numpy as jnp
import numpy as np
from jax import lax
from jax.experimental import pallas as pl
from jax.experimental.pallas import tpu as pltpu
from jax.sharding import PartitionSpec as P

FREQS = 8192
LAGS = 32
CHUNK = 128
PIECE = 128


def passed_along(value, axis, steps):
    count = lax.axis_size(axis)
    pairs = [(source, (source + steps) % count) for source in range(count)]
    return lax.ppermute(value, axis, pairs)


def channel_table(block_size):
    padded = 2 * block_size
    row_index = jnp.arange(padded, dtype=jnp.int32)[:, None]
    col_index = jnp.arange(block_size, dtype=jnp.int32)[None, :]
    angle = 2.0 * jnp.pi / padded * (row_index * col_index % padded).astype(jnp.float32)
    cosine = jnp.cos(angle)
    sine = jnp.sin(angle)
    upper = jnp.concatenate([cosine, sine], axis=1)
    lower = jnp.concatenate([-sine, cosine], axis=1)
    return jnp.concatenate([upper, lower], axis=0).astype(jnp.bfloat16)


def inverse_table(block_size):
    padded = 2 * block_size
    row_index = jnp.arange(padded, dtype=jnp.int32)[:, None]
    col_index = jnp.arange(padded, dtype=jnp.int32)[None, :]
    angle = 2.0 * jnp.pi / padded * (row_index * col_index % padded).astype(jnp.float32)
    return jnp.concatenate([jnp.cos(angle), jnp.sin(angle)], axis=0) / padded


def lag_table(taper_band, start, band_size, lag_count, freq_count):
    freq_index = start + jnp.arange(band_size, dtype=jnp.int32)
    lag_index = jnp.arange(lag_count, dtype=jnp.int32) - lag_count // 2
    phase = lag_index[:, None] * freq_index[None, :] % (2 * freq_count)
    angle = jnp.pi / freq_count * phase.astype(jnp.float32)
    cosine = taper_band[None, :] * jnp.cos(angle)
    sine = taper_band[None, :] * jnp.sin(angle)
    upper = jnp.concatenate([cosine, -sine], axis=1)
    lower = jnp.concatenate([sine, cosine], axis=1)
    return jnp.concatenate([upper, lower], axis=0).astype(jnp.bfloat16)


def cross_spectrum(first, second, sign):
    padded = first.shape[0] // 2
    first_real = first[:padded].astype(jnp.float32)
    first_imag = first[padded:].astype(jnp.float32)
    second_real = second[:padded].astype(jnp.float32)
    second_imag = second[padded:].astype(jnp.float32)
    prod_real = first_real * second_real + first_imag * second_imag
    prod_imag = (first_imag * second_real - first_real * second_imag) * sign
    return jnp.concatenate([prod_real, prod_imag], axis=1).astype(jnp.bfloat16)


def pair_counts(lower_mask, upper_mask):
    block_size = lower_mask.shape[0]
    outer = lower_mask[::-1][:, None] * upper_mask[None, :]
    widened = jnp.pad(outer, ((0, 0), (0, block_size)))
    flat = widened.reshape(-1)[: block_size * (2 * block_size - 1)]
    sheared = flat.reshape(block_size, 2 * block_size - 1)
    histogram = jnp.pad(jnp.sum(sheared, axis=0), (0, 1))
    return jnp.roll(histogram, -(block_size - 1))


def channel_transform(table, data):
    block_size = data.shape[1]
    stacked = data.reshape(2 * block_size, data.shape[2])
    return jnp.dot(table, stacked, preferred_element_type=jnp.float32).astype(jnp.bfloat16)


def shards(spectra, quality, taper):
    block_size = spectra.shape[1]
    band_size = spectra.shape[2]
    padded = 2 * block_size
    blocks = lax.axis_size("ch")
    position = lax.axis_index("ch")
    quality_float = quality.astype(jnp.float32)
    masked = (spectra * quality_float[None, :, None]).astype(jnp.bfloat16)
    mask_half = quality_float.astype(jnp.bfloat16)
    table = channel_table(block_size)
    start = lax.axis_index(("fq", "sub")) * band_size
    own_hat = channel_transform(table, masked)
    weights = lag_table(taper, start, band_size, LAGS, FREQS)

    def accumulate(state, partner_hat, partner_mask, round_index):
        totals, tallies = state
        wrapped = position + round_index >= blocks
        sign = jnp.where(wrapped, -1.0, 1.0).astype(jnp.float32)
        product = cross_spectrum(own_hat, partner_hat, sign)
        term = lax.dot_general(
            weights, product, (((1,), (1,)), ((), ())), preferred_element_type=jnp.float32
        )
        term = term.reshape(2, LAGS, padded)
        offset = jnp.where(wrapped, blocks - round_index, round_index).astype(jnp.int32)
        keep = jnp.where(jnp.logical_and(wrapped, 2 * round_index == blocks), 0.0, 1.0).astype(
            jnp.float32
        )
        lower_mask = jnp.where(wrapped, partner_mask, mask_half).astype(jnp.float32)
        upper_mask = jnp.where(wrapped, mask_half, partner_mask).astype(jnp.float32)
        pairs = pair_counts(lower_mask, upper_mask)
        old_row = lax.dynamic_slice_in_dim(totals, offset, 1, 0)
        totals = lax.dynamic_update_slice_in_dim(totals, old_row + keep * term[None], offset, 0)
        old_tally = lax.dynamic_slice_in_dim(tallies, offset, 1, 0)
        tallies = lax.dynamic_update_slice_in_dim(
            tallies, old_tally + keep * pairs[None], offset, 0
        )
        return (totals, tallies)

    state = (
        jnp.zeros((blocks, 2, LAGS, padded), jnp.float32),
        jnp.zeros((blocks, padded), jnp.float32),
    )
    state = accumulate(state, own_hat, mask_half, 0)

    def advance(round_index, carry):
        current, held, held_mask = carry
        held, held_mask = passed_along((held, held_mask), "ch", -1)
        current = accumulate(current, channel_transform(table, held), held_mask, round_index)
        return (current, held, held_mask)

    state, _, _ = lax.fori_loop(1, blocks // 2 + 1, advance, (state, masked, mask_half))
    totals, tallies = state
    totals, tallies = (
        lax.psum_scatter(totals, "ch", scatter_dimension=0, tiled=True),
        lax.psum_scatter(tallies, "ch", scatter_dimension=0, tiled=True),
    )
    totals = lax.psum_scatter(totals, ("fq", "sub"), scatter_dimension=2, tiled=True)
    combined = jnp.concatenate([totals[0, 0], totals[0, 1]], axis=1)
    lagged = jnp.dot(
        combined,
        inverse_table(block_size),
        precision=lax.Precision.HIGHEST,
        preferred_element_type=jnp.float32,
    )
    scale = jnp.sqrt(2.0 * FREQS * jnp.maximum(tallies[0], 1.0))
    return (lagged / scale[None, :])[None]


def halves_first(first, second, block_size):
    return np.concatenate([
        part[start:start + block_size]
        for start in range(0, 2 * block_size, block_size) for part in (first, second)
    ])


def channel_constant(block_size):
    padded = 2 * block_size
    index = np.outer(np.arange(padded), np.arange(block_size)) % padded
    angle = 2.0 * np.pi / padded * index
    cosine, sine = np.cos(angle), np.sin(angle)
    upper = np.concatenate([cosine, sine], axis=1)
    lower = np.concatenate([-sine, cosine], axis=1)
    return halves_first(upper, lower, block_size).astype(jnp.bfloat16)


def inverse_constant(block_size):
    padded = 2 * block_size
    index = np.outer(np.arange(padded), np.arange(padded)) % padded
    angle = 2.0 * np.pi / padded * index
    full = halves_first(np.cos(angle), np.sin(angle), block_size) / padded
    high = full.astype(np.float32).astype(jnp.bfloat16)
    low = (full - high.astype(np.float64)).astype(np.float32).astype(jnp.bfloat16)
    return np.stack([high, low])


def lag_constant(lag_count, freq_count):
    lag_index = np.arange(lag_count) - lag_count // 2
    phase = np.outer(lag_index, np.arange(freq_count)) % (2 * freq_count)
    angle = np.pi / freq_count * phase
    return np.stack([np.cos(angle), np.sin(angle)]).astype(np.float32)


def kernel(
    sizes, spectra, quality_hbm, taper_hbm, table_hbm, flat_hbm, inverse_hbm, lag_hbm, out,
    taper, raw, send, recv, table, inverse, lagtab, masks, hats, acc, part, part_in, band_sum, band_in, near_in,
    tail_out, tail_in, flat_table, flat_send, flat_recv, flat_hats, flat_weights,
    raw_sem, const_sem, send_sem, recv_sem, mask_sem, mask_send, mask_recv,
    part_send, part_recv, band_send, band_recv, near_send, near_recv, tail_send, tail_recv, piece_send, piece_recv, two_away, three_away,
):
    n, groups, subs, block, chunks = sizes
    padded = 2 * block
    lag_rows = LAGS // groups
    me = lax.axis_index("ch")
    group = lax.axis_index("fq") * subs + lax.axis_index("sub")
    upper = me // 2
    inner = (me * (n - 1 - me)) // 2
    near = me + 1 - 2 * lax.rem(me, 2)
    far_outer = 3 * (1 - upper)
    far_inner = 2 - upper
    sign = (2 * upper - 1).astype(jnp.float32)
    own_slot = 3 - inner

    def ch_peer(step):
        return lax.rem(me + step, n)

    def group_peer(step):
        return lax.rem(group + step, groups)

    def place(ch, index):
        return {"ch": ch, "fq": index // subs, "sub": lax.rem(index, subs)}

    def raw_copy(slot):
        start = pl.multiple_of(slot * CHUNK, CHUNK)
        return pltpu.make_async_copy(
            spectra.at[:, :, pl.ds(start, CHUNK)], raw.at[slot], raw_sem.at[slot]
        )

    def data_copy(target, c, source):
        return pltpu.make_async_remote_copy(
            send.at[target * chunks + c], recv.at[source, c],
            send_sem, recv_sem.at[source, c],
            device_id={"ch": target}, device_id_type=pl.DeviceIdType.MESH,
        )

    def piece_copy(piece):
        rows = pl.ds(pl.multiple_of(piece * PIECE, PIECE), PIECE)
        return pltpu.make_async_remote_copy(
            flat_send.at[rows], flat_recv.at[rows], piece_send.at[piece], piece_recv.at[piece],
            device_id={"ch": far_inner}, device_id_type=pl.DeviceIdType.MESH,
        )

    def mask_copy(target, source):
        return pltpu.make_async_remote_copy(
            masks.at[me], masks.at[source], mask_send, mask_recv,
            device_id={"ch": target}, device_id_type=pl.DeviceIdType.MESH,
        )

    def part_copy(j, target, source):
        return pltpu.make_async_remote_copy(
            part.at[j, target], part_in.at[j, source],
            part_send, part_recv.at[j],
            device_id=place(me, target), device_id_type=pl.DeviceIdType.MESH,
        )

    def band_copy(target, source):
        return pltpu.make_async_remote_copy(
            band_sum.at[target], band_in.at[source], band_send, band_recv,
            device_id={"ch": target}, device_id_type=pl.DeviceIdType.MESH,
        )

    def near_copy(j):
        return pltpu.make_async_remote_copy(
            band_sum.at[j], near_in.at[j], near_send, near_recv.at[j],
            device_id={"ch": near}, device_id_type=pl.DeviceIdType.MESH,
        )

    def tail_copy(kind, target, source):
        return pltpu.make_async_remote_copy(
            tail_out.at[kind, target], tail_in.at[kind, source],
            tail_send.at[kind], tail_recv.at[kind],
            device_id=place(3 - me if kind else me, target), device_id_type=pl.DeviceIdType.MESH,
        )

    def drain(semaphore, ref):
        pltpu.make_async_copy(ref, ref, semaphore).wait()

    def tell(semaphore, target):
        pl.semaphore_signal(
            semaphore, inc=1, device_id={"ch": target}, device_id_type=pl.DeviceIdType.MESH
        )

    barrier = pltpu.get_barrier_semaphore()

    @pl.when(me > 0)
    def _():
        tell(barrier, me - 1)

    @pl.when(me < n - 1)
    def _():
        tell(barrier, me + 1)

    for step in range(1, groups):
        pl.semaphore_signal(
            barrier, inc=1, device_id=place(me, group_peer(step)),
            device_id_type=pl.DeviceIdType.MESH,
        )

    quality_copy = pltpu.make_async_copy(quality_hbm, masks.at[me], mask_sem)
    quality_copy.start()
    for target in (far_inner, near, far_outer):
        raw_copy(target * chunks).start()
    inner_order = [
        (far_outer, 1), (near, 1), (far_outer, 2), (near, 2), (far_outer, 3), (near, 3),
        (far_inner, 1), (far_inner, 2), (far_inner, 3),
    ]
    outer_order = [
        (far_outer, 1), (far_inner, 1), (near, 1), (far_outer, 2), (far_inner, 2), (near, 2),
        (far_outer, 3), (far_inner, 3), (near, 3),
    ]
    order = [
        (inner * a + (1 - inner) * b, inner * a_chunk + (1 - inner) * b_chunk)
        for (a, a_chunk), (b, b_chunk) in zip(inner_order, outer_order)
    ]
    band = n * chunks * CHUNK
    lag_start = pl.multiple_of(group * band, CHUNK)
    consts = [
        pltpu.make_async_copy(table_hbm, table, const_sem.at[0]),
        pltpu.make_async_copy(lag_hbm.at[:, :, pl.ds(lag_start, band)], lagtab, const_sem.at[1]),
        pltpu.make_async_copy(inverse_hbm, inverse, const_sem.at[2]),
        pltpu.make_async_copy(taper_hbm, taper, const_sem.at[3]),
        pltpu.make_async_copy(flat_hbm, flat_table, const_sem.at[4]),
    ]

    quality_copy.wait()
    quality_row = masks[me].astype(jnp.float32)
    column = jnp.transpose(jnp.broadcast_to(quality_row, (CHUNK, block)))

    def mask_block(slot):
        raw_copy(slot).wait()
        for half in range(2):
            send[slot, half * block:(half + 1) * block, :] = (
                raw[slot, half] * column
            ).astype(jnp.bfloat16)

    def send_block(target, c):
        mask_block(target * chunks + c)
        data_copy(target, c, me).start()

    for target in (far_inner, near, far_outer):
        mask_block(target * chunks)
    pl.semaphore_wait(barrier, groups + inner)

    @pl.when(inner == 1)
    def _():
        tell(two_away, me - 1)
        tell(two_away, me + 1)
        data_copy(far_inner, 0, me).start()

    data_copy(near, 0, me).start()
    for target, c in order:
        raw_copy(target * chunks + c).start()
    for c in range(chunks):
        raw_copy(me * chunks + c).start()

    @pl.when(inner == 1)
    def _():
        pl.semaphore_wait(two_away, 1)
        tell(three_away, (n - 1) * (me - 1))
        data_copy(far_outer, 0, me).start()

    @pl.when(inner == 0)
    def _():
        pl.semaphore_wait(two_away, 1)
        data_copy(far_inner, 0, me).start()
        pl.semaphore_wait(three_away, 1)
        data_copy(far_outer, 0, me).start()

    for step in range(1, n):
        mask_copy(ch_peer(step), me).start()
    for target, c in order[:2]:
        send_block(target, c)
    for copy in consts:
        copy.start()
    for target, c in order[2:6]:
        send_block(target, c)
    for target, c in order[6:]:
        mask_block(target * chunks + c)

    @pl.when(inner == 1)
    def _():
        slot = far_inner * chunks + chunks - 1
        for half in range(2):
            flat_send[:, half * block:(half + 1) * block] = jnp.transpose(
                raw[slot, half] * column
            ).astype(jnp.bfloat16)

    for c in range(chunks):
        mask_block(me * chunks + c)
    acc[...] = jnp.zeros_like(acc)
    for index in (0, 1, 3, 4):
        consts[index].wait()

    def lag_factors(start, width):
        lanes = pl.ds(pl.multiple_of(start, CHUNK), width)
        weight = taper[:, lanes]
        return weight * lagtab[0, :, lanes], weight * lagtab[1, :, lanes]

    def transform(data, half):
        rows = table[half * padded:(half + 1) * padded]
        return jnp.dot(rows, data, preferred_element_type=jnp.float32).astype(jnp.bfloat16)

    def contract(weights, product):
        return lax.dot_general(
            weights, product, (((1,), (1,)), ((), ())), preferred_element_type=jnp.float32
        )

    def own_pair(slot, keep):
        data = jnp.concatenate([send[slot], send[slot + 1]], axis=1)
        wcos, wsin = lag_factors(slot * CHUNK, 2 * CHUNK)
        weights = jnp.concatenate([wcos, wsin], axis=0).astype(jnp.bfloat16)
        for half in range(2):
            hat = transform(data, half)
            keep(half, hat)
            real = hat[:block].astype(jnp.float32)
            imag = hat[block:].astype(jnp.float32)
            power = (real * real + imag * imag).astype(jnp.bfloat16)
            acc[0, :, half * block:(half + 1) * block] += contract(weights, power)

    def keep_at(first, second):
        def keep(half, hat):
            rows = slice(half * padded, (half + 1) * padded)
            hats[(*first, rows)] = hat[:, :CHUNK]
            hats[(*second, rows)] = hat[:, CHUNK:]
        return keep

    def other_step(index, carry):
        step = 1 + index // (chunks // 2)
        half = lax.rem(index, chunks // 2)
        own_pair(ch_peer(step) * chunks + 2 * half, lambda half, hat: None)
        return carry

    def own_step(half, carry):
        keep = keep_at((own_slot, 2 * half), (own_slot, 2 * half + 1))
        own_pair(me * chunks + 2 * half, keep)
        return carry

    lax.fori_loop(0, chunks // 2, own_step, 0)
    lax.fori_loop(0, (n - 1) * (chunks // 2), other_step, 0)

    def lag_weights(c):
        wcos, wsin = lag_factors((me * chunks + c) * CHUNK, CHUNK)
        return jnp.concatenate(
            [
                jnp.concatenate([wcos, -sign * wsin], axis=1),
                jnp.concatenate([wsin, sign * wcos], axis=1),
            ],
            axis=0,
        ).astype(jnp.bfloat16)

    def spectrum(slot, c, half):
        first = half * padded
        return (
            hats[slot, c, first:first + block].astype(jnp.float32),
            hats[slot, c, first + block:first + padded].astype(jnp.float32),
        )

    def lag_sums(weights, half, value, pairs):
        for j in sorted({j for j, _, _ in pairs}):
            products = []
            for index, low, high in pairs:
                if index == j:
                    low_real, low_imag = value[low]
                    high_real, high_imag = value[high]
                    products.append(low_real * high_real + low_imag * high_imag)
                    products.append(low_imag * high_real - low_real * high_imag)
            product = jnp.concatenate([p.astype(jnp.bfloat16) for p in products], axis=1)
            repeated = jnp.concatenate([weights] * (len(products) // 2), axis=1)
            acc[j, :, half * block:(half + 1) * block] += contract(repeated, product)

    def inverse_transform(offsets):
        result = 0.0
        for half in range(2):
            lanes = slice(half * block, (half + 1) * block)
            total = jnp.concatenate(
                [jnp.concatenate([acc[j, :LAGS, lanes], acc[j, LAGS:, lanes]], axis=1) for j in offsets],
                axis=0,
            )
            count = len(offsets) * LAGS
            high = total.astype(jnp.bfloat16)
            low_part = (total - high.astype(jnp.float32)).astype(jnp.bfloat16)
            rows = slice(half * padded, (half + 1) * padded)
            both = jnp.dot(
                jnp.concatenate([high, low_part], axis=0), inverse[0, rows],
                preferred_element_type=jnp.float32,
            )
            result += both[:count] + both[count:] + jnp.dot(
                high, inverse[1, rows], preferred_element_type=jnp.float32
            )
        return result

    def share(offsets):
        result = inverse_transform(offsets)
        for index, j in enumerate(offsets):
            for g in range(groups):
                first = index * LAGS + g * lag_rows
                part[j, g] = result[first:first + lag_rows]
            for step in range(1, groups):
                part_copy(j, group_peer(step), group).start()

    def settle(j):
        total = part[j, group]
        drain(part_recv.at[j], part_in.at[j, pl.ds(0, groups - 1)])
        for step in range(1, groups):
            total += part_in[j, group_peer(step)]
        band_sum[j] = total

        @pl.when(jnp.logical_and(inner == 1, far_outer == j))
        def _():
            near_copy(j).wait_recv()
            band_sum[j] += near_in[j]

        @pl.when(inner == 1)
        def _():
            band_copy(j, me).start()

        @pl.when(jnp.logical_and(inner == 0, me != j))
        def _():
            near_copy(j).start()

    consts[2].wait()
    share((0,))

    drain(mask_recv, masks.at[pl.ds(0, n - 1)])
    flip = jnp.where(
        lax.broadcasted_iota(jnp.int32, (block, block), 0)
        + lax.broadcasted_iota(jnp.int32, (block, block), 1) == block - 1, 1.0, 0.0,
    ).astype(jnp.bfloat16)

    def mask_rows(index):
        return jnp.broadcast_to(masks[index].astype(jnp.float32), (8, block))

    first_row = jnp.where(lax.broadcasted_iota(jnp.int32, (8, block), 0) == 0, 1.0, 0.0)
    pairs = jnp.zeros((block, block), jnp.float32)
    for low in range(n):
        valid = jnp.where(low + me < n, 1.0, 0.0)
        upper_mask = (mask_rows(lax.rem(low + me, n)) * (first_row * valid)).astype(jnp.bfloat16)
        lower_mask = jnp.dot(
            mask_rows(low).astype(jnp.bfloat16), flip, preferred_element_type=jnp.float32
        )
        pairs += jnp.dot(
            jnp.transpose(lower_mask).astype(jnp.bfloat16), upper_mask,
            preferred_element_type=jnp.float32,
        )
    widened = jnp.concatenate([pairs, jnp.zeros((block, block), jnp.float32)], axis=1)
    sheared = pltpu.roll(widened, 0, 1, stride=1, stride_axis=0)
    counts = jnp.sum(sheared, axis=0, keepdims=True)
    counts = pltpu.roll(jnp.broadcast_to(counts, (8, padded)), padded - block + 1, 1)
    scale = 1.0 / jnp.sqrt(2.0 * FREQS * jnp.maximum(counts[:1], 1.0))

    def first_phase(c, carry):
        weights = lag_weights(c)
        data_copy(near, c, near).wait_recv()
        data_copy(far_outer, c, far_outer).wait_recv()
        data = jnp.concatenate([recv[near, c], recv[far_outer, c]], axis=1)
        keep = keep_at((5 - own_slot, c), (0, c))
        for half in range(2):
            keep(half, transform(data, half))
            value = {slot: spectrum(slot, c, half) for slot in (0, 2, 3)}
            lag_sums(weights, half, value, ((1, 2, 3), (2, 0, 2), (3, 0, 3)))
        return carry

    def second_phase(c, carry):
        weights = lag_weights(c)
        data_copy(far_inner, c, far_inner).wait_recv()
        for half in range(2):
            hat = transform(recv[far_inner, c], half).astype(jnp.float32)
            value = {slot: spectrum(slot, c, half) for slot in (0, 2, 3)}
            value[1] = hat[:block], hat[block:]
            lag_sums(weights, half, value, ((1, 0, 1), (1, 1, 2), (2, 1, 3)))
        return carry

    first_phase(0, 0)

    @pl.when(inner == 0)
    def _():
        settle(0)
        for target, c in order[6:8] + [(near, chunks - 1)]:
            data_copy(target, c, me).start()

    lax.fori_loop(1, chunks - 1, first_phase, 0)

    @pl.when(inner == 1)
    def _():
        settle(0)
        for target, c in order[6:8]:
            data_copy(target, c, me).start()
        for piece in range(CHUNK // PIECE):
            piece_copy(piece).start()

    first_phase(chunks - 1, 0)
    share((3,))

    @pl.when(inner == 1)
    def _():
        for slot in (0, 2, 3):
            flat_hats[slot] = jnp.transpose(hats[slot, chunks - 1].astype(jnp.float32))
        wcos, wsin = lag_factors((me * chunks + chunks - 1) * CHUNK, CHUNK)
        for piece in range(CHUNK // PIECE):
            cos_part = wcos[:, piece * PIECE:(piece + 1) * PIECE]
            sin_part = wsin[:, piece * PIECE:(piece + 1) * PIECE]
            weights = jnp.concatenate(
                [
                    jnp.concatenate([cos_part, -sign * sin_part], axis=1),
                    jnp.concatenate([sin_part, sign * cos_part], axis=1),
                ],
                axis=0,
            )
            none = jnp.zeros_like(weights)
            flat_weights[piece] = jnp.concatenate(
                [
                    jnp.concatenate([weights, weights, none], axis=1),
                    jnp.concatenate([none, none, weights], axis=1),
                ],
                axis=0,
            ).astype(jnp.bfloat16)

    lax.fori_loop(0, chunks - 1, second_phase, 0)

    def piece_step(piece, carry):
        piece_copy(piece).wait_recv()
        rows = pl.ds(pl.multiple_of(piece * PIECE, PIECE), PIECE)
        hat = jnp.dot(
            flat_recv[rows], flat_table[...], preferred_element_type=jnp.float32
        ).astype(jnp.bfloat16).astype(jnp.float32)
        products = []
        for low, high in ((0, 1), (1, 2), (1, 3)):
            real, imag = [], []
            for half in range(2):
                first = half * padded

                def parts(slot):
                    values = hat if slot == 1 else flat_hats[slot, rows]
                    return values[:, first:first + block], values[:, first + block:first + padded]

                low_real, low_imag = parts(low)
                high_real, high_imag = parts(high)
                real.append(low_real * high_real + low_imag * high_imag)
                imag.append(low_imag * high_real - low_real * high_imag)
            products += [jnp.concatenate(real, axis=1), jnp.concatenate(imag, axis=1)]
        product = jnp.concatenate([p.astype(jnp.bfloat16) for p in products], axis=0)
        sums = jnp.dot(flat_weights[piece], product, preferred_element_type=jnp.float32)
        acc[1] += sums[:2 * LAGS]
        acc[2] += sums[2 * LAGS:]
        return carry

    def wait_sends(blocks, offsets):
        drain(send_sem, send.at[pl.ds(0, blocks)])
        drain(mask_send, masks.at[pl.ds(0, n - 1)])
        drain(part_send, part.at[pl.ds(0, offsets), pl.ds(0, groups - 1)])

    def folded(rows):
        return jnp.concatenate([rows[:, :block], rows[:, block:]], axis=0)

    @pl.when(inner == 1)
    def _():
        settle(3)
        lax.fori_loop(0, CHUNK // PIECE, piece_step, 0)
        near_copy(3 - me).wait_recv()
        passed_on = near_in[3 - me]
        total = jnp.zeros((2 * lag_rows, block), jnp.float32)
        result = inverse_transform((me, 3 - me))
        for kind in (1, 0):
            for g in range(groups):
                first = kind * LAGS + g * lag_rows
                rows = result[first:first + lag_rows]
                if kind == 1:
                    rows += jnp.where(group == g, passed_on, 0.0)
                else:
                    total += jnp.where(group == g, folded(rows), 0.0)
                tail_out[kind, g] = folded(rows).astype(jnp.bfloat16)
            for step in range(1 - kind, groups):
                tail_copy(kind, group_peer(step), group).start()
        near_copy(me).wait_recv()
        total += folded(near_in[me])
        wait_sends((n - 1) * chunks - 1, 2)
        for piece in range(CHUNK // PIECE):
            piece_copy(piece).wait_send()
        drain(band_send, band_sum.at[pl.ds(0, 2)])
        for kind in (0, 1):
            drain(tail_recv.at[kind], tail_in.at[kind, pl.ds(0, groups - 1 + kind)])
            for step in range(1 - kind, groups):
                total += tail_in[kind, group_peer(step)].astype(jnp.float32)
        final = jnp.concatenate([total[:lag_rows], total[lag_rows:]], axis=1)
        out[0] = final * scale
        for kind in (1, 0):
            drain(tail_send.at[kind], tail_out.at[kind, pl.ds(0, groups - 1 + kind)])

    @pl.when(inner == 0)
    def _():
        settle(3)
        second_phase(chunks - 1, 0)
        share((1, 2))
        settle(1)
        settle(2)
        final = band_sum[me]
        drain(band_recv, band_in.at[pl.ds(0, 2)])
        for source in (near, far_inner):
            final += band_in[source]
        out[0] = final * scale
        drain(near_send, band_sum.at[pl.ds(0, n - 1)])
        wait_sends((n - 1) * chunks, n)


def fused_shards(spectra, quality, taper):
    block = spectra.shape[1]
    band = spectra.shape[2]
    padded = 2 * block
    n = lax.axis_size("ch")
    subs = lax.axis_size("sub")
    groups = lax.axis_size("fq") * subs
    chunks = band // (n * CHUNK)
    lag_rows = LAGS // groups
    bf16, f32 = jnp.bfloat16, jnp.float32
    in_hbm = pl.BlockSpec(memory_space=pltpu.HBM)
    operands = (
        spectra, quality.reshape(1, block), taper.reshape(1, band),
        jnp.asarray(channel_constant(block)), jnp.asarray(channel_constant(block).T),
        jnp.asarray(inverse_constant(block)),
        jnp.asarray(lag_constant(LAGS, FREQS)),
    )
    dma = pltpu.SemaphoreType.DMA
    regular = pltpu.SemaphoreType.REGULAR
    return pl.pallas_call(
        functools.partial(kernel, (n, groups, subs, block, chunks)),
        out_shape=jax.ShapeDtypeStruct((1, lag_rows, padded), f32),
        in_specs=[in_hbm] * 7,
        out_specs=pl.BlockSpec(memory_space=pltpu.VMEM),
        scratch_shapes=[
            pltpu.VMEM((1, band), f32),
            pltpu.VMEM((n * chunks, 2, block, CHUNK), f32),
            pltpu.VMEM((n * chunks, padded, CHUNK), bf16),
            pltpu.VMEM((n, chunks, padded, CHUNK), bf16),
            pltpu.VMEM((2 * padded, padded), bf16),
            pltpu.VMEM((2, 2 * padded, padded), bf16),
            pltpu.VMEM((2, LAGS, band), f32),
            pltpu.VMEM((n, 1, block), jnp.int32),
            pltpu.VMEM((n, chunks, 2 * padded, CHUNK), bf16),
            pltpu.VMEM((n, 2 * LAGS, padded), f32),
            pltpu.VMEM((n, groups, lag_rows, padded), f32),
            pltpu.VMEM((n, groups, lag_rows, padded), f32),
            pltpu.VMEM((n, lag_rows, padded), f32),
            pltpu.VMEM((n, lag_rows, padded), f32),
            pltpu.VMEM((n, lag_rows, padded), f32),
            pltpu.VMEM((2, groups, 2 * lag_rows, block), bf16),
            pltpu.VMEM((2, groups, 2 * lag_rows, block), bf16),
            pltpu.VMEM((padded, 2 * padded), bf16),
            pltpu.VMEM((CHUNK, padded), bf16),
            pltpu.VMEM((CHUNK, padded), bf16),
            pltpu.VMEM((n, CHUNK, 2 * padded), f32),
            pltpu.VMEM((CHUNK // PIECE, 4 * LAGS, 6 * PIECE), bf16),
            dma((n * chunks,)), dma((5,)), dma, dma((n, chunks)),
            dma, dma, dma, dma, dma((n,)), dma, dma, dma, dma((n,)), dma((2,)), dma((2,)),
            dma((CHUNK // PIECE,)), dma((CHUNK // PIECE,)), regular, regular,
        ],
        compiler_params=pltpu.CompilerParams(
            collective_id=0, has_side_effects=True, vmem_limit_bytes=40 << 20
        ),
    )(
        *[pltpu.with_memory_space_constraint(operand, pltpu.HBM) for operand in operands]
    )


def fits(mesh):
    blocks = mesh.shape["ch"]
    groups = mesh.shape["fq"] * mesh.shape["sub"]
    return blocks == 4 and FREQS == 4 * groups * blocks * CHUNK and LAGS % (8 * groups) == 0 and groups > 1


def solution(mesh):
    body = fused_shards if fits(mesh) else shards
    in_specs = (P(None, ("grp", "ch"), ("fq", "sub")), P(("grp", "ch")), P(("fq", "sub")))
    out_specs = P(("grp", "ch"), ("fq", "sub"), None)
    return jax.shard_map(body, mesh=mesh, in_specs=in_specs, out_specs=out_specs, check_vma=False)
```

```python
import functools

import jax
import jax.numpy as jnp
import numpy as np
from jax import lax
from jax.experimental import pallas as pl
from jax.experimental.pallas import tpu as pltpu
from jax.sharding import PartitionSpec as P

FREQS = 8192
LAGS = 32
CHUNK = 128
PIECE = 128


def passed_along(value, axis, steps):
    count = lax.axis_size(axis)
    pairs = [(source, (source + steps) % count) for source in range(count)]
    return lax.ppermute(value, axis, pairs)


def channel_table(block_size):
    padded = 2 * block_size
    row_index = jnp.arange(padded, dtype=jnp.int32)[:, None]
    col_index = jnp.arange(block_size, dtype=jnp.int32)[None, :]
    angle = 2.0 * jnp.pi / padded * (row_index * col_index % padded).astype(jnp.float32)
    cosine = jnp.cos(angle)
    sine = jnp.sin(angle)
    upper = jnp.concatenate([cosine, sine], axis=1)
    lower = jnp.concatenate([-sine, cosine], axis=1)
    return jnp.concatenate([upper, lower], axis=0).astype(jnp.bfloat16)


def inverse_table(block_size):
    padded = 2 * block_size
    row_index = jnp.arange(padded, dtype=jnp.int32)[:, None]
    col_index = jnp.arange(padded, dtype=jnp.int32)[None, :]
    angle = 2.0 * jnp.pi / padded * (row_index * col_index % padded).astype(jnp.float32)
    return jnp.concatenate([jnp.cos(angle), jnp.sin(angle)], axis=0) / padded


def lag_table(taper_band, start, band_size, lag_count, freq_count):
    freq_index = start + jnp.arange(band_size, dtype=jnp.int32)
    lag_index = jnp.arange(lag_count, dtype=jnp.int32) - lag_count // 2
    phase = lag_index[:, None] * freq_index[None, :] % (2 * freq_count)
    angle = jnp.pi / freq_count * phase.astype(jnp.float32)
    cosine = taper_band[None, :] * jnp.cos(angle)
    sine = taper_band[None, :] * jnp.sin(angle)
    upper = jnp.concatenate([cosine, -sine], axis=1)
    lower = jnp.concatenate([sine, cosine], axis=1)
    return jnp.concatenate([upper, lower], axis=0).astype(jnp.bfloat16)


def cross_spectrum(first, second, sign):
    padded = first.shape[0] // 2
    first_real = first[:padded].astype(jnp.float32)
    first_imag = first[padded:].astype(jnp.float32)
    second_real = second[:padded].astype(jnp.float32)
    second_imag = second[padded:].astype(jnp.float32)
    prod_real = first_real * second_real + first_imag * second_imag
    prod_imag = (first_imag * second_real - first_real * second_imag) * sign
    return jnp.concatenate([prod_real, prod_imag], axis=1).astype(jnp.bfloat16)


def pair_counts(lower_mask, upper_mask):
    block_size = lower_mask.shape[0]
    outer = lower_mask[::-1][:, None] * upper_mask[None, :]
    widened = jnp.pad(outer, ((0, 0), (0, block_size)))
    flat = widened.reshape(-1)[: block_size * (2 * block_size - 1)]
    sheared = flat.reshape(block_size, 2 * block_size - 1)
    histogram = jnp.pad(jnp.sum(sheared, axis=0), (0, 1))
    return jnp.roll(histogram, -(block_size - 1))


def channel_transform(table, data):
    block_size = data.shape[1]
    stacked = data.reshape(2 * block_size, data.shape[2])
    return jnp.dot(table, stacked, preferred_element_type=jnp.float32).astype(jnp.bfloat16)


def shards(spectra, quality, taper):
    block_size = spectra.shape[1]
    band_size = spectra.shape[2]
    padded = 2 * block_size
    blocks = lax.axis_size("ch")
    position = lax.axis_index("ch")
    quality_float = quality.astype(jnp.float32)
    masked = (spectra * quality_float[None, :, None]).astype(jnp.bfloat16)
    mask_half = quality_float.astype(jnp.bfloat16)
    table = channel_table(block_size)
    start = lax.axis_index(("fq", "sub")) * band_size
    own_hat = channel_transform(table, masked)
    weights = lag_table(taper, start, band_size, LAGS, FREQS)

    def accumulate(state, partner_hat, partner_mask, round_index):
        totals, tallies = state
        wrapped = position + round_index >= blocks
        sign = jnp.where(wrapped, -1.0, 1.0).astype(jnp.float32)
        product = cross_spectrum(own_hat, partner_hat, sign)
        term = lax.dot_general(
            weights, product, (((1,), (1,)), ((), ())), preferred_element_type=jnp.float32
        )
        term = term.reshape(2, LAGS, padded)
        offset = jnp.where(wrapped, blocks - round_index, round_index).astype(jnp.int32)
        keep = jnp.where(jnp.logical_and(wrapped, 2 * round_index == blocks), 0.0, 1.0).astype(
            jnp.float32
        )
        lower_mask = jnp.where(wrapped, partner_mask, mask_half).astype(jnp.float32)
        upper_mask = jnp.where(wrapped, mask_half, partner_mask).astype(jnp.float32)
        pairs = pair_counts(lower_mask, upper_mask)
        old_row = lax.dynamic_slice_in_dim(totals, offset, 1, 0)
        totals = lax.dynamic_update_slice_in_dim(totals, old_row + keep * term[None], offset, 0)
        old_tally = lax.dynamic_slice_in_dim(tallies, offset, 1, 0)
        tallies = lax.dynamic_update_slice_in_dim(
            tallies, old_tally + keep * pairs[None], offset, 0
        )
        return (totals, tallies)

    state = (
        jnp.zeros((blocks, 2, LAGS, padded), jnp.float32),
        jnp.zeros((blocks, padded), jnp.float32),
    )
    state = accumulate(state, own_hat, mask_half, 0)

    def advance(round_index, carry):
        current, held, held_mask = carry
        held, held_mask = passed_along((held, held_mask), "ch", -1)
        current = accumulate(current, channel_transform(table, held), held_mask, round_index)
        return (current, held, held_mask)

    state, _, _ = lax.fori_loop(1, blocks // 2 + 1, advance, (state, masked, mask_half))
    totals, tallies = state
    totals, tallies = (
        lax.psum_scatter(totals, "ch", scatter_dimension=0, tiled=True),
        lax.psum_scatter(tallies, "ch", scatter_dimension=0, tiled=True),
    )
    totals = lax.psum_scatter(totals, ("fq", "sub"), scatter_dimension=2, tiled=True)
    combined = jnp.concatenate([totals[0, 0], totals[0, 1]], axis=1)
    lagged = jnp.dot(
        combined,
        inverse_table(block_size),
        precision=lax.Precision.HIGHEST,
        preferred_element_type=jnp.float32,
    )
    scale = jnp.sqrt(2.0 * FREQS * jnp.maximum(tallies[0], 1.0))
    return (lagged / scale[None, :])[None]


def halves_first(first, second, block_size):
    return np.concatenate([
        part[start:start + block_size]
        for start in range(0, 2 * block_size, block_size) for part in (first, second)
    ])


def channel_constant(block_size):
    padded = 2 * block_size
    index = np.outer(np.arange(padded), np.arange(block_size)) % padded
    angle = 2.0 * np.pi / padded * index
    cosine, sine = np.cos(angle), np.sin(angle)
    upper = np.concatenate([cosine, sine], axis=1)
    lower = np.concatenate([-sine, cosine], axis=1)
    return halves_first(upper, lower, block_size).astype(jnp.bfloat16)


def inverse_constant(block_size):
    padded = 2 * block_size
    index = np.outer(np.arange(padded), np.arange(padded)) % padded
    angle = 2.0 * np.pi / padded * index
    full = halves_first(np.cos(angle), np.sin(angle), block_size) / padded
    high = full.astype(np.float32).astype(jnp.bfloat16)
    low = (full - high.astype(np.float64)).astype(np.float32).astype(jnp.bfloat16)
    return np.stack([high, low])


def lag_constant(lag_count, freq_count):
    lag_index = np.arange(lag_count) - lag_count // 2
    phase = np.outer(lag_index, np.arange(freq_count)) % (2 * freq_count)
    angle = np.pi / freq_count * phase
    return np.stack([np.cos(angle), np.sin(angle)]).astype(np.float32)


def kernel(
    sizes, spectra, quality_hbm, taper_hbm, table_hbm, flat_hbm, inverse_hbm, lag_hbm, out,
    taper, raw, send, recv, table, inverse, lagtab, masks, hats, acc, part, part_in, band_sum, band_in, near_in,
    tail_out, tail_in, flat_table, flat_send, flat_recv, flat_hats, flat_weights,
    raw_sem, const_sem, send_sem, recv_sem, mask_sem, mask_send, mask_recv,
    part_send, part_recv, band_send, band_recv, near_send, near_recv, tail_send, tail_recv, piece_send, piece_recv, two_away, three_away,
):
    n, groups, subs, block, chunks = sizes
    padded = 2 * block
    lag_rows = LAGS // groups
    me = lax.axis_index("ch")
    group = lax.axis_index("fq") * subs + lax.axis_index("sub")
    upper = me // 2
    inner = (me * (n - 1 - me)) // 2
    near = me + 1 - 2 * lax.rem(me, 2)
    far_outer = 3 * (1 - upper)
    far_inner = 2 - upper
    sign = (2 * upper - 1).astype(jnp.float32)
    own_slot = 3 - inner

    def ch_peer(step):
        return lax.rem(me + step, n)

    def group_peer(step):
        return lax.rem(group + step, groups)

    def place(ch, index):
        return {"ch": ch, "fq": index // subs, "sub": lax.rem(index, subs)}

    def raw_copy(slot, turn):
        start = pl.multiple_of(slot * CHUNK, CHUNK)
        return pltpu.make_async_copy(
            spectra.at[:, :, pl.ds(start, CHUNK)], raw.at[slot], raw_sem.at[turn]
        )

    def data_copy(target, c):
        late = jnp.where(target == near, 0, inner)
        return pltpu.make_async_remote_copy(
            send.at[target * chunks + c], recv.at[me, c],
            send_sem, recv_sem.at[late, c],
            device_id={"ch": target}, device_id_type=pl.DeviceIdType.MESH,
        )

    def piece_copy(piece):
        rows = pl.ds(pl.multiple_of(piece * PIECE, PIECE), PIECE)
        return pltpu.make_async_remote_copy(
            flat_send.at[rows], flat_recv.at[rows], piece_send.at[piece], piece_recv.at[piece],
            device_id={"ch": far_inner}, device_id_type=pl.DeviceIdType.MESH,
        )

    def mask_copy(target, source):
        return pltpu.make_async_remote_copy(
            masks.at[me], masks.at[source], mask_send, mask_recv,
            device_id={"ch": target}, device_id_type=pl.DeviceIdType.MESH,
        )

    def part_copy(j, target, source):
        return pltpu.make_async_remote_copy(
            part.at[j, target], part_in.at[j, source],
            part_send, part_recv.at[j],
            device_id=place(me, target), device_id_type=pl.DeviceIdType.MESH,
        )

    def band_copy(target, source):
        return pltpu.make_async_remote_copy(
            band_sum.at[target], band_in.at[source], band_send, band_recv,
            device_id={"ch": target}, device_id_type=pl.DeviceIdType.MESH,
        )

    def near_copy(j):
        return pltpu.make_async_remote_copy(
            band_sum.at[j], near_in.at[j], near_send, near_recv.at[j],
            device_id={"ch": near}, device_id_type=pl.DeviceIdType.MESH,
        )

    def tail_copy(kind, target, source):
        return pltpu.make_async_remote_copy(
            tail_out.at[kind, target], tail_in.at[kind, source],
            tail_send.at[kind], tail_recv.at[kind],
            device_id=place(3 - me if kind else me, target), device_id_type=pl.DeviceIdType.MESH,
        )

    def drain(semaphore, ref):
        pltpu.make_async_copy(ref, ref, semaphore).wait()

    def tell(semaphore, target):
        pl.semaphore_signal(
            semaphore, inc=1, device_id={"ch": target}, device_id_type=pl.DeviceIdType.MESH
        )

    barrier = pltpu.get_barrier_semaphore()

    @pl.when(me > 0)
    def _():
        tell(barrier, me - 1)

    @pl.when(me < n - 1)
    def _():
        tell(barrier, me + 1)

    for step in range(1, groups):
        pl.semaphore_signal(
            barrier, inc=1, device_id=place(me, group_peer(step)),
            device_id_type=pl.DeviceIdType.MESH,
        )

    quality_copy = pltpu.make_async_copy(quality_hbm, masks.at[me], mask_sem)
    quality_copy.start()
    for target in (far_inner, near, far_outer):
        raw_copy(target * chunks, 0).start()
    inner_order = [
        (far_outer, 1), (near, 1), (far_outer, 2), (near, 2), (far_outer, 3), (near, 3),
        (far_inner, 1), (far_inner, 2), (far_inner, 3),
    ]
    outer_order = [
        (far_outer, 1), (far_inner, 1), (near, 1), (far_outer, 2), (far_inner, 2), (near, 2),
        (far_outer, 3), (far_inner, 3), (near, 3),
    ]
    order = [
        (inner * a + (1 - inner) * b, inner * a_chunk + (1 - inner) * b_chunk)
        for (a, a_chunk), (b, b_chunk) in zip(inner_order, outer_order)
    ]
    band = n * chunks * CHUNK
    lag_start = pl.multiple_of(group * band, CHUNK)
    consts = [
        pltpu.make_async_copy(table_hbm, table, const_sem.at[0]),
        pltpu.make_async_copy(lag_hbm.at[:, :, pl.ds(lag_start, band)], lagtab, const_sem.at[1]),
        pltpu.make_async_copy(inverse_hbm, inverse, const_sem.at[2]),
        pltpu.make_async_copy(taper_hbm, taper, const_sem.at[3]),
        pltpu.make_async_copy(flat_hbm, flat_table, const_sem.at[4]),
    ]

    quality_copy.wait()
    quality_row = masks[me].astype(jnp.float32)
    column = jnp.transpose(jnp.broadcast_to(quality_row, (CHUNK, block)))

    def mask_block(slot):
        for half in range(2):
            send[slot, half * block:(half + 1) * block, :] = (
                raw[slot, half] * column
            ).astype(jnp.bfloat16)

    def send_block(index):
        target, c = order[index]
        raw_copy(target * chunks + c, 3 + index).wait()
        mask_block(target * chunks + c)
        data_copy(target, c).start()

    drain(raw_sem.at[0], raw.at[pl.ds(0, n - 1)])

    for target in (far_inner, near, far_outer):
        mask_block(target * chunks)
    pl.semaphore_wait(barrier, groups + inner)

    @pl.when(inner == 1)
    def _():
        tell(two_away, me - 1)
        tell(two_away, me + 1)
        data_copy(far_inner, 0).start()

    data_copy(near, 0).start()
    for index, (target, c) in enumerate(order):
        raw_copy(target * chunks + c, 3 + index if index < 6 else 2).start()
    for c in range(chunks):
        raw_copy(me * chunks + c, 1).start()

    @pl.when(inner == 1)
    def _():
        pl.semaphore_wait(two_away, 1)
        tell(three_away, (n - 1) * (me - 1))
        data_copy(far_outer, 0).start()

    @pl.when(inner == 0)
    def _():
        pl.semaphore_wait(two_away, 1)
        data_copy(far_inner, 0).start()
        pl.semaphore_wait(three_away, 1)
        data_copy(far_outer, 0).start()

    for step in range(1, n):
        mask_copy(ch_peer(step), me).start()
    for index in range(2):
        send_block(index)
    for copy in consts:
        copy.start()
    for index in range(2, 6):
        send_block(index)
    drain(raw_sem.at[2], raw.at[pl.ds(0, 3)])
    for target, c in order[6:]:
        mask_block(target * chunks + c)

    @pl.when(inner == 1)
    def _():
        slot = far_inner * chunks + chunks - 1
        for half in range(2):
            flat_send[:, half * block:(half + 1) * block] = jnp.transpose(
                raw[slot, half] * column
            ).astype(jnp.bfloat16)

    drain(raw_sem.at[1], raw.at[pl.ds(0, chunks)])
    for c in range(chunks):
        mask_block(me * chunks + c)
    acc[...] = jnp.zeros_like(acc)
    for index in (0, 1, 3, 4):
        consts[index].wait()

    def lag_factors(start, width):
        lanes = pl.ds(pl.multiple_of(start, CHUNK), width)
        weight = taper[:, lanes]
        return weight * lagtab[0, :, lanes], weight * lagtab[1, :, lanes]

    def transform(data, half):
        rows = table[half * padded:(half + 1) * padded]
        return jnp.dot(rows, data, preferred_element_type=jnp.float32).astype(jnp.bfloat16)

    def contract(weights, product):
        return lax.dot_general(
            weights, product, (((1,), (1,)), ((), ())), preferred_element_type=jnp.float32
        )

    def own_pair(slot, keep):
        data = jnp.concatenate([send[slot], send[slot + 1]], axis=1)
        wcos, wsin = lag_factors(slot * CHUNK, 2 * CHUNK)
        weights = jnp.concatenate([wcos, wsin], axis=0).astype(jnp.bfloat16)
        for half in range(2):
            hat = transform(data, half)
            keep(half, hat)
            real = hat[:block].astype(jnp.float32)
            imag = hat[block:].astype(jnp.float32)
            power = (real * real + imag * imag).astype(jnp.bfloat16)
            acc[0, :, half * block:(half + 1) * block] += contract(weights, power)

    def keep_at(first, second):
        def keep(half, hat):
            rows = slice(half * padded, (half + 1) * padded)
            hats[(*first, rows)] = hat[:, :CHUNK]
            hats[(*second, rows)] = hat[:, CHUNK:]
        return keep

    def other_step(index, carry):
        step = 1 + index // (chunks // 2)
        half = lax.rem(index, chunks // 2)
        own_pair(ch_peer(step) * chunks + 2 * half, lambda half, hat: None)
        return carry

    def own_step(half, carry):
        keep = keep_at((own_slot, 2 * half), (own_slot, 2 * half + 1))
        own_pair(me * chunks + 2 * half, keep)
        return carry

    lax.fori_loop(0, chunks // 2, own_step, 0)
    lax.fori_loop(0, (n - 1) * (chunks // 2), other_step, 0)

    def lag_weights(c):
        wcos, wsin = lag_factors((me * chunks + c) * CHUNK, CHUNK)
        return jnp.concatenate(
            [
                jnp.concatenate([wcos, -sign * wsin], axis=1),
                jnp.concatenate([wsin, sign * wcos], axis=1),
            ],
            axis=0,
        ).astype(jnp.bfloat16)

    def spectrum(slot, c, half):
        first = half * padded
        return (
            hats[slot, c, first:first + block].astype(jnp.float32),
            hats[slot, c, first + block:first + padded].astype(jnp.float32),
        )

    def lag_sums(weights, half, value, pairs):
        for j in sorted({j for j, _, _ in pairs}):
            products = []
            for index, low, high in pairs:
                if index == j:
                    low_real, low_imag = value[low]
                    high_real, high_imag = value[high]
                    products.append(low_real * high_real + low_imag * high_imag)
                    products.append(low_imag * high_real - low_real * high_imag)
            product = jnp.concatenate([p.astype(jnp.bfloat16) for p in products], axis=1)
            repeated = jnp.concatenate([weights] * (len(products) // 2), axis=1)
            acc[j, :, half * block:(half + 1) * block] += contract(repeated, product)

    def inverse_transform(offsets):
        result = 0.0
        for half in range(2):
            lanes = slice(half * block, (half + 1) * block)
            total = jnp.concatenate(
                [jnp.concatenate([acc[j, :LAGS, lanes], acc[j, LAGS:, lanes]], axis=1) for j in offsets],
                axis=0,
            )
            count = len(offsets) * LAGS
            high = total.astype(jnp.bfloat16)
            low_part = (total - high.astype(jnp.float32)).astype(jnp.bfloat16)
            rows = slice(half * padded, (half + 1) * padded)
            both = jnp.dot(
                jnp.concatenate([high, low_part], axis=0), inverse[0, rows],
                preferred_element_type=jnp.float32,
            )
            result += both[:count] + both[count:] + jnp.dot(
                high, inverse[1, rows], preferred_element_type=jnp.float32
            )
        return result

    def share(offsets):
        result = inverse_transform(offsets)
        for index, j in enumerate(offsets):
            for g in range(groups):
                first = index * LAGS + g * lag_rows
                part[j, g] = result[first:first + lag_rows]
            for step in range(1, groups):
                part_copy(j, group_peer(step), group).start()

    def settle(j):
        total = part[j, group]
        drain(part_recv.at[j], part_in.at[j, pl.ds(0, groups - 1)])
        for step in range(1, groups):
            total += part_in[j, group_peer(step)]
        band_sum[j] = total

        @pl.when(jnp.logical_and(inner == 1, far_outer == j))
        def _():
            near_copy(j).wait_recv()
            band_sum[j] += near_in[j]

        @pl.when(inner == 1)
        def _():
            band_copy(j, me).start()

        @pl.when(jnp.logical_and(inner == 0, me != j))
        def _():
            near_copy(j).start()

    consts[2].wait()
    share((0,))

    drain(mask_recv, masks.at[pl.ds(0, n - 1)])
    flip = jnp.where(
        lax.broadcasted_iota(jnp.int32, (block, block), 0)
        + lax.broadcasted_iota(jnp.int32, (block, block), 1) == block - 1, 1.0, 0.0,
    ).astype(jnp.bfloat16)

    def mask_rows(index):
        return jnp.broadcast_to(masks[index].astype(jnp.float32), (8, block))

    first_row = jnp.where(lax.broadcasted_iota(jnp.int32, (8, block), 0) == 0, 1.0, 0.0)
    pairs = jnp.zeros((block, block), jnp.float32)
    for low in range(n):
        valid = jnp.where(low + me < n, 1.0, 0.0)
        upper_mask = (mask_rows(lax.rem(low + me, n)) * (first_row * valid)).astype(jnp.bfloat16)
        lower_mask = jnp.dot(
            mask_rows(low).astype(jnp.bfloat16), flip, preferred_element_type=jnp.float32
        )
        pairs += jnp.dot(
            jnp.transpose(lower_mask).astype(jnp.bfloat16), upper_mask,
            preferred_element_type=jnp.float32,
        )
    widened = jnp.concatenate([pairs, jnp.zeros((block, block), jnp.float32)], axis=1)
    sheared = pltpu.roll(widened, 0, 1, stride=1, stride_axis=0)
    counts = jnp.sum(sheared, axis=0, keepdims=True)
    counts = pltpu.roll(jnp.broadcast_to(counts, (8, padded)), padded - block + 1, 1)
    scale = 1.0 / jnp.sqrt(2.0 * FREQS * jnp.maximum(counts[:1], 1.0))

    def first_phase(c, carry):
        weights = lag_weights(c)
        drain(recv_sem.at[0, c], recv.at[pl.ds(0, 2), c])
        data = jnp.concatenate([recv[near, c], recv[far_outer, c]], axis=1)
        keep = keep_at((5 - own_slot, c), (0, c))
        for half in range(2):
            keep(half, transform(data, half))
            value = {slot: spectrum(slot, c, half) for slot in (0, 2, 3)}
            lag_sums(weights, half, value, ((1, 2, 3), (2, 0, 2), (3, 0, 3)))
        return carry

    def second_phase(c, carry):
        weights = lag_weights(c)
        drain(recv_sem.at[1, c], recv.at[far_inner, c])
        for half in range(2):
            hat = transform(recv[far_inner, c], half).astype(jnp.float32)
            value = {slot: spectrum(slot, c, half) for slot in (0, 2, 3)}
            value[1] = hat[:block], hat[block:]
            lag_sums(weights, half, value, ((1, 0, 1), (1, 1, 2), (2, 1, 3)))
        return carry

    first_phase(0, 0)

    @pl.when(inner == 0)
    def _():
        settle(0)
        for target, c in order[6:8] + [(near, chunks - 1)]:
            data_copy(target, c).start()

    lax.fori_loop(1, chunks - 1, first_phase, 0)

    @pl.when(inner == 1)
    def _():
        settle(0)
        for target, c in order[6:8]:
            data_copy(target, c).start()
        for piece in range(CHUNK // PIECE):
            piece_copy(piece).start()

    first_phase(chunks - 1, 0)
    share((3,))

    @pl.when(inner == 1)
    def _():
        for slot in (0, 2, 3):
            flat_hats[slot] = jnp.transpose(hats[slot, chunks - 1].astype(jnp.float32))
        wcos, wsin = lag_factors((me * chunks + chunks - 1) * CHUNK, CHUNK)
        for piece in range(CHUNK // PIECE):
            cos_part = wcos[:, piece * PIECE:(piece + 1) * PIECE]
            sin_part = wsin[:, piece * PIECE:(piece + 1) * PIECE]
            weights = jnp.concatenate(
                [
                    jnp.concatenate([cos_part, -sign * sin_part], axis=1),
                    jnp.concatenate([sin_part, sign * cos_part], axis=1),
                ],
                axis=0,
            )
            none = jnp.zeros_like(weights)
            flat_weights[piece] = jnp.concatenate(
                [
                    jnp.concatenate([weights, weights, none], axis=1),
                    jnp.concatenate([none, none, weights], axis=1),
                ],
                axis=0,
            ).astype(jnp.bfloat16)

    lax.fori_loop(0, chunks - 1, second_phase, 0)

    def piece_step(piece, carry):
        piece_copy(piece).wait_recv()
        rows = pl.ds(pl.multiple_of(piece * PIECE, PIECE), PIECE)
        hat = jnp.dot(
            flat_recv[rows], flat_table[...], preferred_element_type=jnp.float32
        ).astype(jnp.bfloat16).astype(jnp.float32)
        products = []
        for low, high in ((0, 1), (1, 2), (1, 3)):
            real, imag = [], []
            for half in range(2):
                first = half * padded

                def parts(slot):
                    values = hat if slot == 1 else flat_hats[slot, rows]
                    return values[:, first:first + block], values[:, first + block:first + padded]

                low_real, low_imag = parts(low)
                high_real, high_imag = parts(high)
                real.append(low_real * high_real + low_imag * high_imag)
                imag.append(low_imag * high_real - low_real * high_imag)
            products += [jnp.concatenate(real, axis=1), jnp.concatenate(imag, axis=1)]
        product = jnp.concatenate([p.astype(jnp.bfloat16) for p in products], axis=0)
        sums = jnp.dot(flat_weights[piece], product, preferred_element_type=jnp.float32)
        acc[1] += sums[:2 * LAGS]
        acc[2] += sums[2 * LAGS:]
        return carry

    def wait_sends(blocks, offsets):
        drain(send_sem, send.at[pl.ds(0, blocks)])
        drain(mask_send, masks.at[pl.ds(0, n - 1)])
        drain(part_send, part.at[pl.ds(0, offsets), pl.ds(0, groups - 1)])

    def folded(rows):
        return jnp.concatenate([rows[:, :block], rows[:, block:]], axis=0)

    @pl.when(inner == 1)
    def _():
        settle(3)
        lax.fori_loop(0, CHUNK // PIECE, piece_step, 0)
        near_copy(3 - me).wait_recv()
        passed_on = near_in[3 - me]
        total = jnp.zeros((2 * lag_rows, block), jnp.float32)
        result = inverse_transform((me, 3 - me))
        for kind in (1, 0):
            for g in range(groups):
                first = kind * LAGS + g * lag_rows
                rows = result[first:first + lag_rows]
                if kind == 1:
                    rows += jnp.where(group == g, passed_on, 0.0)
                else:
                    total += jnp.where(group == g, folded(rows), 0.0)
                tail_out[kind, g] = folded(rows).astype(jnp.bfloat16)
            for step in range(1 - kind, groups):
                tail_copy(kind, group_peer(step), group).start()
        near_copy(me).wait_recv()
        total += folded(near_in[me])
        wait_sends((n - 1) * chunks - 1, 2)
        for piece in range(CHUNK // PIECE):
            piece_copy(piece).wait_send()
        drain(band_send, band_sum.at[pl.ds(0, 2)])
        for kind in (0, 1):
            drain(tail_recv.at[kind], tail_in.at[kind, pl.ds(0, groups - 1 + kind)])
            for step in range(1 - kind, groups):
                total += tail_in[kind, group_peer(step)].astype(jnp.float32)
        final = jnp.concatenate([total[:lag_rows], total[lag_rows:]], axis=1)
        out[0] = final * scale
        for kind in (1, 0):
            drain(tail_send.at[kind], tail_out.at[kind, pl.ds(0, groups - 1 + kind)])

    @pl.when(inner == 0)
    def _():
        settle(3)
        second_phase(chunks - 1, 0)
        share((1, 2))
        settle(1)
        settle(2)
        final = band_sum[me]
        drain(band_recv, band_in.at[pl.ds(0, 2)])
        for source in (near, far_inner):
            final += band_in[source]
        out[0] = final * scale
        drain(near_send, band_sum.at[pl.ds(0, n - 1)])
        wait_sends((n - 1) * chunks, n)


def fused_shards(spectra, quality, taper):
    block = spectra.shape[1]
    band = spectra.shape[2]
    padded = 2 * block
    n = lax.axis_size("ch")
    subs = lax.axis_size("sub")
    groups = lax.axis_size("fq") * subs
    chunks = band // (n * CHUNK)
    lag_rows = LAGS // groups
    bf16, f32 = jnp.bfloat16, jnp.float32
    in_hbm = pl.BlockSpec(memory_space=pltpu.HBM)
    operands = (
        spectra, quality.reshape(1, block), taper.reshape(1, band),
        jnp.asarray(channel_constant(block)), jnp.asarray(channel_constant(block).T),
        jnp.asarray(inverse_constant(block)),
        jnp.asarray(lag_constant(LAGS, FREQS)),
    )
    dma = pltpu.SemaphoreType.DMA
    regular = pltpu.SemaphoreType.REGULAR
    return pl.pallas_call(
        functools.partial(kernel, (n, groups, subs, block, chunks)),
        out_shape=jax.ShapeDtypeStruct((1, lag_rows, padded), f32),
        in_specs=[in_hbm] * 7,
        out_specs=pl.BlockSpec(memory_space=pltpu.VMEM),
        scratch_shapes=[
            pltpu.VMEM((1, band), f32),
            pltpu.VMEM((n * chunks, 2, block, CHUNK), f32),
            pltpu.VMEM((n * chunks, padded, CHUNK), bf16),
            pltpu.VMEM((n, chunks, padded, CHUNK), bf16),
            pltpu.VMEM((2 * padded, padded), bf16),
            pltpu.VMEM((2, 2 * padded, padded), bf16),
            pltpu.VMEM((2, LAGS, band), f32),
            pltpu.VMEM((n, 1, block), jnp.int32),
            pltpu.VMEM((n, chunks, 2 * padded, CHUNK), bf16),
            pltpu.VMEM((n, 2 * LAGS, padded), f32),
            pltpu.VMEM((n, groups, lag_rows, padded), f32),
            pltpu.VMEM((n, groups, lag_rows, padded), f32),
            pltpu.VMEM((n, lag_rows, padded), f32),
            pltpu.VMEM((n, lag_rows, padded), f32),
            pltpu.VMEM((n, lag_rows, padded), f32),
            pltpu.VMEM((2, groups, 2 * lag_rows, block), bf16),
            pltpu.VMEM((2, groups, 2 * lag_rows, block), bf16),
            pltpu.VMEM((padded, 2 * padded), bf16),
            pltpu.VMEM((CHUNK, padded), bf16),
            pltpu.VMEM((CHUNK, padded), bf16),
            pltpu.VMEM((n, CHUNK, 2 * padded), f32),
            pltpu.VMEM((CHUNK // PIECE, 4 * LAGS, 6 * PIECE), bf16),
            dma((9,)), dma((5,)), dma, dma((2, chunks)),
            dma, dma, dma, dma, dma((n,)), dma, dma, dma, dma((n,)), dma((2,)), dma((2,)),
            dma((CHUNK // PIECE,)), dma((CHUNK // PIECE,)), regular, regular,
        ],
        compiler_params=pltpu.CompilerParams(
            collective_id=0, has_side_effects=True, vmem_limit_bytes=40 << 20
        ),
    )(
        *[pltpu.with_memory_space_constraint(operand, pltpu.HBM) for operand in operands]
    )


def fits(mesh):
    blocks = mesh.shape["ch"]
    groups = mesh.shape["fq"] * mesh.shape["sub"]
    return blocks == 4 and FREQS == 4 * groups * blocks * CHUNK and LAGS % (8 * groups) == 0 and groups > 1


def solution(mesh):
    body = fused_shards if fits(mesh) else shards
    in_specs = (P(None, ("grp", "ch"), ("fq", "sub")), P(("grp", "ch")), P(("fq", "sub")))
    out_specs = P(("grp", "ch"), ("fq", "sub"), None)
    return jax.shard_map(body, mesh=mesh, in_specs=in_specs, out_specs=out_specs, check_vma=False)
```

```python
import functools

import jax
import jax.numpy as jnp
import numpy as np
from jax import lax
from jax.experimental import pallas as pl
from jax.experimental.pallas import tpu as pltpu
from jax.sharding import PartitionSpec as P

FREQS = 8192
LAGS = 32
CHUNK = 128
PIECE = 128


def passed_along(value, axis, steps):
    count = lax.axis_size(axis)
    pairs = [(source, (source + steps) % count) for source in range(count)]
    return lax.ppermute(value, axis, pairs)


def channel_table(block_size):
    padded = 2 * block_size
    row_index = jnp.arange(padded, dtype=jnp.int32)[:, None]
    col_index = jnp.arange(block_size, dtype=jnp.int32)[None, :]
    angle = 2.0 * jnp.pi / padded * (row_index * col_index % padded).astype(jnp.float32)
    cosine = jnp.cos(angle)
    sine = jnp.sin(angle)
    upper = jnp.concatenate([cosine, sine], axis=1)
    lower = jnp.concatenate([-sine, cosine], axis=1)
    return jnp.concatenate([upper, lower], axis=0).astype(jnp.bfloat16)


def inverse_table(block_size):
    padded = 2 * block_size
    row_index = jnp.arange(padded, dtype=jnp.int32)[:, None]
    col_index = jnp.arange(padded, dtype=jnp.int32)[None, :]
    angle = 2.0 * jnp.pi / padded * (row_index * col_index % padded).astype(jnp.float32)
    return jnp.concatenate([jnp.cos(angle), jnp.sin(angle)], axis=0) / padded


def lag_table(taper_band, start, band_size, lag_count, freq_count):
    freq_index = start + jnp.arange(band_size, dtype=jnp.int32)
    lag_index = jnp.arange(lag_count, dtype=jnp.int32) - lag_count // 2
    phase = lag_index[:, None] * freq_index[None, :] % (2 * freq_count)
    angle = jnp.pi / freq_count * phase.astype(jnp.float32)
    cosine = taper_band[None, :] * jnp.cos(angle)
    sine = taper_band[None, :] * jnp.sin(angle)
    upper = jnp.concatenate([cosine, -sine], axis=1)
    lower = jnp.concatenate([sine, cosine], axis=1)
    return jnp.concatenate([upper, lower], axis=0).astype(jnp.bfloat16)


def cross_spectrum(first, second, sign):
    padded = first.shape[0] // 2
    first_real = first[:padded].astype(jnp.float32)
    first_imag = first[padded:].astype(jnp.float32)
    second_real = second[:padded].astype(jnp.float32)
    second_imag = second[padded:].astype(jnp.float32)
    prod_real = first_real * second_real + first_imag * second_imag
    prod_imag = (first_imag * second_real - first_real * second_imag) * sign
    return jnp.concatenate([prod_real, prod_imag], axis=1).astype(jnp.bfloat16)


def pair_counts(lower_mask, upper_mask):
    block_size = lower_mask.shape[0]
    outer = lower_mask[::-1][:, None] * upper_mask[None, :]
    widened = jnp.pad(outer, ((0, 0), (0, block_size)))
    flat = widened.reshape(-1)[: block_size * (2 * block_size - 1)]
    sheared = flat.reshape(block_size, 2 * block_size - 1)
    histogram = jnp.pad(jnp.sum(sheared, axis=0), (0, 1))
    return jnp.roll(histogram, -(block_size - 1))


def channel_transform(table, data):
    block_size = data.shape[1]
    stacked = data.reshape(2 * block_size, data.shape[2])
    return jnp.dot(table, stacked, preferred_element_type=jnp.float32).astype(jnp.bfloat16)


def shards(spectra, quality, taper):
    block_size = spectra.shape[1]
    band_size = spectra.shape[2]
    padded = 2 * block_size
    blocks = lax.axis_size("ch")
    position = lax.axis_index("ch")
    quality_float = quality.astype(jnp.float32)
    masked = (spectra * quality_float[None, :, None]).astype(jnp.bfloat16)
    mask_half = quality_float.astype(jnp.bfloat16)
    table = channel_table(block_size)
    start = lax.axis_index(("fq", "sub")) * band_size
    own_hat = channel_transform(table, masked)
    weights = lag_table(taper, start, band_size, LAGS, FREQS)

    def accumulate(state, partner_hat, partner_mask, round_index):
        totals, tallies = state
        wrapped = position + round_index >= blocks
        sign = jnp.where(wrapped, -1.0, 1.0).astype(jnp.float32)
        product = cross_spectrum(own_hat, partner_hat, sign)
        term = lax.dot_general(
            weights, product, (((1,), (1,)), ((), ())), preferred_element_type=jnp.float32
        )
        term = term.reshape(2, LAGS, padded)
        offset = jnp.where(wrapped, blocks - round_index, round_index).astype(jnp.int32)
        keep = jnp.where(jnp.logical_and(wrapped, 2 * round_index == blocks), 0.0, 1.0).astype(
            jnp.float32
        )
        lower_mask = jnp.where(wrapped, partner_mask, mask_half).astype(jnp.float32)
        upper_mask = jnp.where(wrapped, mask_half, partner_mask).astype(jnp.float32)
        pairs = pair_counts(lower_mask, upper_mask)
        old_row = lax.dynamic_slice_in_dim(totals, offset, 1, 0)
        totals = lax.dynamic_update_slice_in_dim(totals, old_row + keep * term[None], offset, 0)
        old_tally = lax.dynamic_slice_in_dim(tallies, offset, 1, 0)
        tallies = lax.dynamic_update_slice_in_dim(
            tallies, old_tally + keep * pairs[None], offset, 0
        )
        return (totals, tallies)

    state = (
        jnp.zeros((blocks, 2, LAGS, padded), jnp.float32),
        jnp.zeros((blocks, padded), jnp.float32),
    )
    state = accumulate(state, own_hat, mask_half, 0)

    def advance(round_index, carry):
        current, held, held_mask = carry
        held, held_mask = passed_along((held, held_mask), "ch", -1)
        current = accumulate(current, channel_transform(table, held), held_mask, round_index)
        return (current, held, held_mask)

    state, _, _ = lax.fori_loop(1, blocks // 2 + 1, advance, (state, masked, mask_half))
    totals, tallies = state
    totals, tallies = (
        lax.psum_scatter(totals, "ch", scatter_dimension=0, tiled=True),
        lax.psum_scatter(tallies, "ch", scatter_dimension=0, tiled=True),
    )
    totals = lax.psum_scatter(totals, ("fq", "sub"), scatter_dimension=2, tiled=True)
    combined = jnp.concatenate([totals[0, 0], totals[0, 1]], axis=1)
    lagged = jnp.dot(
        combined,
        inverse_table(block_size),
        precision=lax.Precision.HIGHEST,
        preferred_element_type=jnp.float32,
    )
    scale = jnp.sqrt(2.0 * FREQS * jnp.maximum(tallies[0], 1.0))
    return (lagged / scale[None, :])[None]


def halves_first(first, second, block_size):
    return np.concatenate([
        part[start:start + block_size]
        for start in range(0, 2 * block_size, block_size) for part in (first, second)
    ])


def channel_constant(block_size):
    padded = 2 * block_size
    index = np.outer(np.arange(padded), np.arange(block_size)) % padded
    angle = 2.0 * np.pi / padded * index
    cosine, sine = np.cos(angle), np.sin(angle)
    upper = np.concatenate([cosine, sine], axis=1)
    lower = np.concatenate([-sine, cosine], axis=1)
    return halves_first(upper, lower, block_size).astype(jnp.bfloat16)


def inverse_constant(block_size):
    padded = 2 * block_size
    index = np.outer(np.arange(padded), np.arange(padded)) % padded
    angle = 2.0 * np.pi / padded * index
    full = halves_first(np.cos(angle), np.sin(angle), block_size) / padded
    high = full.astype(np.float32).astype(jnp.bfloat16)
    low = (full - high.astype(np.float64)).astype(np.float32).astype(jnp.bfloat16)
    return np.stack([high, low])


def lag_constant(lag_count, freq_count):
    lag_index = np.arange(lag_count) - lag_count // 2
    phase = np.outer(lag_index, np.arange(freq_count)) % (2 * freq_count)
    angle = np.pi / freq_count * phase
    return np.stack([np.cos(angle), np.sin(angle)]).astype(np.float32)


def kernel(
    sizes, spectra, quality_hbm, taper_hbm, table_hbm, flat_hbm, inverse_hbm, lag_hbm, out,
    taper, raw, send, recv, table, inverse, lagtab, masks, hats, acc, part, part_in, band_sum, band_in, near_in,
    tail_out, tail_in, flat_table, flat_send, flat_recv, flat_hats, flat_weights,
    raw_sem, const_sem, send_sem, recv_sem, mask_sem, mask_send, mask_recv,
    part_send, part_recv, band_send, band_recv, near_send, near_recv, tail_send, tail_recv, piece_send, piece_recv, two_away, three_away,
):
    n, groups, subs, block, chunks = sizes
    padded = 2 * block
    lag_rows = LAGS // groups
    me = lax.axis_index("ch")
    group = lax.axis_index("fq") * subs + lax.axis_index("sub")
    upper = me // 2
    inner = (me * (n - 1 - me)) // 2
    near = me + 1 - 2 * lax.rem(me, 2)
    far_outer = 3 * (1 - upper)
    far_inner = 2 - upper
    sign = (2 * upper - 1).astype(jnp.float32)
    own_slot = 3 - inner

    def ch_peer(step):
        return lax.rem(me + step, n)

    def group_peer(step):
        return lax.rem(group + step, groups)

    def place(ch, index):
        return {"ch": ch, "fq": index // subs, "sub": lax.rem(index, subs)}

    def raw_copy(slot, turn):
        start = pl.multiple_of(slot * CHUNK, CHUNK)
        return pltpu.make_async_copy(
            spectra.at[:, :, pl.ds(start, CHUNK)], raw.at[slot], raw_sem.at[turn]
        )

    def data_copy(target, c):
        late = jnp.where(target == near, 0, inner)
        return pltpu.make_async_remote_copy(
            send.at[target * chunks + c], recv.at[me, c],
            send_sem, recv_sem.at[late, c],
            device_id={"ch": target}, device_id_type=pl.DeviceIdType.MESH,
        )

    def piece_copy(piece):
        rows = pl.ds(pl.multiple_of(piece * PIECE, PIECE), PIECE)
        return pltpu.make_async_remote_copy(
            flat_send.at[rows], flat_recv.at[rows], piece_send.at[piece], piece_recv.at[piece],
            device_id={"ch": far_inner}, device_id_type=pl.DeviceIdType.MESH,
        )

    def mask_copy(target, source):
        return pltpu.make_async_remote_copy(
            masks.at[me], masks.at[source], mask_send, mask_recv,
            device_id={"ch": target}, device_id_type=pl.DeviceIdType.MESH,
        )

    def part_copy(j, target, source):
        return pltpu.make_async_remote_copy(
            part.at[j, target], part_in.at[j, source],
            part_send, part_recv.at[j],
            device_id=place(me, target), device_id_type=pl.DeviceIdType.MESH,
        )

    def band_copy(target, source):
        return pltpu.make_async_remote_copy(
            band_sum.at[target], band_in.at[source], band_send, band_recv,
            device_id={"ch": target}, device_id_type=pl.DeviceIdType.MESH,
        )

    def near_copy(j):
        return pltpu.make_async_remote_copy(
            band_sum.at[j], near_in.at[j], near_send, near_recv.at[j],
            device_id={"ch": near}, device_id_type=pl.DeviceIdType.MESH,
        )

    def tail_copy(kind, target, source):
        return pltpu.make_async_remote_copy(
            tail_out.at[kind, target], tail_in.at[kind, source],
            tail_send.at[kind], tail_recv.at[kind],
            device_id=place(3 - me if kind else me, target), device_id_type=pl.DeviceIdType.MESH,
        )

    def drain(semaphore, ref):
        pltpu.make_async_copy(ref, ref, semaphore).wait()

    def tell(semaphore, target):
        pl.semaphore_signal(
            semaphore, inc=1, device_id={"ch": target}, device_id_type=pl.DeviceIdType.MESH
        )

    barrier = pltpu.get_barrier_semaphore()

    @pl.when(me > 0)
    def _():
        tell(barrier, me - 1)

    @pl.when(me < n - 1)
    def _():
        tell(barrier, me + 1)

    for step in range(1, groups):
        pl.semaphore_signal(
            barrier, inc=1, device_id=place(me, group_peer(step)),
            device_id_type=pl.DeviceIdType.MESH,
        )

    quality_copy = pltpu.make_async_copy(quality_hbm, masks.at[me], mask_sem)
    quality_copy.start()
    for target in (far_inner, near, far_outer):
        raw_copy(target * chunks, 0).start()
    inner_order = [
        (far_outer, 1), (near, 1), (far_outer, 2), (near, 2), (far_outer, 3), (near, 3),
        (far_inner, 1), (far_inner, 2), (far_inner, 3),
    ]
    outer_order = [
        (far_outer, 1), (far_inner, 1), (near, 1), (far_outer, 2), (far_inner, 2), (near, 2),
        (far_outer, 3), (far_inner, 3), (near, 3),
    ]
    order = [
        (inner * a + (1 - inner) * b, inner * a_chunk + (1 - inner) * b_chunk)
        for (a, a_chunk), (b, b_chunk) in zip(inner_order, outer_order)
    ]
    band = n * chunks * CHUNK
    lag_start = pl.multiple_of(group * band, CHUNK)
    consts = [
        pltpu.make_async_copy(table_hbm, table, const_sem.at[0]),
        pltpu.make_async_copy(lag_hbm.at[:, :, pl.ds(lag_start, band)], lagtab, const_sem.at[1]),
        pltpu.make_async_copy(inverse_hbm, inverse, const_sem.at[2]),
        pltpu.make_async_copy(taper_hbm, taper, const_sem.at[3]),
        pltpu.make_async_copy(flat_hbm, flat_table, const_sem.at[4]),
    ]

    quality_copy.wait()
    quality_row = masks[me].astype(jnp.float32)
    column = jnp.transpose(jnp.broadcast_to(quality_row, (CHUNK, block)))

    def mask_block(slot):
        for half in range(2):
            send[slot, half * block:(half + 1) * block, :] = (
                raw[slot, half] * column
            ).astype(jnp.bfloat16)

    def send_block(index):
        target, c = order[index]
        if index % 2 == 0:
            drain(raw_sem.at[3 + index // 2], raw.at[pl.ds(0, 2)])
        mask_block(target * chunks + c)
        data_copy(target, c).start()

    drain(raw_sem.at[0], raw.at[pl.ds(0, n - 1)])

    for target in (far_inner, near, far_outer):
        mask_block(target * chunks)
    pl.semaphore_wait(barrier, groups + inner)

    @pl.when(inner == 1)
    def _():
        tell(two_away, me - 1)
        tell(two_away, me + 1)
        data_copy(far_inner, 0).start()

    data_copy(near, 0).start()
    for index, (target, c) in enumerate(order):
        raw_copy(target * chunks + c, 3 + index // 2 if index < 6 else 2).start()
    for c in range(chunks):
        raw_copy(me * chunks + c, 1).start()

    @pl.when(inner == 1)
    def _():
        pl.semaphore_wait(two_away, 1)
        tell(three_away, (n - 1) * (me - 1))
        data_copy(far_outer, 0).start()

    @pl.when(inner == 0)
    def _():
        pl.semaphore_wait(two_away, 1)
        data_copy(far_inner, 0).start()
        pl.semaphore_wait(three_away, 1)
        data_copy(far_outer, 0).start()

    for step in range(1, n):
        mask_copy(ch_peer(step), me).start()
    for index in range(2):
        send_block(index)
    for copy in consts:
        copy.start()
    for index in range(2, 6):
        send_block(index)
    drain(raw_sem.at[2], raw.at[pl.ds(0, 3)])
    for target, c in order[6:]:
        mask_block(target * chunks + c)

    @pl.when(inner == 1)
    def _():
        slot = far_inner * chunks + chunks - 1
        for half in range(2):
            flat_send[:, half * block:(half + 1) * block] = jnp.transpose(
                raw[slot, half] * column
            ).astype(jnp.bfloat16)

    drain(raw_sem.at[1], raw.at[pl.ds(0, chunks)])
    for c in range(chunks):
        mask_block(me * chunks + c)
    acc[...] = jnp.zeros_like(acc)
    for index in (0, 1, 3, 4):
        consts[index].wait()

    def lag_factors(start, width):
        lanes = pl.ds(pl.multiple_of(start, CHUNK), width)
        weight = taper[:, lanes]
        return weight * lagtab[0, :, lanes], weight * lagtab[1, :, lanes]

    def transform(data, half):
        rows = table[half * padded:(half + 1) * padded]
        return jnp.dot(rows, data, preferred_element_type=jnp.float32).astype(jnp.bfloat16)

    def contract(weights, product):
        return lax.dot_general(
            weights, product, (((1,), (1,)), ((), ())), preferred_element_type=jnp.float32
        )

    def own_pair(slot, keep):
        data = jnp.concatenate([send[slot], send[slot + 1]], axis=1)
        wcos, wsin = lag_factors(slot * CHUNK, 2 * CHUNK)
        weights = jnp.concatenate([wcos, wsin], axis=0).astype(jnp.bfloat16)
        for half in range(2):
            hat = transform(data, half)
            keep(half, hat)
            real = hat[:block].astype(jnp.float32)
            imag = hat[block:].astype(jnp.float32)
            power = (real * real + imag * imag).astype(jnp.bfloat16)
            acc[0, :, half * block:(half + 1) * block] += contract(weights, power)

    def keep_at(first, second):
        def keep(half, hat):
            rows = slice(half * padded, (half + 1) * padded)
            hats[(*first, rows)] = hat[:, :CHUNK]
            hats[(*second, rows)] = hat[:, CHUNK:]
        return keep

    def other_step(index, carry):
        step = 1 + index // (chunks // 2)
        half = lax.rem(index, chunks // 2)
        own_pair(ch_peer(step) * chunks + 2 * half, lambda half, hat: None)
        return carry

    def own_step(half, carry):
        keep = keep_at((own_slot, 2 * half), (own_slot, 2 * half + 1))
        own_pair(me * chunks + 2 * half, keep)
        return carry

    lax.fori_loop(0, chunks // 2, own_step, 0)
    lax.fori_loop(0, (n - 1) * (chunks // 2), other_step, 0)

    def lag_weights(c):
        wcos, wsin = lag_factors((me * chunks + c) * CHUNK, CHUNK)
        return jnp.concatenate(
            [
                jnp.concatenate([wcos, -sign * wsin], axis=1),
                jnp.concatenate([wsin, sign * wcos], axis=1),
            ],
            axis=0,
        ).astype(jnp.bfloat16)

    def spectrum(slot, c, half):
        first = half * padded
        return (
            hats[slot, c, first:first + block].astype(jnp.float32),
            hats[slot, c, first + block:first + padded].astype(jnp.float32),
        )

    def lag_sums(weights, half, value, pairs):
        for j in sorted({j for j, _, _ in pairs}):
            products = []
            for index, low, high in pairs:
                if index == j:
                    low_real, low_imag = value[low]
                    high_real, high_imag = value[high]
                    products.append(low_real * high_real + low_imag * high_imag)
                    products.append(low_imag * high_real - low_real * high_imag)
            product = jnp.concatenate([p.astype(jnp.bfloat16) for p in products], axis=1)
            repeated = jnp.concatenate([weights] * (len(products) // 2), axis=1)
            acc[j, :, half * block:(half + 1) * block] += contract(repeated, product)

    def inverse_transform(offsets):
        result = 0.0
        for half in range(2):
            lanes = slice(half * block, (half + 1) * block)
            total = jnp.concatenate(
                [jnp.concatenate([acc[j, :LAGS, lanes], acc[j, LAGS:, lanes]], axis=1) for j in offsets],
                axis=0,
            )
            count = len(offsets) * LAGS
            high = total.astype(jnp.bfloat16)
            low_part = (total - high.astype(jnp.float32)).astype(jnp.bfloat16)
            rows = slice(half * padded, (half + 1) * padded)
            both = jnp.dot(
                jnp.concatenate([high, low_part], axis=0), inverse[0, rows],
                preferred_element_type=jnp.float32,
            )
            result += both[:count] + both[count:] + jnp.dot(
                high, inverse[1, rows], preferred_element_type=jnp.float32
            )
        return result

    def share(offsets):
        result = inverse_transform(offsets)
        for index, j in enumerate(offsets):
            for g in range(groups):
                first = index * LAGS + g * lag_rows
                part[j, g] = result[first:first + lag_rows]
            for step in range(1, groups):
                part_copy(j, group_peer(step), group).start()

    def settle(j):
        total = part[j, group]
        drain(part_recv.at[j], part_in.at[j, pl.ds(0, groups - 1)])
        for step in range(1, groups):
            total += part_in[j, group_peer(step)]
        band_sum[j] = total

        @pl.when(jnp.logical_and(inner == 1, far_outer == j))
        def _():
            near_copy(j).wait_recv()
            band_sum[j] += near_in[j]

        @pl.when(inner == 1)
        def _():
            band_copy(j, me).start()

        @pl.when(jnp.logical_and(inner == 0, me != j))
        def _():
            near_copy(j).start()

    consts[2].wait()
    share((0,))

    drain(mask_recv, masks.at[pl.ds(0, n - 1)])
    flip = jnp.where(
        lax.broadcasted_iota(jnp.int32, (block, block), 0)
        + lax.broadcasted_iota(jnp.int32, (block, block), 1) == block - 1, 1.0, 0.0,
    ).astype(jnp.bfloat16)

    def mask_rows(index):
        return jnp.broadcast_to(masks[index].astype(jnp.float32), (8, block))

    first_row = jnp.where(lax.broadcasted_iota(jnp.int32, (8, block), 0) == 0, 1.0, 0.0)
    pairs = jnp.zeros((block, block), jnp.float32)
    for low in range(n):
        valid = jnp.where(low + me < n, 1.0, 0.0)
        upper_mask = (mask_rows(lax.rem(low + me, n)) * (first_row * valid)).astype(jnp.bfloat16)
        lower_mask = jnp.dot(
            mask_rows(low).astype(jnp.bfloat16), flip, preferred_element_type=jnp.float32
        )
        pairs += jnp.dot(
            jnp.transpose(lower_mask).astype(jnp.bfloat16), upper_mask,
            preferred_element_type=jnp.float32,
        )
    widened = jnp.concatenate([pairs, jnp.zeros((block, block), jnp.float32)], axis=1)
    sheared = pltpu.roll(widened, 0, 1, stride=1, stride_axis=0)
    counts = jnp.sum(sheared, axis=0, keepdims=True)
    counts = pltpu.roll(jnp.broadcast_to(counts, (8, padded)), padded - block + 1, 1)
    scale = 1.0 / jnp.sqrt(2.0 * FREQS * jnp.maximum(counts[:1], 1.0))

    def first_phase(c, carry):
        weights = lag_weights(c)
        drain(recv_sem.at[0, c], recv.at[pl.ds(0, 2), c])
        data = jnp.concatenate([recv[near, c], recv[far_outer, c]], axis=1)
        keep = keep_at((5 - own_slot, c), (0, c))
        for half in range(2):
            keep(half, transform(data, half))
            value = {slot: spectrum(slot, c, half) for slot in (0, 2, 3)}
            lag_sums(weights, half, value, ((1, 2, 3), (2, 0, 2), (3, 0, 3)))
        return carry

    def second_phase(c, carry):
        weights = lag_weights(c)
        drain(recv_sem.at[1, c], recv.at[far_inner, c])
        for half in range(2):
            hat = transform(recv[far_inner, c], half).astype(jnp.float32)
            value = {slot: spectrum(slot, c, half) for slot in (0, 2, 3)}
            value[1] = hat[:block], hat[block:]
            lag_sums(weights, half, value, ((1, 0, 1), (1, 1, 2), (2, 1, 3)))
        return carry

    first_phase(0, 0)

    @pl.when(inner == 0)
    def _():
        settle(0)
        for target, c in order[6:8] + [(near, chunks - 1)]:
            data_copy(target, c).start()

    lax.fori_loop(1, chunks - 1, first_phase, 0)

    @pl.when(inner == 1)
    def _():
        settle(0)
        for target, c in order[6:8]:
            data_copy(target, c).start()
        for piece in range(CHUNK // PIECE):
            piece_copy(piece).start()

    first_phase(chunks - 1, 0)
    share((3,))

    @pl.when(inner == 1)
    def _():
        for slot in (0, 2, 3):
            flat_hats[slot] = jnp.transpose(hats[slot, chunks - 1].astype(jnp.float32))
        wcos, wsin = lag_factors((me * chunks + chunks - 1) * CHUNK, CHUNK)
        for piece in range(CHUNK // PIECE):
            cos_part = wcos[:, piece * PIECE:(piece + 1) * PIECE]
            sin_part = wsin[:, piece * PIECE:(piece + 1) * PIECE]
            weights = jnp.concatenate(
                [
                    jnp.concatenate([cos_part, -sign * sin_part], axis=1),
                    jnp.concatenate([sin_part, sign * cos_part], axis=1),
                ],
                axis=0,
            )
            none = jnp.zeros_like(weights)
            flat_weights[piece] = jnp.concatenate(
                [
                    jnp.concatenate([weights, weights, none], axis=1),
                    jnp.concatenate([none, none, weights], axis=1),
                ],
                axis=0,
            ).astype(jnp.bfloat16)

    lax.fori_loop(0, chunks - 1, second_phase, 0)

    def piece_step(piece, carry):
        piece_copy(piece).wait_recv()
        rows = pl.ds(pl.multiple_of(piece * PIECE, PIECE), PIECE)
        hat = jnp.dot(
            flat_recv[rows], flat_table[...], preferred_element_type=jnp.float32
        ).astype(jnp.bfloat16).astype(jnp.float32)
        products = []
        for low, high in ((0, 1), (1, 2), (1, 3)):
            real, imag = [], []
            for half in range(2):
                first = half * padded

                def parts(slot):
                    values = hat if slot == 1 else flat_hats[slot, rows]
                    return values[:, first:first + block], values[:, first + block:first + padded]

                low_real, low_imag = parts(low)
                high_real, high_imag = parts(high)
                real.append(low_real * high_real + low_imag * high_imag)
                imag.append(low_imag * high_real - low_real * high_imag)
            products += [jnp.concatenate(real, axis=1), jnp.concatenate(imag, axis=1)]
        product = jnp.concatenate([p.astype(jnp.bfloat16) for p in products], axis=0)
        sums = jnp.dot(flat_weights[piece], product, preferred_element_type=jnp.float32)
        acc[1] += sums[:2 * LAGS]
        acc[2] += sums[2 * LAGS:]
        return carry

    def wait_sends(blocks, offsets):
        drain(send_sem, send.at[pl.ds(0, blocks)])
        drain(mask_send, masks.at[pl.ds(0, n - 1)])
        drain(part_send, part.at[pl.ds(0, offsets), pl.ds(0, groups - 1)])

    def folded(rows):
        return jnp.concatenate([rows[:, :block], rows[:, block:]], axis=0)

    @pl.when(inner == 1)
    def _():
        settle(3)
        for piece in range(CHUNK // PIECE):
            piece_step(piece, 0)
        near_copy(3 - me).wait_recv()
        passed_on = near_in[3 - me]
        total = jnp.zeros((2 * lag_rows, block), jnp.float32)
        result = inverse_transform((me, 3 - me))
        for kind in (1, 0):
            for g in range(groups):
                first = kind * LAGS + g * lag_rows
                rows = result[first:first + lag_rows]
                if kind == 1:
                    rows += jnp.where(group == g, passed_on, 0.0)
                else:
                    total += jnp.where(group == g, folded(rows), 0.0)
                tail_out[kind, g] = folded(rows).astype(jnp.bfloat16)
            for step in range(1 - kind, groups):
                tail_copy(kind, group_peer(step), group).start()
        near_copy(me).wait_recv()
        total += folded(near_in[me])
        wait_sends((n - 1) * chunks - 1, 2)
        for piece in range(CHUNK // PIECE):
            piece_copy(piece).wait_send()
        drain(band_send, band_sum.at[pl.ds(0, 2)])
        for kind in (0, 1):
            drain(tail_recv.at[kind], tail_in.at[kind, pl.ds(0, groups - 1 + kind)])
            for step in range(1 - kind, groups):
                total += tail_in[kind, group_peer(step)].astype(jnp.float32)
        final = jnp.concatenate([total[:lag_rows], total[lag_rows:]], axis=1)
        out[0] = final * scale
        for kind in (1, 0):
            drain(tail_send.at[kind], tail_out.at[kind, pl.ds(0, groups - 1 + kind)])

    @pl.when(inner == 0)
    def _():
        settle(3)
        second_phase(chunks - 1, 0)
        share((1, 2))
        settle(1)
        settle(2)
        final = band_sum[me]
        drain(band_recv, band_in.at[pl.ds(0, 2)])
        for source in (near, far_inner):
            final += band_in[source]
        out[0] = final * scale
        drain(near_send, band_sum.at[pl.ds(0, n - 1)])
        wait_sends((n - 1) * chunks, n)


def fused_shards(spectra, quality, taper):
    block = spectra.shape[1]
    band = spectra.shape[2]
    padded = 2 * block
    n = lax.axis_size("ch")
    subs = lax.axis_size("sub")
    groups = lax.axis_size("fq") * subs
    chunks = band // (n * CHUNK)
    lag_rows = LAGS // groups
    bf16, f32 = jnp.bfloat16, jnp.float32
    in_hbm = pl.BlockSpec(memory_space=pltpu.HBM)
    operands = (
        spectra, quality.reshape(1, block), taper.reshape(1, band),
        jnp.asarray(channel_constant(block)), jnp.asarray(channel_constant(block).T),
        jnp.asarray(inverse_constant(block)),
        jnp.asarray(lag_constant(LAGS, FREQS)),
    )
    dma = pltpu.SemaphoreType.DMA
    regular = pltpu.SemaphoreType.REGULAR
    return pl.pallas_call(
        functools.partial(kernel, (n, groups, subs, block, chunks)),
        out_shape=jax.ShapeDtypeStruct((1, lag_rows, padded), f32),
        in_specs=[in_hbm] * 7,
        out_specs=pl.BlockSpec(memory_space=pltpu.VMEM),
        scratch_shapes=[
            pltpu.VMEM((1, band), f32),
            pltpu.VMEM((n * chunks, 2, block, CHUNK), f32),
            pltpu.VMEM((n * chunks, padded, CHUNK), bf16),
            pltpu.VMEM((n, chunks, padded, CHUNK), bf16),
            pltpu.VMEM((2 * padded, padded), bf16),
            pltpu.VMEM((2, 2 * padded, padded), bf16),
            pltpu.VMEM((2, LAGS, band), f32),
            pltpu.VMEM((n, 1, block), jnp.int32),
            pltpu.VMEM((n, chunks, 2 * padded, CHUNK), bf16),
            pltpu.VMEM((n, 2 * LAGS, padded), f32),
            pltpu.VMEM((n, groups, lag_rows, padded), f32),
            pltpu.VMEM((n, groups, lag_rows, padded), f32),
            pltpu.VMEM((n, lag_rows, padded), f32),
            pltpu.VMEM((n, lag_rows, padded), f32),
            pltpu.VMEM((n, lag_rows, padded), f32),
            pltpu.VMEM((2, groups, 2 * lag_rows, block), bf16),
            pltpu.VMEM((2, groups, 2 * lag_rows, block), bf16),
            pltpu.VMEM((padded, 2 * padded), bf16),
            pltpu.VMEM((CHUNK, padded), bf16),
            pltpu.VMEM((CHUNK, padded), bf16),
            pltpu.VMEM((n, CHUNK, 2 * padded), f32),
            pltpu.VMEM((CHUNK // PIECE, 4 * LAGS, 6 * PIECE), bf16),
            dma((6,)), dma((5,)), dma, dma((2, chunks)),
            dma, dma, dma, dma, dma((n,)), dma, dma, dma, dma((n,)), dma((2,)), dma((2,)),
            dma((CHUNK // PIECE,)), dma((CHUNK // PIECE,)), regular, regular,
        ],
        compiler_params=pltpu.CompilerParams(
            collective_id=0, has_side_effects=True, vmem_limit_bytes=40 << 20
        ),
    )(
        *[pltpu.with_memory_space_constraint(operand, pltpu.HBM) for operand in operands]
    )


def fits(mesh):
    blocks = mesh.shape["ch"]
    groups = mesh.shape["fq"] * mesh.shape["sub"]
    return blocks == 4 and FREQS == 4 * groups * blocks * CHUNK and LAGS % (8 * groups) == 0 and groups > 1


def solution(mesh):
    body = fused_shards if fits(mesh) else shards
    in_specs = (P(None, ("grp", "ch"), ("fq", "sub")), P(("grp", "ch")), P(("fq", "sub")))
    out_specs = P(("grp", "ch"), ("fq", "sub"), None)
    return jax.shard_map(body, mesh=mesh, in_specs=in_specs, out_specs=out_specs, check_vma=False)
```
